32 devices in a mesh: wide: 8 (over z, x), narrow: 4 (over y, core).
Axes of the slice: x: 2, y: 2, z: 4, core: 2. Of those that a mesh axis runs over, the one named last changes fastest.
Arguments:
- block_in: bfloat16 [160, 200, 768], P(('wide', 'narrow')), may hold values from -6 to 6
- out_grad: bfloat16 [160, 200, 768], P(('wide', 'narrow')), may hold values from -6 to 6
- mim_mask: int32 [160, 200], P(('wide', 'narrow')), may hold values from 0 to 1, as said below
- rel_index: int32 [200, 200], replicated, may hold values from 0 to 731
- qkv_weight: bfloat16 [768, 2304], replicated, may hold values from -0.21875 to 0.21875
- proj_weight: bfloat16 [768, 768], replicated, may hold values from -0.875 to 0.875
- up_weight: bfloat16 [768, 3072], P(None, 'narrow'), may hold values from -0.21875 to 0.21875
- down_weight: bfloat16 [768, 3072], P(None, 'narrow'), may hold values from -0.109375 to 0.109375
- vectors: float32 [10, 768], replicated
- up_bias: float32 [3072], replicated, may hold values from -1.5 to 1.5
- rel_table: float32 [732, 12], replicated, may hold values from -4 to 4
- qkv_master: float32 [768, 2304], P('wide', 'narrow'), may hold values from -0.21875 to 0.21875
- qkv_mean: float32 [768, 2304], P('wide', 'narrow'), may hold values from -0.00061035156 to 0.00061035156
- qkv_square: float32 [768, 2304], P('wide', 'narrow'), may hold values from 7.064254e-11 to 1.1302806e-09
- proj_master: float32 [768, 768], P('wide', 'narrow'), may hold values from -0.875 to 0.875
- proj_mean: float32 [768, 768], P('wide', 'narrow'), may hold values from -0.00061035156 to 0.00061035156
- proj_square: float32 [768, 768], P('wide', 'narrow'), may hold values from 7.064254e-11 to 1.1302806e-09
- up_master: float32 [768, 3072], P('wide', 'narrow'), may hold values from -0.21875 to 0.21875
- up_mean: float32 [768, 3072], P('wide', 'narrow'), may hold values from -0.00061035156 to 0.00061035156
- up_square: float32 [768, 3072], P('wide', 'narrow'), may hold values from 7.064254e-11 to 1.1302806e-09
- down_master: float32 [768, 3072], P('wide', 'narrow'), may hold values from -0.109375 to 0.109375
- down_mean: float32 [768, 3072], P('wide', 'narrow'), may hold values from -0.00061035156 to 0.00061035156
- down_square: float32 [768, 3072], P('wide', 'narrow'), may hold values from 7.064254e-11 to 1.1302806e-09
- vector_mean: float32 [10, 768], replicated, may hold values from -0.001953125 to 0.001953125
- vector_square: float32 [10, 768], replicated, may hold values from 6.3578287e-10 to 1.0172526e-08
- bias_mean: float32 [3072], replicated, may hold values from -0.001953125 to 0.001953125
- bias_square: float32 [3072], replicated, may hold values from 4.2385526e-11 to 1.695421e-10
- table_mean: float32 [732, 12], replicated, may hold values from -0.001953125 to 0.001953125
- table_square: float32 [732, 12], replicated, may hold values from 4.2385526e-11 to 1.695421e-10
Outputs:
- block_out: bfloat16 [160, 200, 768], P(('wide', 'narrow'))
- input_grad: float32 [160, 200, 768], P(('wide', 'narrow'))
- grad_norm: float32 [], replicated
- qkv_mean_new: float32 [768, 2304], P('wide', 'narrow')
- qkv_square_new: float32 [768, 2304], P('wide', 'narrow')
- qkv_new: float32 [768, 2304], P('wide', 'narrow')
- qkv_copy: bfloat16 [768, 2304], P('wide', 'narrow')
- proj_mean_new: float32 [768, 768], P('wide', 'narrow')
- proj_square_new: float32 [768, 768], P('wide', 'narrow')
- proj_new: float32 [768, 768], P('wide', 'narrow')
- proj_copy: bfloat16 [768, 768], P('wide', 'narrow')
- up_mean_new: float32 [768, 3072], P('wide', 'narrow')
- up_square_new: float32 [768, 3072], P('wide', 'narrow')
- up_new: float32 [768, 3072], P('wide', 'narrow')
- up_copy: bfloat16 [768, 3072], P('wide', 'narrow')
- down_mean_new: float32 [768, 3072], P('wide', 'narrow')
- down_square_new: float32 [768, 3072], P('wide', 'narrow')
- down_new: float32 [768, 3072], P('wide', 'narrow')
- down_copy: bfloat16 [768, 3072], P('wide', 'narrow')
- vector_mean_new: float32 [10, 768], replicated
- vector_square_new: float32 [10, 768], replicated
- vectors_new: float32 [10, 768], replicated
- bias_mean_new: float32 [3072], replicated
- bias_square_new: float32 [3072], replicated
- up_bias_new: float32 [3072], replicated
- table_mean_new: float32 [732, 12], replicated
- table_square_new: float32 [732, 12], replicated
- table_new: float32 [732, 12], replicated
The draws below stay inside these ranges and needn't reach their ends.
Inputs may be any that keep to these rules, and one draw needn't show every extreme that they name: `mim_mask`: each image masks its own share of patches, from almost none to about three quarters, very unequal between images; position 0 and positions from 197 on are never masked.
All inputs are finite; a program needn't handle non-finite values.
Results may differ from the reference program's by a relative error of at most 0.012.
Values may be sent and summed in bfloat16 or wider, within the bound.
No kernel may reach another device: no remote copies, remote signals or barrier semaphores. Data moves between devices by JAX's collectives and lax.ppermute only.
A program may use at most 192 MiB of HBM per device.

```python
import math
import jax
import jax.numpy as jnp
from jax import lax

D = 768
HEADS = 12
HEAD_DIM = 64
FF = 3072
NREL = 732
SEQ = 200
VALID = 197
STEP = 10
IMAGES = 160


def draw_mim_mask(key, part):
    first_key, second_key = jax.random.split(key, 2)
    level = jax.random.randint(first_key, (IMAGES, 1), 1, 10)
    share = level * level * level
    rolled = jax.random.randint(second_key, (IMAGES, SEQ), 0, 1000)
    position = jnp.arange(SEQ, dtype=jnp.int32)[None, :]
    usable = (position >= 1) & (position < VALID)
    return jnp.where(usable & (rolled < share), 1, 0).astype(jnp.int32)


def draw_vectors(key, part):
    first_key, second_key = jax.random.split(key, 2)
    noise = jax.random.normal(first_key, (10, D), jnp.float32)
    levels = jax.random.uniform(second_key, (10, D), jnp.float32, 0.5, 1.5)
    row_index = jnp.arange(10, dtype=jnp.int32)[:, None]
    is_gain = (row_index == 4) | (row_index == 6) | (row_index == 8) | (row_index == 9)
    return jnp.where(is_gain, levels, 0.2 * noise).astype(jnp.float32)


def with_ends(array, key, smallest, high):
    shape = array.shape
    index_at = [jax.random.randint(jax.random.fold_in(key, axis), (), 0, shape[axis]) for axis in range(len(shape))]
    array = array.at[tuple(index_at)].set(smallest)
    longest = shape.index(max(shape))
    index_at[longest] = (index_at[longest] + 1) % shape[longest]
    return array.at[tuple(index_at)].set(high)


def spiked(array, rng, source, target, blocks, factor):
    owner, partner = [(jnp.arange(array.shape[axis_at]) // (array.shape[axis_at] // blocks)).reshape([-1 if axis == axis_at else 1 for axis in range(array.ndim)]) for axis_at in (source, target)]
    chosen = jax.random.permutation(rng, blocks)[partner]
    strong = (owner == chosen) | (owner == (partner + blocks // 2) % blocks)
    return jnp.where(strong, factor * array, array)


def block_levels(rng, dims, cuts, low, high):
    loudness, own = 1.0, jax.random.fold_in(rng, 6)
    for axis_at, blocks in cuts:
        heights = jnp.exp(jax.random.uniform(jax.random.fold_in(own, axis_at), (blocks,), jnp.float32, low / len(cuts), high / len(cuts)))
        loudness = loudness * jnp.repeat(heights, dims[axis_at] // blocks).reshape([-1 if axis == axis_at else 1 for axis in range(len(dims))])
    return loudness


def bell_draw(rng, extent, scale, bound, cuts=(), held_as=jnp.bfloat16):
    factor_of = block_levels(rng, extent, cuts, -0.22, 0.18) if cuts else 1.0
    result = jax.random.normal(rng, extent, jnp.float32) * scale * factor_of
    return jnp.minimum(jnp.maximum(result, -bound), bound).astype(held_as)


def bell_draw_with(own_key, shape, scale, most, shards, heavy, kind=jnp.bfloat16):
    drawn = scale * jax.random.normal(own_key, shape, jnp.float32)
    if shards:
        drawn = drawn * block_levels(own_key, shape, shards, -0.22, 0.18)
    return jnp.clip(spiked(drawn, jax.random.fold_in(own_key, 3), *heavy), -most, most).astype(kind)


def setup_inputs(seed: int = 0) -> dict:
    seeds = jax.random.split(jax.random.key(seed), 30)
    return {
        "block_in": bell_draw(seeds[0], (IMAGES, SEQ, D), 1.0, 6.0, ((0, 32),)),
        "out_grad": bell_draw_with(seeds[1], (IMAGES, SEQ, D), 1.0, 6.0, ((0, 32),), (0, 2, 32, 2.75)),
        "mim_mask": draw_mim_mask(jax.random.fold_in(seeds[29], 71), 0),
        "rel_index": with_ends(jax.random.randint(seeds[3], (SEQ, SEQ), 0, NREL), jax.random.fold_in(seeds[3], 1), 0, NREL - 1).astype(jnp.int32),
        "qkv_weight": bell_draw(seeds[4], (D, 3 * D), D ** -0.5, 0.21875),
        "proj_weight": bell_draw(seeds[5], (D, D), (D // 16) ** -0.5, 0.875),
        "up_weight": bell_draw(seeds[6], (D, FF), D ** -0.5, 0.21875, ((1, 4),)),
        "down_weight": bell_draw(seeds[7], (D, FF), FF ** -0.5, 0.109375, ((1, 4),)),
        "vectors": draw_vectors(jax.random.fold_in(seeds[29], 71), 0),
        "up_bias": bell_draw(seeds[9], (FF,), 0.3, 1.5, (), jnp.float32),
        "rel_table": bell_draw(seeds[10], (NREL, HEADS), 1.0, 4.0, (), jnp.float32),
        "qkv_master": bell_draw(seeds[11], (D, 3 * D), D ** -0.5, 0.21875, ((0, 8), (1, 4)), jnp.float32),
        "qkv_mean": bell_draw(seeds[12], (D, 3 * D), (0.11 * (4 * D * D + 2 * D * FF) ** -0.5), 0.00061035156, ((0, 8), (1, 4)), jnp.float32),
        "qkv_square": jnp.clip(jnp.exp(math.log(1.130280646854942e-09) - 2.7725887 * jax.random.uniform(seeds[13], (D, 3 * D), jnp.float32) ** block_levels(seeds[13], (D, 3 * D), ((0, 8), (1, 4)), -0.2, 0.2)), 7.064254042843388e-11, 1.130280646854942e-09),
        "proj_master": bell_draw(seeds[14], (D, D), (D // 16) ** -0.5, 0.875, ((0, 8), (1, 4)), jnp.float32),
        "proj_mean": bell_draw(seeds[15], (D, D), (0.11 * (4 * D * D + 2 * D * FF) ** -0.5), 0.00061035156, ((0, 8), (1, 4)), jnp.float32),
        "proj_square": jnp.clip(jnp.exp(math.log(1.130280646854942e-09) - 2.7725887 * jax.random.uniform(seeds[16], (D, D), jnp.float32) ** block_levels(seeds[16], (D, D), ((0, 8), (1, 4)), -0.2, 0.2)), 7.064254042843388e-11, 1.130280646854942e-09),
        "up_master": bell_draw(seeds[17], (D, FF), D ** -0.5, 0.21875, ((0, 8), (1, 4)), jnp.float32),
        "up_mean": bell_draw(seeds[18], (D, FF), (0.11 * (4 * D * D + 2 * D * FF) ** -0.5), 0.00061035156, ((0, 8), (1, 4)), jnp.float32),
        "up_square": jnp.clip(jnp.exp(math.log(1.130280646854942e-09) - 2.7725887 * jax.random.uniform(seeds[19], (D, FF), jnp.float32) ** block_levels(seeds[19], (D, FF), ((0, 8), (1, 4)), -0.2, 0.2)), 7.064254042843388e-11, 1.130280646854942e-09),
        "down_master": bell_draw(seeds[20], (D, FF), FF ** -0.5, 0.109375, ((0, 8), (1, 4)), jnp.float32),
        "down_mean": bell_draw(seeds[21], (D, FF), (0.11 * (4 * D * D + 2 * D * FF) ** -0.5), 0.00061035156, ((0, 8), (1, 4)), jnp.float32),
        "down_square": jnp.clip(jnp.exp(math.log(1.130280646854942e-09) - 2.7725887 * jax.random.uniform(seeds[22], (D, FF), jnp.float32) ** block_levels(seeds[22], (D, FF), ((0, 8), (1, 4)), -0.2, 0.2)), 7.064254042843388e-11, 1.130280646854942e-09),
        "vector_mean": bell_draw(seeds[23], (10, D), (0.33 * (4 * D * D + 2 * D * FF) ** -0.5), 0.001953125, (), jnp.float32),
        "vector_square": jnp.clip(jnp.exp(jax.random.uniform(seeds[24], (10, D), jnp.float32, math.log(6.357828707947988e-10), math.log(1.017252593271678e-08))), 6.357828707947988e-10, 1.017252593271678e-08),
        "bias_mean": bell_draw(seeds[25], (FF,), (0.33 * (4 * D * D + 2 * D * FF) ** -0.5), 0.001953125, (), jnp.float32),
        "bias_square": jnp.clip(jnp.exp(jax.random.uniform(seeds[26], (FF,), jnp.float32, math.log(4.2385525644839106e-11), math.log(1.6954210257935642e-10))), 4.2385525644839106e-11, 1.6954210257935642e-10),
        "table_mean": bell_draw(seeds[27], (NREL, HEADS), (0.33 * (4 * D * D + 2 * D * FF) ** -0.5), 0.001953125, (), jnp.float32),
        "table_square": jnp.clip(jnp.exp(jax.random.uniform(seeds[28], (NREL, HEADS), jnp.float32, math.log(4.2385525644839106e-11), math.log(1.6954210257935642e-10))), 4.2385525644839106e-11, 1.6954210257935642e-10),
    }


@jax.custom_vjp
def low(v):
    return lax.optimization_barrier(v.astype(jnp.bfloat16)).astype(jnp.float32)

@jax.custom_vjp
def low_back(v):
    return v

def low_keep(v):
    return (low(v), None)

def low_pass(kept, grad):
    return (grad,)

def back_keep(v):
    return (v, None)

def back_low(kept, grad):
    return (low(grad),)
low.defvjp(low_keep, low_pass)
low_back.defvjp(back_keep, back_low)
exact_prec = lax.Precision.HIGHEST
norm_eps = 1e-06
clip_eps = 1e-06
max_norm = 1.0
beta_one = 0.9
beta_two = 0.999
adam_eps = 1e-08
rate_matrix = 0.05
rate_small = 0.4
weight_decay = 0.05

def layer_norm(values, gain_vec, shift_vec):
    center = values - lax.optimization_barrier(jnp.mean(values, -1, keepdims=True))
    spread = lax.optimization_barrier(jnp.mean(center * center, -1, keepdims=True))
    return center * lax.rsqrt(spread + norm_eps) * gain_vec + shift_vec

def gelu_exact(values):
    return 0.5 * values * (1.0 + jax.scipy.special.erf(values * 0.7071067811865476))

def rel_bias(rel_index, rel_table):
    blocks = rel_index.reshape(8, SEQ // 8, SEQ)

    def one_block(index_rows):
        onehot = (index_rows[:, :, None] == jnp.arange(NREL, dtype=jnp.int32)[None, None, :]).astype(jnp.float32)
        return jnp.einsum('qkr,rh->hqk', onehot, rel_table, precision=exact_prec)
    pieces = lax.map(jax.checkpoint(one_block), blocks)
    return jnp.transpose(pieces, (1, 0, 2, 3)).reshape(HEADS, SEQ, SEQ)

def group_forward(params, images_in, bias_all):
    qkv_w, proj_w, up_w, down_w, vectors, up_bias = params
    count = images_in.shape[0]
    first = low(layer_norm(images_in, vectors[4], vectors[5]))
    qkv_bias = jnp.concatenate([vectors[0], jnp.zeros_like(vectors[0]), vectors[1]])
    qkv = low(low_back(jnp.einsum('gsd,de->gse', first, qkv_w, precision=exact_prec) + qkv_bias))
    parts = qkv.reshape(count, SEQ, 3, HEADS, HEAD_DIM)
    query, keys, values = (parts[:, :, 0], parts[:, :, 1], parts[:, :, 2])
    scores = jnp.einsum('gqhd,gkhd->ghqk', query, keys, precision=exact_prec) * HEAD_DIM ** (-0.5) + bias_all[None]
    key_keep = (jnp.arange(SEQ) < VALID)[None, None, None, :]
    scores = jnp.where(key_keep, low_back(scores), -1e+30)
    probs = jax.nn.softmax(scores, -1)
    mixed = jnp.einsum('ghqk,gkhd->gqhd', low(probs), values, precision=exact_prec)
    heads_out = low(low_back(mixed.reshape(count, SEQ, D)))
    attn = low_back(jnp.einsum('gsd,de->gse', heads_out, proj_w, precision=exact_prec) + vectors[2])
    middle = images_in + vectors[8] * attn
    second = low(layer_norm(middle, vectors[6], vectors[7]))
    hidden_pre = low_back(jnp.einsum('gsd,df->gsf', second, up_w, precision=exact_prec) + up_bias)
    active = low(gelu_exact(hidden_pre))
    mlp_out = low_back(jnp.einsum('gsf,df->gsd', active, down_w, precision=exact_prec) + vectors[3])
    return middle + vectors[9] * mlp_out

def adam_update(master, mean, square, grad, rate, decay):
    mean_new = beta_one * mean + (1.0 - beta_one) * grad
    square_new = beta_two * square + (1.0 - beta_two) * grad * grad
    fix_one = 1.0 - beta_one ** STEP
    fix_two = 1.0 - beta_two ** STEP
    direction = mean_new / fix_one / (jnp.sqrt(square_new / fix_two) + adam_eps)
    master_new = master - rate * (direction + decay * master)
    return (mean_new, square_new, master_new)

def reference(block_in, out_grad, mim_mask, rel_index, qkv_weight, proj_weight, up_weight, down_weight, vectors, up_bias, rel_table, qkv_master, qkv_mean, qkv_square, proj_master, proj_mean, proj_square, up_master, up_mean, up_square, down_master, down_mean, down_square, vector_mean, vector_square, bias_mean, bias_square, table_mean, table_square):
    params = (qkv_weight.astype(jnp.float32), proj_weight.astype(jnp.float32), up_weight.astype(jnp.float32), down_weight.astype(jnp.float32), vectors, up_bias)
    inputs = block_in.astype(jnp.float32)
    cotangent = out_grad.astype(jnp.float32) * mim_mask[:, :, None].astype(jnp.float32)
    group_size = math.gcd(IMAGES, 16)

    def full_layer(params, rel_table, inputs):
        bias_all = rel_bias(rel_index, rel_table)
        grouped = inputs.reshape(IMAGES // group_size, group_size, SEQ, D)
        outputs = lax.map(lambda images_in: jax.checkpoint(group_forward)(params, images_in, bias_all), grouped)
        return outputs.reshape(IMAGES, SEQ, D)
    output, pullback = jax.vjp(full_layer, params, rel_table, inputs)
    grad_params, grad_table, grad_input = pullback(cotangent)
    grad_qkv, grad_proj, grad_up, grad_down, grad_vectors, grad_bias = grad_params
    everything = (grad_qkv, grad_proj, grad_up, grad_down, grad_vectors, grad_bias, grad_table)
    total = jnp.zeros((), jnp.float32)
    for grad in everything:
        total = total + jnp.sum(grad * grad)
    grad_norm = jnp.sqrt(total)
    clip = jnp.minimum(1.0, max_norm / (grad_norm + clip_eps))
    results = [output.astype(jnp.bfloat16), grad_input, grad_norm]
    for master, mean, square, grad in ((qkv_master, qkv_mean, qkv_square, grad_qkv), (proj_master, proj_mean, proj_square, grad_proj), (up_master, up_mean, up_square, grad_up), (down_master, down_mean, down_square, grad_down)):
        mean_new, square_new, master_new = adam_update(master, mean, square, clip * grad, rate_matrix, weight_decay)
        results += [mean_new, square_new, master_new, master_new.astype(jnp.bfloat16)]
    for master, mean, square, grad in ((vectors, vector_mean, vector_square, grad_vectors), (up_bias, bias_mean, bias_square, grad_bias), (rel_table, table_mean, table_square, grad_table)):
        mean_new, square_new, master_new = adam_update(master, mean, square, clip * grad, rate_small, 0.0)
        results += [mean_new, square_new, master_new]
    return tuple(results)
```

```python
import functools

import jax
import jax.numpy as jnp
from jax import lax
from jax.experimental import pallas as pl
from jax.experimental.pallas import tpu as pltpu
from jax.sharding import PartitionSpec as P

VALID = 197
STEP = 10
LANES = 128

norm_eps = 1e-06
clip_eps = 1e-06
max_norm = 1.0
beta_one = 0.9
beta_two = 0.999
adam_eps = 1e-08
rate_matrix = 0.05
rate_small = 0.4
weight_decay = 0.05
BF = jnp.bfloat16
F32 = jnp.float32
ROWS_ROWS = (((0,), (0,)), ((), ()))
COLS_COLS = (((1,), (1,)), ((), ()))
VMEM_LIMIT = 60000 * 1024


def mm(a, b):
    return jnp.dot(a, b, preferred_element_type=F32)


def mm_nt(a, b):
    return lax.dot_general(a, b, COLS_COLS, preferred_element_type=F32)


def mm_tn(a, b):
    return lax.dot_general(a, b, ROWS_ROWS, preferred_element_type=F32)


def params(steps=1):
    return pltpu.CompilerParams(
        dimension_semantics=("arbitrary",) * steps, vmem_limit_bytes=VMEM_LIMIT
    )


def whole(shape):
    zeros = (0,) * len(shape)
    return pl.BlockSpec(shape, lambda i: zeros)


def fixed(shape):
    zeros = (0,) * len(shape)
    return pl.BlockSpec(shape, lambda i: zeros, pipeline_mode=pl.Buffered(1))


def per_step(shape):
    rest = (0,) * (len(shape) - 1)
    return pl.BlockSpec((1,) + tuple(shape[1:]), lambda i: (i,) + rest)


def normalized(values):
    center = values - jnp.mean(values, -1, keepdims=True)
    factor = lax.rsqrt(jnp.mean(center * center, -1, keepdims=True) + norm_eps)
    return center * factor, factor


def layer_back(grad, normed, factor, gain_vec):
    scaled = grad * gain_vec
    return factor * (
        scaled
        - jnp.mean(scaled, -1, keepdims=True)
        - normed * jnp.mean(scaled * normed, -1, keepdims=True)
    )


def head_masks(pair_width, head_dim):
    lane = lax.broadcasted_iota(jnp.int32, (1, pair_width), 1)
    return [
        ((lane >= e * head_dim) & (lane < (e + 1) * head_dim)) for e in range(pair_width // head_dim)
    ]


def bias_kernel(idx_ref, tab_ref, out_ref):
    heads, seq = out_ref.shape[1], out_ref.shape[2]
    chunks = tab_ref.shape[1]

    def rows(step, carry):
        at = pl.multiple_of(step * 8, 8)
        for half in range(idx_ref.shape[2] // LANES):
            width = min(LANES, seq - half * LANES)
            index = idx_ref[0, pl.ds(at, 8), half * LANES : (half + 1) * LANES]
            low, high = index & (LANES - 1), index >> 7
            match = [high == c for c in range(chunks)]
            for h in range(heads):
                found = jnp.full((8, LANES), -1e30, F32)
                for c in range(chunks):
                    row = jnp.broadcast_to(tab_ref[h, c : c + 1, :], (8, LANES))
                    taken = jnp.take_along_axis(row, low, axis=1, mode="promise_in_bounds")
                    found = jnp.where(match[c], taken, found)
                out_ref[0, h, pl.ds(at, 8), half * LANES : half * LANES + width] = found[:, :width]
        return carry

    lax.fori_loop(0, seq // 8, rows, 0)


def bias_tables(indices, table_rows):
    both, seq, padded = indices.shape
    heads, chunks, _ = table_rows.shape
    return pl.pallas_call(
        bias_kernel,
        grid=(both,),
        in_specs=[per_step(indices.shape), whole(table_rows.shape)],
        out_specs=per_step((both, heads, seq, seq)),
        out_shape=jax.ShapeDtypeStruct((both, heads, seq, seq), F32),
        compiler_params=params(),
        name="bias_tables",
    )(indices, table_rows)


def table_kernel(idx_ref, ds_ref, out_ref):
    seq, heads, _ = ds_ref.shape
    chunks = out_ref.shape[0] // (2 * heads)
    out_ref[...] = jnp.zeros_like(out_ref)
    kinds = lax.broadcasted_iota(jnp.int32, (LANES, seq), 0)

    def one_key(j, total):
        index = idx_ref[pl.ds(j, 1), :]
        low, high = index & (LANES - 1), index >> 7
        onehot = jnp.where(jnp.broadcast_to(low, (LANES, seq)) == kinds, 1.0, 0.0).astype(BF)
        grads = ds_ref[j]
        top = grads.astype(BF).astype(F32)
        both = jnp.concatenate([top, grads - top], 0)
        high_all = jnp.broadcast_to(high, both.shape)
        parts = jnp.concatenate([jnp.where(high_all == c, both, 0.0) for c in range(chunks)], 0)
        return total + mm_nt(parts.astype(BF), onehot)

    out_ref[...] = lax.fori_loop(0, seq, one_key, jnp.zeros(out_ref.shape, F32), unroll=2)


def table_sums(index_t, grads, chunks):
    seq, heads, _ = grads.shape
    out = (chunks * 2 * heads, LANES)
    return pl.pallas_call(
        table_kernel,
        grid=(1,),
        in_specs=[whole(index_t.shape), whole(grads.shape)],
        out_specs=whole(out),
        out_shape=jax.ShapeDtypeStruct(out, F32),
        compiler_params=params(),
        name="table_sums",
    )(index_t, grads)


def front_kernel(heads, x_ref, wqkv_ref, wproj_ref, vec_ref, bias_ref, a_ref, qkv_ref, o_ref, attn_ref, hn_ref):
    width = x_ref.shape[2]
    head_dim = width // heads
    scale = head_dim ** (-0.5)
    x = x_ref[0].astype(F32)
    normed, _ = normalized(x)
    first = (normed * vec_ref[4:5, :] + vec_ref[5:6, :]).astype(BF)
    a_ref[0] = first
    for part, row in ((0, 0), (1, None), (2, 1)):
        cols = slice(part * width, (part + 1) * width)
        value = mm(first, wqkv_ref[:, cols])
        if row is not None:
            value = value + vec_ref[row : row + 1, :]
        qkv_ref[0, :, cols] = value.astype(BF)
    pair = LANES
    masks = head_masks(pair, head_dim)
    per = pair // head_dim

    def one_pair(g, carry):
        at = pl.multiple_of(g * pair, pair)
        q = qkv_ref[0, :, pl.ds(at, pair)]
        k = qkv_ref[0, :, pl.ds(at + width, pair)]
        v = qkv_ref[0, :, pl.ds(at + 2 * width, pair)]
        out = None
        for e in range(per):
            qm = q * jnp.where(masks[e], scale, 0.0).astype(BF)
            s = mm_nt(qm, k) + bias_ref[0, g * per + e]
            p = jnp.exp(s - jnp.max(s, -1, keepdims=True))
            p = p * (1.0 / jnp.sum(p, -1, keepdims=True))
            mixed = mm(p.astype(BF), v)
            out = mixed if out is None else jnp.where(masks[e], mixed, out)
        o_ref[0, :, pl.ds(at, pair)] = out.astype(BF)
        return carry

    lax.fori_loop(0, width // pair, one_pair, 0)
    attn = mm(o_ref[0], wproj_ref[...]) + vec_ref[2:3, :]
    attn_ref[0] = attn
    middle, _ = normalized(x + vec_ref[8:9, :] * attn)
    hn_ref[0] = (middle * vec_ref[6:7, :] + vec_ref[7:8, :]).astype(BF)


def front(x, qkv_weight, proj_weight, vectors, bias, heads):
    images, seq, width = x.shape
    shapes = [
        jax.ShapeDtypeStruct((images, seq, width), BF),
        jax.ShapeDtypeStruct((images, seq, 3 * width), BF),
        jax.ShapeDtypeStruct((images, seq, width), BF),
        jax.ShapeDtypeStruct((images, seq, width), F32),
        jax.ShapeDtypeStruct((images, seq, width), BF),
    ]
    return pl.pallas_call(
        functools.partial(front_kernel, heads),
        grid=(images,),
        in_specs=[
            per_step(x.shape),
            fixed(qkv_weight.shape),
            fixed(proj_weight.shape),
            fixed(vectors.shape),
            pl.BlockSpec((1,) + bias.shape[1:], lambda i: (0, 0, 0, 0), pipeline_mode=pl.Buffered(1)),
        ],
        out_specs=[per_step(s.shape) for s in shapes],
        out_shape=shapes,
        compiler_params=params(),
        name="front",
    )(x, qkv_weight, proj_weight, vectors, bias)


def mlp_kernel(chunk, hn_ref, gy_ref, vec_ref, bup_ref, wup_ref, wdn_ref, m_ref, dhn_ref, gup_ref, gdn_ref, gb_ref, dm_ref, z_ref, du_ref):
    tokens = hn_ref.shape[0]
    first = pl.program_id(0) == 0

    @pl.when(first)
    def _():
        m_ref[...] = jnp.zeros_like(m_ref)
        dhn_ref[...] = jnp.zeros_like(dhn_ref)

        def rows(step, carry):
            at = pl.ds(pl.multiple_of(step * chunk, chunk), chunk)
            dm_ref[at, :] = (vec_ref[9:10, :] * gy_ref[at, :].astype(F32)).astype(BF)
            return carry

        lax.fori_loop(0, tokens // chunk, rows, 0)

    gb_ref[...] = jnp.zeros_like(gb_ref)

    def rows(step, carry):
        at = pl.ds(pl.multiple_of(step * chunk, chunk), chunk)
        u = mm(hn_ref[at, :], wup_ref[0]) + bup_ref[0]
        gate = 0.5 * (1.0 + lax.erf(u * 0.7071067811865476))
        z = (u * gate).astype(BF)
        slope = gate + u * jnp.exp(-0.5 * u * u) * 0.3989422804014327
        z_ref[at, :] = z
        m_ref[at, :] += mm_nt(z, wdn_ref[0])
        du = (mm(dm_ref[at, :], wdn_ref[0]) * slope).astype(BF)
        du_ref[at, :] = du
        gb_ref[0] += jnp.sum(du.astype(F32), 0, keepdims=True)
        dhn_ref[at, :] += mm_nt(du, wup_ref[0])
        return carry

    lax.fori_loop(0, tokens // chunk, rows, 0)
    gdn_ref[0] = mm_tn(dm_ref[...], z_ref[...]).astype(BF)
    gup_ref[0] = mm_tn(hn_ref[...], du_ref[...]).astype(BF)


def mlp(hn, gy, vectors, up_bias, up_all, down_all, chunk):
    tokens, width = hn.shape
    blocks, _, hidden = up_all.shape
    shapes = [
        jax.ShapeDtypeStruct((tokens, width), F32),
        jax.ShapeDtypeStruct((tokens, width), F32),
        jax.ShapeDtypeStruct((blocks, width, hidden), BF),
        jax.ShapeDtypeStruct((blocks, width, hidden), BF),
        jax.ShapeDtypeStruct((blocks, 1, hidden), F32),
    ]
    return pl.pallas_call(
        functools.partial(mlp_kernel, chunk),
        grid=(blocks,),
        in_specs=[
            fixed(hn.shape),
            fixed(gy.shape),
            fixed(vectors.shape),
            per_step(up_bias.shape),
            per_step(up_all.shape),
            per_step(down_all.shape),
        ],
        out_specs=[fixed(s.shape) for s in shapes[:2]] + [per_step(s.shape) for s in shapes[2:]],
        out_shape=shapes,
        scratch_shapes=[
            pltpu.VMEM((tokens, width), BF),
            pltpu.VMEM((tokens, hidden), BF),
            pltpu.VMEM((tokens, hidden), BF),
        ],
        compiler_params=params(),
        name="mlp",
    )(hn, gy, vectors, up_bias, up_all, down_all)


def back_kernel(
    heads, x_ref, gy_ref, attn_ref, m_ref, dhn_ref, qkv_ref, wproj_ref, vec_ref, bias_ref,
    out_ref, dmid_ref, dat_ref, dqkv_ref, ds_ref, gvec_ref, gcol_ref, do_ref,
):
    seq, width = x_ref.shape[1], x_ref.shape[2]
    head_dim = width // heads
    scale = head_dim ** (-0.5)

    @pl.when(pl.program_id(0) == 0)
    def _():
        ds_ref[...] = jnp.zeros_like(ds_ref)
        gvec_ref[...] = jnp.zeros_like(gvec_ref)
        gcol_ref[...] = jnp.zeros_like(gcol_ref)

    attn = attn_ref[0]
    middle = x_ref[0].astype(F32) + vec_ref[8:9, :] * attn
    branch = m_ref[0] + vec_ref[3:4, :]
    out_ref[0] = (middle + vec_ref[9:10, :] * branch).astype(BF)
    cotangent = gy_ref[0].astype(F32)
    normed, factor = normalized(middle)
    dhn = dhn_ref[0]
    dmid = cotangent + layer_back(dhn, normed, factor, vec_ref[6:7, :])
    dmid_ref[0] = dmid
    dat = (vec_ref[8:9, :] * dmid).astype(BF)
    dat_ref[0] = dat
    down_in = (vec_ref[9:10, :] * cotangent).astype(BF)
    for row, value in enumerate(
        (dat.astype(F32), down_in.astype(F32), dhn * normed, dhn, dmid * attn, cotangent * branch)
    ):
        gvec_ref[row : row + 1, :] += jnp.sum(value, 0, keepdims=True)
    do_ref[...] = mm_nt(dat, wproj_ref[...]).astype(BF)
    pair = LANES
    masks = head_masks(pair, head_dim)
    per = pair // head_dim

    def one_pair(g, carry):
        at = pl.multiple_of(g * pair, pair)
        q = qkv_ref[0, :, pl.ds(at, pair)]
        k = qkv_ref[0, :, pl.ds(at + width, pair)]
        v = qkv_ref[0, :, pl.ds(at + 2 * width, pair)]
        do = do_ref[:, pl.ds(at, pair)]
        dq = dk = dv = None
        for e in range(per):
            pick = jnp.where(masks[e], scale, 0.0).astype(BF)
            keep = jnp.where(masks[e], 1.0, 0.0).astype(BF)
            qm, km, dom = q * pick, k * pick, do * keep
            s = mm_nt(k, qm) + bias_ref[0, g * per + e]
            p = jnp.exp(s - jnp.max(s, 0, keepdims=True))
            p = p * (1.0 / jnp.sum(p, 0, keepdims=True))
            dv_e = mm(p.astype(BF), dom)
            dp = mm_nt(v, dom)
            ds = (p * (dp - jnp.sum(dp * p, 0, keepdims=True))).astype(BF)
            ds_ref[g * per + e] += ds.astype(F32)
            dk_e = mm(ds, qm)
            dq_e = mm_tn(ds, km)
            dq = dq_e if dq is None else dq + dq_e
            dk = dk_e if dk is None else dk + dk_e
            dv = dv_e if dv is None else dv + dv_e
        for part, value in ((0, dq), (1, dk), (2, dv)):
            rounded = value.astype(BF)
            dqkv_ref[0, :, pl.ds(at + part * width, pair)] = rounded
            gcol_ref[:, pl.ds(at + part * width, pair)] += jnp.sum(rounded.astype(F32), 0, keepdims=True)
        return carry

    lax.fori_loop(0, width // pair, one_pair, 0)


def back(x, gy, attn, m, dhn, qkv, proj_weight, vectors, bias, heads):
    images, seq, width = x.shape
    shapes = [
        jax.ShapeDtypeStruct((images, seq, width), BF),
        jax.ShapeDtypeStruct((images, seq, width), F32),
        jax.ShapeDtypeStruct((images, seq, width), BF),
        jax.ShapeDtypeStruct((images, seq, 3 * width), BF),
        jax.ShapeDtypeStruct((heads, seq, seq), F32),
        jax.ShapeDtypeStruct((8, width), F32),
        jax.ShapeDtypeStruct((1, 3 * width), F32),
    ]
    return pl.pallas_call(
        functools.partial(back_kernel, heads),
        grid=(images,),
        in_specs=[per_step(v.shape) for v in (x, gy, attn, m, dhn, qkv)]
        + [
            fixed(proj_weight.shape),
            fixed(vectors.shape),
            pl.BlockSpec((1,) + bias.shape[1:], lambda i: (1, 0, 0, 0), pipeline_mode=pl.Buffered(1)),
        ],
        out_specs=[per_step(s.shape) for s in shapes[:4]] + [fixed(s.shape) for s in shapes[4:]],
        out_shape=shapes,
        scratch_shapes=[pltpu.VMEM((seq, width), BF)],
        compiler_params=params(),
        name="back",
    )(x, gy, attn, m, dhn, qkv, proj_weight, vectors, bias)


def grads_kernel(blocks, a_ref, dqkv_ref, o_ref, dat_ref, out_ref):
    wide_cols, thin_cols = dqkv_ref.shape[1] // blocks, dat_ref.shape[1] // blocks
    for n in range(blocks):
        out_ref[n, :, :wide_cols] = mm_tn(
            a_ref[...], dqkv_ref[:, n * wide_cols : (n + 1) * wide_cols]
        ).astype(BF)
        out_ref[n, :, wide_cols:] = mm_tn(
            o_ref[...], dat_ref[:, n * thin_cols : (n + 1) * thin_cols]
        ).astype(BF)


def attention_grads(first, dqkv, mixed, dat, blocks):
    width = first.shape[1]
    cols = (dqkv.shape[1] + dat.shape[1]) // blocks
    return pl.pallas_call(
        functools.partial(grads_kernel, blocks),
        grid=(1,),
        in_specs=[whole(v.shape) for v in (first, dqkv, mixed, dat)],
        out_specs=whole((blocks, width, cols)),
        out_shape=jax.ShapeDtypeStruct((blocks, width, cols), BF),
        compiler_params=params(),
        name="attention_grads",
    )(first, dqkv, mixed, dat)


def input_kernel(x_ref, dqkv_ref, dmid_ref, wqkv_ref, vec_ref, out_ref, gvec_ref):
    @pl.when(pl.program_id(0) == 0)
    def _():
        gvec_ref[...] = jnp.zeros_like(gvec_ref)

    da = mm_nt(dqkv_ref[0], wqkv_ref[...])
    normed, factor = normalized(x_ref[0].astype(F32))
    gvec_ref[0:1, :] += jnp.sum(da * normed, 0, keepdims=True)
    gvec_ref[1:2, :] += jnp.sum(da, 0, keepdims=True)
    out_ref[0] = dmid_ref[0] + layer_back(da, normed, factor, vec_ref[4:5, :])


def input_grads(x, dqkv, dmid, qkv_weight, vectors):
    images, seq, width = x.shape
    shapes = [
        jax.ShapeDtypeStruct((images, seq, width), F32),
        jax.ShapeDtypeStruct((8, width), F32),
    ]
    return pl.pallas_call(
        input_kernel,
        grid=(images,),
        in_specs=[per_step(v.shape) for v in (x, dqkv, dmid)]
        + [fixed(qkv_weight.shape), fixed(vectors.shape)],
        out_specs=[per_step(shapes[0].shape), fixed(shapes[1].shape)],
        out_shape=shapes,
        compiler_params=params(),
        name="input_grads",
    )(x, dqkv, dmid, qkv_weight, vectors)


def adam_update(master, mean, square, grad, rate, decay):
    mean_new = beta_one * mean + (1.0 - beta_one) * grad
    square_new = beta_two * square + (1.0 - beta_two) * grad * grad
    fix_one = 1.0 - beta_one**STEP
    fix_two = 1.0 - beta_two**STEP
    direction = mean_new / fix_one / (jnp.sqrt(square_new / fix_two) + adam_eps)
    return (mean_new, square_new, master - rate * (direction + decay * master))


def axis_bits():
    found = []
    for axis in ("narrow", "wide"):
        count = lax.axis_size(axis).bit_length() - 1
        found += [(axis, count - 1 - at) for at in range(count)]
    return found


def swap(value, axis, bit):
    size = lax.axis_size(axis)
    return lax.ppermute(value, axis, [(i, i ^ (1 << bit)) for i in range(size)])


def scattered_sum(grads, order):
    bits = axis_bits()
    pieces = [grads.reshape((2,) * len(bits) + grads.shape[2:])]
    for dim in order:
        axis, bit = bits[dim]
        mine = (lax.axis_index(axis) >> bit) & 1

        def half(piece, side):
            return lax.dynamic_slice_in_dim(piece, side, 1, dim)

        sent = sum(half(p, 1 - mine).astype(F32) for p in pieces).astype(BF)
        arrived = swap(sent, axis, bit)
        pieces = [half(p, mine) for p in pieces] + [arrived]
    return sum(p.astype(F32) for p in pieces).reshape(grads.shape[2:])


def summed(value):
    for axis, bit in reversed(axis_bits()):
        value = value + swap(value, axis, bit)
    return value


def local_work(
    block_in, out_grad, mim_mask, rel_index, qkv_weight, proj_weight, up_all, down_all, vectors, up_bias, rel_table
):
    images, seq, width = block_in.shape
    table_rows, heads = rel_table.shape
    blocks, _, hidden = up_all.shape
    tokens = images * seq
    chunks = -(-table_rows // LANES)
    padded_seq = -(-seq // LANES) * LANES
    key_at = jnp.arange(seq, dtype=jnp.int32)
    index = jnp.where(key_at[None, :] < VALID, rel_index, chunks * LANES)
    index_t = index.T
    indices = jnp.pad(jnp.stack([index, index_t]), ((0, 0), (0, 0), (0, padded_seq - seq)))
    table_t = jnp.pad(rel_table, ((0, chunks * LANES - table_rows), (0, 0))).T.reshape(heads, chunks, LANES)
    bias = bias_tables(indices, table_t)
    gy = out_grad * mim_mask.astype(BF)[:, :, None]
    first, qkv, mixed, attn, hn = front(block_in, qkv_weight, proj_weight, vectors, bias, heads)
    flat = lambda v: v.reshape(tokens, v.shape[-1])
    m, dhn, grad_up, grad_down, grad_bias = mlp(
        flat(hn), flat(gy), vectors, up_bias.reshape(blocks, 1, hidden), up_all, down_all, seq
    )
    fold = lambda v: v.reshape(images, seq, width)
    block_out, dmid, dat, dqkv, ds, gvec, gcol = back(
        block_in, gy, attn, fold(m), fold(dhn), qkv, proj_weight, vectors, bias, heads
    )
    grad_attn = attention_grads(flat(first), flat(dqkv), flat(mixed), flat(dat), blocks)
    input_grad, gvec_one = input_grads(block_in, dqkv, dmid, qkv_weight, vectors)
    by_key = jnp.pad(ds.transpose(1, 0, 2), ((0, 0), (0, (-heads) % 8), (0, 0)))
    sums = table_sums(index_t, by_key, chunks)
    sums = sums.reshape(chunks, 2, -1, LANES).sum(1)[:, :heads]
    grad_table = sums.transpose(1, 0, 2).reshape(heads * chunks * LANES // width, width)
    small = jnp.concatenate(
        [
            gcol[:, :width],
            gcol[:, 2 * width :],
            gvec[:2],
            gvec_one[:2],
            gvec[2:6],
            grad_bias.reshape(-1, width),
            grad_table,
        ]
    )
    return block_out, input_grad, grad_attn, grad_up, grad_down, small


def shards(
    block_in,
    out_grad,
    mim_mask,
    rel_index,
    qkv_weight,
    proj_weight,
    up_weight,
    down_weight,
    vectors,
    up_bias,
    rel_table,
    qkv_master,
    qkv_mean,
    qkv_square,
    proj_master,
    proj_mean,
    proj_square,
    up_master,
    up_mean,
    up_square,
    down_master,
    down_mean,
    down_square,
    vector_mean,
    vector_square,
    bias_mean,
    bias_square,
    table_mean,
    table_square,
):
    width = block_in.shape[2]
    table_rows, heads = rel_table.shape
    wide = lax.axis_size("wide")
    narrow = lax.axis_size("narrow")
    up_all = lax.all_gather(up_weight, "narrow", axis=0)
    down_all = lax.all_gather(down_weight, "narrow", axis=0)
    block_out, input_grad, grad_attn, grad_up, grad_down, small = local_work(
        block_in, out_grad, mim_mask, rel_index, qkv_weight, proj_weight, up_all, down_all, vectors, up_bias, rel_table
    )
    small = summed(small)
    lead = [n for n in range(narrow.bit_length() - 1)]
    trail = [len(lead) + n for n in range(wide.bit_length() - 1)]
    order_a = lead[::-1] + trail[::-1]
    order_b = lead[-1:] + trail[::-1] + lead[:-1]
    cut = lambda v: v.reshape(narrow, wide, width // wide, v.shape[-1])
    up_shard = scattered_sum(cut(grad_up), order_a)
    down_shard = scattered_sum(cut(grad_down), order_b)
    grad_attn = cut(grad_attn)
    half = grad_attn.shape[2] // 2
    attn_shard = jnp.concatenate(
        [scattered_sum(grad_attn[:, :, :half], order_a), scattered_sum(grad_attn[:, :, half:], order_b)]
    )
    split = qkv_master.shape[1]
    qkv_shard, proj_shard = attn_shard[:, :split], attn_shard[:, split:]
    shard_squares = jnp.sum(attn_shard * attn_shard) + jnp.sum(up_shard * up_shard) + jnp.sum(down_shard * down_shard)
    large_squares = summed(jnp.full((1, LANES), shard_squares))[0, 0]
    small_squares = jnp.sum(small * small)
    grad_vectors = small[:10]
    grad_bias = small[10 : 10 + up_bias.shape[0] // width].reshape(up_bias.shape)
    grad_table = small[10 + up_bias.shape[0] // width :].reshape(heads, -1).T[:table_rows]
    grad_norm = jnp.sqrt(large_squares + small_squares)
    clip = jnp.minimum(1.0, max_norm / (grad_norm + clip_eps))
    results = [block_out, input_grad, grad_norm]
    for master, mean, square, grad in (
        (qkv_master, qkv_mean, qkv_square, qkv_shard),
        (proj_master, proj_mean, proj_square, proj_shard),
        (up_master, up_mean, up_square, up_shard),
        (down_master, down_mean, down_square, down_shard),
    ):
        mean_new, square_new, master_new = adam_update(
            master, mean, square, clip * grad, rate_matrix, weight_decay
        )
        results += [mean_new, square_new, master_new, master_new.astype(jnp.bfloat16)]
    for master, mean, square, grad in (
        (vectors, vector_mean, vector_square, grad_vectors),
        (up_bias, bias_mean, bias_square, grad_bias),
        (rel_table, table_mean, table_square, grad_table),
    ):
        mean_new, square_new, master_new = adam_update(
            master, mean, square, clip * grad, rate_small, 0.0
        )
        results += [mean_new, square_new, master_new]
    return tuple(results)


def solution(mesh):
    token = P(("wide", "narrow"), None, None)
    whole_spec = P()
    shard = P("wide", "narrow")
    in_specs = (
        (token, token, P(("wide", "narrow"), None))
        + (whole_spec,) * 3
        + (P(None, "narrow"),) * 2
        + (whole_spec,) * 3
        + (shard,) * 12
        + (whole_spec,) * 6
    )
    out_specs = (token, token, whole_spec) + (shard,) * 16 + (whole_spec,) * 9
    return jax.shard_map(shards, mesh=mesh, in_specs=in_specs, out_specs=out_specs, check_vma=False)
```

```python
import functools

import jax
import jax.numpy as jnp
from jax import lax
from jax.experimental import pallas as pl
from jax.experimental.pallas import tpu as pltpu
from jax.sharding import PartitionSpec as P

VALID = 197
STEP = 10
LANES = 128

norm_eps = 1e-06
clip_eps = 1e-06
max_norm = 1.0
beta_one = 0.9
beta_two = 0.999
adam_eps = 1e-08
rate_matrix = 0.05
rate_small = 0.4
weight_decay = 0.05
BF = jnp.bfloat16
F32 = jnp.float32
ROWS_ROWS = (((0,), (0,)), ((), ()))
COLS_COLS = (((1,), (1,)), ((), ()))
VMEM_LIMIT = 60000 * 1024
UNROLL_F = 3
UNROLL_B = 3
UNROLL_T = 8


def mm(a, b):
    return jnp.dot(a, b, preferred_element_type=F32)


def mm_nt(a, b):
    return lax.dot_general(a, b, COLS_COLS, preferred_element_type=F32)


def mm_tn(a, b):
    return lax.dot_general(a, b, ROWS_ROWS, preferred_element_type=F32)


def params(steps=1):
    return pltpu.CompilerParams(
        dimension_semantics=("arbitrary",) * steps, vmem_limit_bytes=VMEM_LIMIT
    )


def whole(shape):
    zeros = (0,) * len(shape)
    return pl.BlockSpec(shape, lambda i: zeros)


def fixed(shape):
    zeros = (0,) * len(shape)
    return pl.BlockSpec(shape, lambda i: zeros, pipeline_mode=pl.Buffered(1))


def per_step(shape):
    rest = (0,) * (len(shape) - 1)
    return pl.BlockSpec((1,) + tuple(shape[1:]), lambda i: (i,) + rest)


def normalized(values):
    center = values - jnp.mean(values, -1, keepdims=True)
    factor = lax.rsqrt(jnp.mean(center * center, -1, keepdims=True) + norm_eps)
    return center * factor, factor


def layer_back(grad, normed, factor, gain_vec):
    scaled = grad * gain_vec
    return factor * (
        scaled
        - jnp.mean(scaled, -1, keepdims=True)
        - normed * jnp.mean(scaled * normed, -1, keepdims=True)
    )


def head_masks(pair_width, head_dim):
    lane = lax.broadcasted_iota(jnp.int32, (1, pair_width), 1)
    return [
        ((lane >= e * head_dim) & (lane < (e + 1) * head_dim)) for e in range(pair_width // head_dim)
    ]


def bias_kernel(idx_ref, tab_ref, out_ref, back_ref, work_ref):
    heads, seq = out_ref.shape[0], out_ref.shape[1]
    chunks = tab_ref.shape[1]

    def rows(step, carry):
        at = pl.multiple_of(step * 8, 8)
        for half in range(idx_ref.shape[1] // LANES):
            cols = slice(half * LANES, (half + 1) * LANES)
            index = idx_ref[pl.ds(at, 8), cols]
            low, high = index & (LANES - 1), index >> 7
            match = [high == c for c in range(chunks)]
            for h in range(heads):
                found = jnp.full((8, LANES), -1e30, F32)
                for c in range(chunks):
                    row = jnp.broadcast_to(tab_ref[h, c : c + 1, :], (8, LANES))
                    taken = jnp.take_along_axis(row, low, axis=1, mode="promise_in_bounds")
                    found = jnp.where(match[c], taken, found)
                work_ref[h, pl.ds(at, 8), cols] = found
        return carry

    lax.fori_loop(0, seq // 8, rows, 0)

    def turn(h, carry):
        out_ref[h] = work_ref[h, :seq, :seq]
        back_ref[h] = work_ref[h].T[:seq, :seq]
        return carry

    lax.fori_loop(0, heads, turn, 0)


def bias_tables(index, table_rows):
    seq, padded = index.shape
    heads, chunks, _ = table_rows.shape
    shape = (heads, seq, seq)
    return pl.pallas_call(
        bias_kernel,
        grid=(1,),
        in_specs=[whole(index.shape), whole(table_rows.shape)],
        out_specs=[whole(shape)] * 2,
        out_shape=[jax.ShapeDtypeStruct(shape, F32)] * 2,
        scratch_shapes=[pltpu.VMEM((heads, padded, padded), F32)],
        compiler_params=params(),
        name="bias_tables",
    )(index, table_rows)


def table_kernel(idx_ref, ds_ref, out_ref):
    seq, heads, _ = ds_ref.shape
    chunks = out_ref.shape[0] // (2 * heads)
    out_ref[...] = jnp.zeros_like(out_ref)
    kinds = lax.broadcasted_iota(jnp.int32, (LANES, seq), 0)

    def one_key(j, total):
        index = idx_ref[pl.ds(j, 1), :]
        low, high = index & (LANES - 1), index >> 7
        onehot = jnp.where(jnp.broadcast_to(low, (LANES, seq)) == kinds, 1.0, 0.0).astype(BF)
        grads = ds_ref[j]
        top = grads.astype(BF).astype(F32)
        both = jnp.concatenate([top, grads - top], 0)
        high_all = jnp.broadcast_to(high, both.shape)
        parts = jnp.concatenate([jnp.where(high_all == c, both, 0.0) for c in range(chunks)], 0)
        return total + mm_nt(parts.astype(BF), onehot)

    out_ref[...] = lax.fori_loop(0, seq, one_key, jnp.zeros(out_ref.shape, F32), unroll=UNROLL_T)


def table_sums(index_t, grads, chunks):
    seq, heads, _ = grads.shape
    out = (chunks * 2 * heads, LANES)
    return pl.pallas_call(
        table_kernel,
        grid=(1,),
        in_specs=[whole(index_t.shape), whole(grads.shape)],
        out_specs=whole(out),
        out_shape=jax.ShapeDtypeStruct(out, F32),
        compiler_params=params(),
        name="table_sums",
    )(index_t, grads)


def front_kernel(heads, x_ref, wqkv_ref, wproj_ref, vec_ref, bias_ref, a_ref, qkv_ref, o_ref, attn_ref, hn_ref):
    width = x_ref.shape[2]
    head_dim = width // heads
    scale = head_dim ** (-0.5)
    x = x_ref[0].astype(F32)
    normed, _ = normalized(x)
    first = (normed * vec_ref[4:5, :] + vec_ref[5:6, :]).astype(BF)
    a_ref[0] = first
    for part, row in ((0, 0), (1, None), (2, 1)):
        cols = slice(part * width, (part + 1) * width)
        value = mm(first, wqkv_ref[:, cols])
        if row is not None:
            value = value + vec_ref[row : row + 1, :]
        qkv_ref[0, :, cols] = value.astype(BF)
    pair = LANES
    masks = head_masks(pair, head_dim)
    per = pair // head_dim

    def one_pair(g, carry):
        at = pl.multiple_of(g * pair, pair)
        q = qkv_ref[0, :, pl.ds(at, pair)]
        k = qkv_ref[0, :, pl.ds(at + width, pair)]
        v = qkv_ref[0, :, pl.ds(at + 2 * width, pair)]
        out = None
        for e in range(per):
            qm = q * jnp.where(masks[e], scale, 0.0).astype(BF)
            s = mm_nt(qm, k) + bias_ref[g * per + e]
            p = jnp.exp(s - jnp.max(s, -1, keepdims=True))
            p = p * (1.0 / jnp.sum(p, -1, keepdims=True))
            mixed = mm(p.astype(BF), v)
            out = mixed if out is None else jnp.where(masks[e], mixed, out)
        o_ref[0, :, pl.ds(at, pair)] = out.astype(BF)
        return carry

    lax.fori_loop(0, width // pair, one_pair, 0, unroll=UNROLL_F)
    attn = mm(o_ref[0], wproj_ref[...]) + vec_ref[2:3, :]
    attn_ref[0] = attn
    middle, _ = normalized(x + vec_ref[8:9, :] * attn)
    hn_ref[0] = (middle * vec_ref[6:7, :] + vec_ref[7:8, :]).astype(BF)


def front(x, qkv_weight, proj_weight, vectors, bias, heads):
    images, seq, width = x.shape
    shapes = [
        jax.ShapeDtypeStruct((images, seq, width), BF),
        jax.ShapeDtypeStruct((images, seq, 3 * width), BF),
        jax.ShapeDtypeStruct((images, seq, width), BF),
        jax.ShapeDtypeStruct((images, seq, width), F32),
        jax.ShapeDtypeStruct((images, seq, width), BF),
    ]
    return pl.pallas_call(
        functools.partial(front_kernel, heads),
        grid=(images,),
        in_specs=[
            per_step(x.shape),
            fixed(qkv_weight.shape),
            fixed(proj_weight.shape),
            fixed(vectors.shape),
            fixed(bias.shape),
        ],
        out_specs=[per_step(s.shape) for s in shapes],
        out_shape=shapes,
        compiler_params=params(),
        name="front",
    )(x, qkv_weight, proj_weight, vectors, bias)


def mlp_in_kernel(chunk, hn_ref, gy_ref, vec_ref, bup_ref, wup_ref, z_ref, slope_ref, gdn_ref, dm_ref, turned_ref):
    tokens = hn_ref.shape[0]

    @pl.when(pl.program_id(0) == 0)
    def _():
        def rows(step, carry):
            at = pl.ds(pl.multiple_of(step * chunk, chunk), chunk)
            dm_ref[at, :] = (vec_ref[9:10, :] * gy_ref[at, :].astype(F32)).astype(BF)
            return carry

        lax.fori_loop(0, tokens // chunk, rows, 0)
        turned_ref[...] = dm_ref[...].T

    def rows(step, carry):
        at = pl.ds(pl.multiple_of(step * chunk, chunk), chunk)
        u = mm(hn_ref[at, :], wup_ref[0]) + bup_ref[0]
        gate = 0.5 * (1.0 + lax.erf(u * 0.7071067811865476))
        z_ref[0, at, :] = (u * gate).astype(BF)
        slope_ref[0, at, :] = (gate + u * jnp.exp(-0.5 * u * u) * 0.3989422804014327).astype(BF)
        return carry

    lax.fori_loop(0, tokens // chunk, rows, 0)
    gdn_ref[0] = mm(turned_ref[...], z_ref[0]).astype(BF)


def mlp_in(hn, gy, vectors, up_bias, up_all, chunk):
    tokens, width = hn.shape
    blocks, _, hidden = up_all.shape
    shapes = [
        jax.ShapeDtypeStruct((blocks, tokens, hidden), BF),
        jax.ShapeDtypeStruct((blocks, tokens, hidden), BF),
        jax.ShapeDtypeStruct((blocks, width, hidden), BF),
    ]
    return pl.pallas_call(
        functools.partial(mlp_in_kernel, chunk),
        grid=(blocks,),
        in_specs=[
            fixed(hn.shape),
            fixed(gy.shape),
            fixed(vectors.shape),
            per_step(up_bias.shape),
            per_step(up_all.shape),
        ],
        out_specs=[per_step(s.shape) for s in shapes] + [fixed((tokens, width))],
        out_shape=shapes + [jax.ShapeDtypeStruct((tokens, width), BF)],
        scratch_shapes=[pltpu.VMEM((width, tokens), BF)],
        compiler_params=params(),
        name="mlp_in",
    )(hn, gy, vectors, up_bias, up_all)


def mlp_out_kernel(chunk, hn_ref, dm_ref, z_ref, slope_ref, wup_ref, wdn_ref, m_ref, dhn_ref, gup_ref, gb_ref, du_ref, turned_ref):
    tokens = hn_ref.shape[0]

    @pl.when(pl.program_id(0) == 0)
    def _():
        m_ref[...] = jnp.zeros_like(m_ref)
        dhn_ref[...] = jnp.zeros_like(dhn_ref)
        turned_ref[...] = hn_ref[...].T

    gb_ref[...] = jnp.zeros_like(gb_ref)

    def rows(step, carry):
        at = pl.ds(pl.multiple_of(step * chunk, chunk), chunk)
        m_ref[at, :] += mm_nt(z_ref[0, at, :], wdn_ref[0])
        du = (mm(dm_ref[at, :], wdn_ref[0]) * slope_ref[0, at, :].astype(F32)).astype(BF)
        du_ref[at, :] = du
        gb_ref[0] += jnp.sum(du.astype(F32), 0, keepdims=True)
        dhn_ref[at, :] += mm_nt(du, wup_ref[0])
        return carry

    lax.fori_loop(0, tokens // chunk, rows, 0)
    gup_ref[0] = mm(turned_ref[...], du_ref[...]).astype(BF)


def mlp_out(hn, dm, z, slope, up_all, down_all, chunk):
    tokens, width = hn.shape
    blocks, _, hidden = up_all.shape
    shapes = [
        jax.ShapeDtypeStruct((tokens, width), F32),
        jax.ShapeDtypeStruct((tokens, width), F32),
        jax.ShapeDtypeStruct((blocks, width, hidden), BF),
        jax.ShapeDtypeStruct((blocks, 1, hidden), F32),
    ]
    return pl.pallas_call(
        functools.partial(mlp_out_kernel, chunk),
        grid=(blocks,),
        in_specs=[fixed(hn.shape), fixed(dm.shape)] + [per_step(v.shape) for v in (z, slope, up_all, down_all)],
        out_specs=[fixed(s.shape) for s in shapes[:2]] + [per_step(s.shape) for s in shapes[2:]],
        out_shape=shapes,
        scratch_shapes=[pltpu.VMEM((tokens, hidden), BF), pltpu.VMEM((width, tokens), BF)],
        compiler_params=params(),
        name="mlp_out",
    )(hn, dm, z, slope, up_all, down_all)


def back_kernel(
    heads, x_ref, gy_ref, attn_ref, m_ref, dhn_ref, qkv_ref, wproj_ref, vec_ref, bias_ref,
    out_ref, dmid_ref, dat_ref, dqkv_ref, ds_ref, gvec_ref, gcol_ref, do_ref,
):
    seq, width = x_ref.shape[1], x_ref.shape[2]
    head_dim = width // heads
    scale = head_dim ** (-0.5)

    @pl.when(pl.program_id(0) == 0)
    def _():
        ds_ref[...] = jnp.zeros_like(ds_ref)
        gvec_ref[...] = jnp.zeros_like(gvec_ref)
        gcol_ref[...] = jnp.zeros_like(gcol_ref)

    attn = attn_ref[0]
    middle = x_ref[0].astype(F32) + vec_ref[8:9, :] * attn
    branch = m_ref[0] + vec_ref[3:4, :]
    out_ref[0] = (middle + vec_ref[9:10, :] * branch).astype(BF)
    cotangent = gy_ref[0].astype(F32)
    normed, factor = normalized(middle)
    dhn = dhn_ref[0]
    dmid = cotangent + layer_back(dhn, normed, factor, vec_ref[6:7, :])
    dmid_ref[0] = dmid
    dat = (vec_ref[8:9, :] * dmid).astype(BF)
    dat_ref[0] = dat
    down_in = (vec_ref[9:10, :] * cotangent).astype(BF)
    for row, value in enumerate(
        (dat.astype(F32), down_in.astype(F32), dhn * normed, dhn, dmid * attn, cotangent * branch)
    ):
        gvec_ref[row : row + 1, :] += jnp.sum(value, 0, keepdims=True)
    do_ref[...] = mm_nt(dat, wproj_ref[...]).astype(BF)
    pair = LANES
    masks = head_masks(pair, head_dim)
    per = pair // head_dim

    def one_pair(g, carry):
        at = pl.multiple_of(g * pair, pair)
        q = qkv_ref[0, :, pl.ds(at, pair)]
        k = qkv_ref[0, :, pl.ds(at + width, pair)]
        v = qkv_ref[0, :, pl.ds(at + 2 * width, pair)]
        do = do_ref[:, pl.ds(at, pair)]
        dq = dk = dv = None
        for e in range(per):
            pick = jnp.where(masks[e], scale, 0.0).astype(BF)
            keep = jnp.where(masks[e], 1.0, 0.0).astype(BF)
            qm, km, dom = q * pick, k * pick, do * keep
            s = mm_nt(k, qm) + bias_ref[g * per + e]
            p = jnp.exp(s - jnp.max(s, 0, keepdims=True))
            p = p * (1.0 / jnp.sum(p, 0, keepdims=True))
            dv_e = mm(p.astype(BF), dom)
            dp = mm_nt(v, dom)
            ds = (p * (dp - jnp.sum(dp * p, 0, keepdims=True))).astype(BF)
            ds_ref[g * per + e] += ds.astype(F32)
            dk_e = mm(ds, qm)
            dq_e = mm_tn(ds, km)
            dq = dq_e if dq is None else dq + dq_e
            dk = dk_e if dk is None else dk + dk_e
            dv = dv_e if dv is None else dv + dv_e
        for part, value in ((0, dq), (1, dk), (2, dv)):
            rounded = value.astype(BF)
            dqkv_ref[0, :, pl.ds(at + part * width, pair)] = rounded
            gcol_ref[:, pl.ds(at + part * width, pair)] += jnp.sum(rounded.astype(F32), 0, keepdims=True)
        return carry

    lax.fori_loop(0, width // pair, one_pair, 0, unroll=UNROLL_B)


def back(x, gy, attn, m, dhn, qkv, proj_weight, vectors, bias, heads):
    images, seq, width = x.shape
    shapes = [
        jax.ShapeDtypeStruct((images, seq, width), BF),
        jax.ShapeDtypeStruct((images, seq, width), F32),
        jax.ShapeDtypeStruct((images, seq, width), BF),
        jax.ShapeDtypeStruct((images, seq, 3 * width), BF),
        jax.ShapeDtypeStruct((heads, seq, seq), F32),
        jax.ShapeDtypeStruct((8, width), F32),
        jax.ShapeDtypeStruct((1, 3 * width), F32),
    ]
    return pl.pallas_call(
        functools.partial(back_kernel, heads),
        grid=(images,),
        in_specs=[per_step(v.shape) for v in (x, gy, attn, m, dhn, qkv)]
        + [
            fixed(proj_weight.shape),
            fixed(vectors.shape),
            fixed(bias.shape),
        ],
        out_specs=[per_step(s.shape) for s in shapes[:4]] + [fixed(s.shape) for s in shapes[4:]],
        out_shape=shapes,
        scratch_shapes=[pltpu.VMEM((seq, width), BF)],
        compiler_params=params(),
        name="back",
    )(x, gy, attn, m, dhn, qkv, proj_weight, vectors, bias)


def grads_kernel(blocks, a_ref, dqkv_ref, o_ref, dat_ref, out_ref, turned_a, turned_o):
    wide_cols, thin_cols = dqkv_ref.shape[1] // blocks, dat_ref.shape[1] // blocks
    turned_a[...] = a_ref[...].T
    turned_o[...] = o_ref[...].T
    for n in range(blocks):
        out_ref[n, :, :wide_cols] = mm(
            turned_a[...], dqkv_ref[:, n * wide_cols : (n + 1) * wide_cols]
        ).astype(BF)
        out_ref[n, :, wide_cols:] = mm(
            turned_o[...], dat_ref[:, n * thin_cols : (n + 1) * thin_cols]
        ).astype(BF)


def attention_grads(first, dqkv, mixed, dat, blocks):
    width = first.shape[1]
    cols = (dqkv.shape[1] + dat.shape[1]) // blocks
    return pl.pallas_call(
        functools.partial(grads_kernel, blocks),
        grid=(1,),
        in_specs=[whole(v.shape) for v in (first, dqkv, mixed, dat)],
        out_specs=whole((blocks, width, cols)),
        out_shape=jax.ShapeDtypeStruct((blocks, width, cols), BF),
        scratch_shapes=[pltpu.VMEM((width, first.shape[0]), BF)] * 2,
        compiler_params=params(),
        name="attention_grads",
    )(first, dqkv, mixed, dat)


def input_kernel(x_ref, dqkv_ref, dmid_ref, wqkv_ref, vec_ref, out_ref, gvec_ref):
    @pl.when(pl.program_id(0) == 0)
    def _():
        gvec_ref[...] = jnp.zeros_like(gvec_ref)

    da = mm_nt(dqkv_ref[0], wqkv_ref[...])
    normed, factor = normalized(x_ref[0].astype(F32))
    gvec_ref[0:1, :] += jnp.sum(da * normed, 0, keepdims=True)
    gvec_ref[1:2, :] += jnp.sum(da, 0, keepdims=True)
    out_ref[0] = dmid_ref[0] + layer_back(da, normed, factor, vec_ref[4:5, :])


def input_grads(x, dqkv, dmid, qkv_weight, vectors):
    images, seq, width = x.shape
    shapes = [
        jax.ShapeDtypeStruct((images, seq, width), F32),
        jax.ShapeDtypeStruct((8, width), F32),
    ]
    return pl.pallas_call(
        input_kernel,
        grid=(images,),
        in_specs=[per_step(v.shape) for v in (x, dqkv, dmid)]
        + [fixed(qkv_weight.shape), fixed(vectors.shape)],
        out_specs=[per_step(shapes[0].shape), fixed(shapes[1].shape)],
        out_shape=shapes,
        compiler_params=params(),
        name="input_grads",
    )(x, dqkv, dmid, qkv_weight, vectors)


def adam_update(master, mean, square, grad, rate, decay):
    mean_new = beta_one * mean + (1.0 - beta_one) * grad
    square_new = beta_two * square + (1.0 - beta_two) * grad * grad
    fix_one = 1.0 - beta_one**STEP
    fix_two = 1.0 - beta_two**STEP
    direction = mean_new / fix_one / (jnp.sqrt(square_new / fix_two) + adam_eps)
    return (mean_new, square_new, master - rate * (direction + decay * master))


def axis_bits():
    found = []
    for axis in ("narrow", "wide"):
        count = lax.axis_size(axis).bit_length() - 1
        found += [(axis, count - 1 - at) for at in range(count)]
    return found


def swap(value, axis, bit):
    size = lax.axis_size(axis)
    return lax.ppermute(value, axis, [(i, i ^ (1 << bit)) for i in range(size)])


def scattered_sum(grads, order):
    bits = axis_bits()
    pieces = [grads.reshape((2,) * len(bits) + grads.shape[2:])]
    for dim in order:
        axis, bit = bits[dim]
        mine = (lax.axis_index(axis) >> bit) & 1

        def half(piece, side):
            return lax.dynamic_slice_in_dim(piece, side, 1, dim)

        sent = sum(half(p, 1 - mine).astype(F32) for p in pieces).astype(BF)
        arrived = swap(sent, axis, bit)
        pieces = [half(p, mine) for p in pieces] + [arrived]
    return sum(p.astype(F32) for p in pieces).reshape(grads.shape[2:])


def summed(value):
    for axis, bit in reversed(axis_bits()):
        value = value + swap(value, axis, bit)
    return value


def local_work(
    block_in, out_grad, mim_mask, rel_index, qkv_weight, proj_weight, up_all, down_all, vectors, up_bias, rel_table
):
    images, seq, width = block_in.shape
    table_rows, heads = rel_table.shape
    blocks, _, hidden = up_all.shape
    tokens = images * seq
    chunks = -(-table_rows // LANES)
    padded_seq = -(-seq // LANES) * LANES
    key_at = jnp.arange(seq, dtype=jnp.int32)
    index = jnp.where(key_at[None, :] < VALID, rel_index, chunks * LANES)
    index_t = index.T
    padded = jnp.pad(index, ((0, 0), (0, padded_seq - seq)))
    table_t = jnp.pad(rel_table, ((0, chunks * LANES - table_rows), (0, 0))).T.reshape(heads, chunks, LANES)
    bias, bias_t = bias_tables(padded, table_t)
    gy = out_grad * mim_mask.astype(BF)[:, :, None]
    first, qkv, mixed, attn, hn = front(block_in, qkv_weight, proj_weight, vectors, bias, heads)
    flat = lambda v: v.reshape(tokens, v.shape[-1])
    z, slope, grad_down, dm = mlp_in(flat(hn), flat(gy), vectors, up_bias.reshape(blocks, 1, hidden), up_all, seq)
    m, dhn, grad_up, grad_bias = mlp_out(flat(hn), dm, z, slope, up_all, down_all, seq)
    fold = lambda v: v.reshape(images, seq, width)
    block_out, dmid, dat, dqkv, ds, gvec, gcol = back(
        block_in, gy, attn, fold(m), fold(dhn), qkv, proj_weight, vectors, bias_t, heads
    )
    grad_attn = attention_grads(flat(first), flat(dqkv), flat(mixed), flat(dat), blocks)
    input_grad, gvec_one = input_grads(block_in, dqkv, dmid, qkv_weight, vectors)
    by_key = jnp.pad(ds.transpose(1, 0, 2), ((0, 0), (0, (-heads) % 8), (0, 0)))
    sums = table_sums(index_t, by_key, chunks)
    sums = sums.reshape(chunks, 2, -1, LANES).sum(1)[:, :heads]
    grad_table = sums.transpose(1, 0, 2).reshape(heads * chunks * LANES // width, width)
    small = jnp.concatenate(
        [
            gcol[:, :width],
            gcol[:, 2 * width :],
            gvec[:2],
            gvec_one[:2],
            gvec[2:6],
            grad_bias.reshape(-1, width),
            grad_table,
        ]
    )
    return block_out, input_grad, grad_attn, grad_up, grad_down, small


def shards(
    block_in,
    out_grad,
    mim_mask,
    rel_index,
    qkv_weight,
    proj_weight,
    up_weight,
    down_weight,
    vectors,
    up_bias,
    rel_table,
    qkv_master,
    qkv_mean,
    qkv_square,
    proj_master,
    proj_mean,
    proj_square,
    up_master,
    up_mean,
    up_square,
    down_master,
    down_mean,
    down_square,
    vector_mean,
    vector_square,
    bias_mean,
    bias_square,
    table_mean,
    table_square,
):
    width = block_in.shape[2]
    table_rows, heads = rel_table.shape
    wide = lax.axis_size("wide")
    narrow = lax.axis_size("narrow")
    up_all = lax.all_gather(up_weight, "narrow", axis=0)
    down_all = lax.all_gather(down_weight, "narrow", axis=0)
    block_out, input_grad, grad_attn, grad_up, grad_down, small = local_work(
        block_in, out_grad, mim_mask, rel_index, qkv_weight, proj_weight, up_all, down_all, vectors, up_bias, rel_table
    )
    small = summed(small)
    lead = [n for n in range(narrow.bit_length() - 1)]
    trail = [len(lead) + n for n in range(wide.bit_length() - 1)]
    order_a = lead[::-1] + trail[::-1]
    order_b = lead[-1:] + trail[::-1] + lead[:-1]
    cut = lambda v: v.reshape(narrow, wide, width // wide, v.shape[-1])
    up_shard = scattered_sum(cut(grad_up), order_a)
    down_shard = scattered_sum(cut(grad_down), order_b)
    grad_attn = cut(grad_attn)
    half = grad_attn.shape[2] // 2
    attn_shard = jnp.concatenate(
        [scattered_sum(grad_attn[:, :, :half], order_a), scattered_sum(grad_attn[:, :, half:], order_b)]
    )
    split = qkv_master.shape[1]
    qkv_shard, proj_shard = attn_shard[:, :split], attn_shard[:, split:]
    shard_squares = jnp.sum(attn_shard * attn_shard) + jnp.sum(up_shard * up_shard) + jnp.sum(down_shard * down_shard)
    large_squares = summed(jnp.full((1, LANES), shard_squares))[0, 0]
    small_squares = jnp.sum(small * small)
    grad_vectors = small[:10]
    grad_bias = small[10 : 10 + up_bias.shape[0] // width].reshape(up_bias.shape)
    grad_table = small[10 + up_bias.shape[0] // width :].reshape(heads, -1).T[:table_rows]
    grad_norm = jnp.sqrt(large_squares + small_squares)
    clip = jnp.minimum(1.0, max_norm / (grad_norm + clip_eps))
    results = [block_out, input_grad, grad_norm]
    for master, mean, square, grad in (
        (qkv_master, qkv_mean, qkv_square, qkv_shard),
        (proj_master, proj_mean, proj_square, proj_shard),
        (up_master, up_mean, up_square, up_shard),
        (down_master, down_mean, down_square, down_shard),
    ):
        mean_new, square_new, master_new = adam_update(
            master, mean, square, clip * grad, rate_matrix, weight_decay
        )
        results += [mean_new, square_new, master_new, master_new.astype(jnp.bfloat16)]
    for master, mean, square, grad in (
        (vectors, vector_mean, vector_square, grad_vectors),
        (up_bias, bias_mean, bias_square, grad_bias),
        (rel_table, table_mean, table_square, grad_table),
    ):
        mean_new, square_new, master_new = adam_update(
            master, mean, square, clip * grad, rate_small, 0.0
        )
        results += [mean_new, square_new, master_new]
    return tuple(results)


def solution(mesh):
    token = P(("wide", "narrow"), None, None)
    whole_spec = P()
    shard = P("wide", "narrow")
    in_specs = (
        (token, token, P(("wide", "narrow"), None))
        + (whole_spec,) * 3
        + (P(None, "narrow"),) * 2
        + (whole_spec,) * 3
        + (shard,) * 12
        + (whole_spec,) * 6
    )
    out_specs = (token, token, whole_spec) + (shard,) * 16 + (whole_spec,) * 9
    return jax.shard_map(shards, mesh=mesh, in_specs=in_specs, out_specs=out_specs, check_vma=False)
```

```python
import functools

import jax
import jax.numpy as jnp
from jax import lax
from jax.experimental import pallas as pl
from jax.experimental.pallas import tpu as pltpu
from jax.sharding import PartitionSpec as P

VALID = 197
STEP = 10
LANES = 128

norm_eps = 1e-06
clip_eps = 1e-06
max_norm = 1.0
beta_one = 0.9
beta_two = 0.999
adam_eps = 1e-08
rate_matrix = 0.05
rate_small = 0.4
weight_decay = 0.05
BF = jnp.bfloat16
F32 = jnp.float32
ROWS_ROWS = (((0,), (0,)), ((), ()))
COLS_COLS = (((1,), (1,)), ((), ()))
VMEM_LIMIT = 60000 * 1024
UNROLL_F = 3
UNROLL_B = 3
UNROLL_T = 8


def mm(a, b):
    return jnp.dot(a, b, preferred_element_type=F32)


def mm_nt(a, b):
    return lax.dot_general(a, b, COLS_COLS, preferred_element_type=F32)


def mm_tn(a, b):
    return lax.dot_general(a, b, ROWS_ROWS, preferred_element_type=F32)


def params(steps=1):
    return pltpu.CompilerParams(
        dimension_semantics=("arbitrary",) * steps, vmem_limit_bytes=VMEM_LIMIT
    )


def whole(shape):
    zeros = (0,) * len(shape)
    return pl.BlockSpec(shape, lambda i: zeros)


def fixed(shape):
    zeros = (0,) * len(shape)
    return pl.BlockSpec(shape, lambda i: zeros, pipeline_mode=pl.Buffered(1))


def per_step(shape):
    rest = (0,) * (len(shape) - 1)
    return pl.BlockSpec((1,) + tuple(shape[1:]), lambda i: (i,) + rest)


def normalized(values):
    center = values - jnp.mean(values, -1, keepdims=True)
    factor = lax.rsqrt(jnp.mean(center * center, -1, keepdims=True) + norm_eps)
    return center * factor, factor


def layer_back(grad, normed, factor, gain_vec):
    scaled = grad * gain_vec
    return factor * (
        scaled
        - jnp.mean(scaled, -1, keepdims=True)
        - normed * jnp.mean(scaled * normed, -1, keepdims=True)
    )


def head_masks(pair_width, head_dim):
    lane = lax.broadcasted_iota(jnp.int32, (1, pair_width), 1)
    return [
        ((lane >= e * head_dim) & (lane < (e + 1) * head_dim)) for e in range(pair_width // head_dim)
    ]


def bias_kernel(idx_ref, tab_ref, out_ref, back_ref, work_ref):
    heads, seq = out_ref.shape[0], out_ref.shape[1]
    chunks = tab_ref.shape[1]

    def rows(step, carry):
        at = pl.multiple_of(step * 8, 8)
        for half in range(idx_ref.shape[1] // LANES):
            cols = slice(half * LANES, (half + 1) * LANES)
            index = idx_ref[pl.ds(at, 8), cols]
            low, high = index & (LANES - 1), index >> 7
            match = [high == c for c in range(chunks)]
            for h in range(heads):
                found = jnp.full((8, LANES), -1e30, F32)
                for c in range(chunks):
                    row = jnp.broadcast_to(tab_ref[h, c : c + 1, :], (8, LANES))
                    taken = jnp.take_along_axis(row, low, axis=1, mode="promise_in_bounds")
                    found = jnp.where(match[c], taken, found)
                work_ref[h, pl.ds(at, 8), cols] = found
        return carry

    lax.fori_loop(0, seq // 8, rows, 0)

    def turn(h, carry):
        out_ref[h] = work_ref[h, :seq, :seq]
        back_ref[h] = work_ref[h].T[:seq, :seq]
        return carry

    lax.fori_loop(0, heads, turn, 0)


def bias_tables(index, table_rows):
    seq, padded = index.shape
    heads, chunks, _ = table_rows.shape
    shape = (heads, seq, seq)
    return pl.pallas_call(
        bias_kernel,
        grid=(1,),
        in_specs=[whole(index.shape), whole(table_rows.shape)],
        out_specs=[whole(shape)] * 2,
        out_shape=[jax.ShapeDtypeStruct(shape, F32)] * 2,
        scratch_shapes=[pltpu.VMEM((heads, padded, padded), F32)],
        compiler_params=params(),
        name="bias_tables",
    )(index, table_rows)


def table_kernel(idx_ref, ds_ref, out_ref):
    seq, heads, _ = ds_ref.shape
    chunks = out_ref.shape[0] // (2 * heads)
    out_ref[...] = jnp.zeros_like(out_ref)
    kinds = lax.broadcasted_iota(jnp.int32, (LANES, seq), 0)

    def one_key(j, total):
        index = idx_ref[pl.ds(j, 1), :]
        low, high = index & (LANES - 1), index >> 7
        onehot = jnp.where(jnp.broadcast_to(low, (LANES, seq)) == kinds, 1.0, 0.0).astype(BF)
        grads = ds_ref[j]
        top = grads.astype(BF).astype(F32)
        both = jnp.concatenate([top, grads - top], 0)
        high_all = jnp.broadcast_to(high, both.shape)
        parts = jnp.concatenate([jnp.where(high_all == c, both, 0.0) for c in range(chunks)], 0)
        return total + mm_nt(parts.astype(BF), onehot)

    out_ref[...] = lax.fori_loop(0, seq, one_key, jnp.zeros(out_ref.shape, F32), unroll=UNROLL_T)


def table_sums(index_t, grads, chunks):
    seq, heads, _ = grads.shape
    out = (chunks * 2 * heads, LANES)
    return pl.pallas_call(
        table_kernel,
        grid=(1,),
        in_specs=[whole(index_t.shape), whole(grads.shape)],
        out_specs=whole(out),
        out_shape=jax.ShapeDtypeStruct(out, F32),
        compiler_params=params(),
        name="table_sums",
    )(index_t, grads)


def front_kernel(heads, x_ref, wqkv_ref, wproj_ref, vec_ref, bias_ref, a_ref, qkv_ref, o_ref, attn_ref, hn_ref):
    width = x_ref.shape[2]
    head_dim = width // heads
    scale = head_dim ** (-0.5)
    x = x_ref[0].astype(F32)
    normed, _ = normalized(x)
    first = (normed * vec_ref[4:5, :] + vec_ref[5:6, :]).astype(BF)
    a_ref[0] = first
    for part, row in ((0, 0), (1, None), (2, 1)):
        cols = slice(part * width, (part + 1) * width)
        value = mm(first, wqkv_ref[:, cols])
        if row is not None:
            value = value + vec_ref[row : row + 1, :]
        qkv_ref[0, :, cols] = value.astype(BF)
    pair = LANES
    masks = head_masks(pair, head_dim)
    per = pair // head_dim

    def one_pair(g, carry):
        at = pl.multiple_of(g * pair, pair)
        q = qkv_ref[0, :, pl.ds(at, pair)]
        k = qkv_ref[0, :, pl.ds(at + width, pair)]
        v = qkv_ref[0, :, pl.ds(at + 2 * width, pair)]
        out = None
        for e in range(per):
            qm = q * jnp.where(masks[e], scale, 0.0).astype(BF)
            s = mm_nt(qm, k) + bias_ref[g * per + e]
            p = jnp.exp(s - jnp.max(s, -1, keepdims=True))
            p = p * (1.0 / jnp.sum(p, -1, keepdims=True))
            mixed = mm(p.astype(BF), v)
            out = mixed if out is None else jnp.where(masks[e], mixed, out)
        o_ref[0, :, pl.ds(at, pair)] = out.astype(BF)
        return carry

    lax.fori_loop(0, width // pair, one_pair, 0, unroll=UNROLL_F)
    attn = mm(o_ref[0], wproj_ref[...]) + vec_ref[2:3, :]
    attn_ref[0] = attn
    middle, _ = normalized(x + vec_ref[8:9, :] * attn)
    hn_ref[0] = (middle * vec_ref[6:7, :] + vec_ref[7:8, :]).astype(BF)


def front(x, qkv_weight, proj_weight, vectors, bias, heads):
    images, seq, width = x.shape
    shapes = [
        jax.ShapeDtypeStruct((images, seq, width), BF),
        jax.ShapeDtypeStruct((images, seq, 3 * width), BF),
        jax.ShapeDtypeStruct((images, seq, width), BF),
        jax.ShapeDtypeStruct((images, seq, width), F32),
        jax.ShapeDtypeStruct((images, seq, width), BF),
    ]
    return pl.pallas_call(
        functools.partial(front_kernel, heads),
        grid=(images,),
        in_specs=[
            per_step(x.shape),
            fixed(qkv_weight.shape),
            fixed(proj_weight.shape),
            fixed(vectors.shape),
            fixed(bias.shape),
        ],
        out_specs=[per_step(s.shape) for s in shapes],
        out_shape=shapes,
        compiler_params=params(),
        name="front",
    )(x, qkv_weight, proj_weight, vectors, bias)


def mlp_in_kernel(chunk, hn_ref, gy_ref, vec_ref, bup_ref, wup_ref, z_ref, slope_ref, gdn_ref, dm_ref, turned_ref):
    tokens = hn_ref.shape[0]

    @pl.when(pl.program_id(0) == 0)
    def _():
        def rows(step, carry):
            at = pl.ds(pl.multiple_of(step * chunk, chunk), chunk)
            dm_ref[at, :] = (vec_ref[9:10, :] * gy_ref[at, :].astype(F32)).astype(BF)
            return carry

        lax.fori_loop(0, tokens // chunk, rows, 0)
        turned_ref[...] = dm_ref[...].T

    def rows(step, carry):
        at = pl.ds(pl.multiple_of(step * chunk, chunk), chunk)
        u = mm(hn_ref[at, :], wup_ref[0]) + bup_ref[0]
        gate = 0.5 * (1.0 + lax.erf(u * 0.7071067811865476))
        z_ref[0, at, :] = (u * gate).astype(BF)
        slope_ref[0, at, :] = (gate + u * jnp.exp(-0.5 * u * u) * 0.3989422804014327).astype(BF)
        return carry

    lax.fori_loop(0, tokens // chunk, rows, 0)
    gdn_ref[0] = mm(turned_ref[...], z_ref[0]).astype(BF)


def mlp_in(hn, gy, vectors, up_bias, up_all, chunk):
    tokens, width = hn.shape
    blocks, _, hidden = up_all.shape
    shapes = [
        jax.ShapeDtypeStruct((blocks, tokens, hidden), BF),
        jax.ShapeDtypeStruct((blocks, tokens, hidden), BF),
        jax.ShapeDtypeStruct((blocks, width, hidden), BF),
    ]
    return pl.pallas_call(
        functools.partial(mlp_in_kernel, chunk),
        grid=(blocks,),
        in_specs=[
            fixed(hn.shape),
            fixed(gy.shape),
            fixed(vectors.shape),
            per_step(up_bias.shape),
            per_step(up_all.shape),
        ],
        out_specs=[per_step(s.shape) for s in shapes] + [fixed((tokens, width))],
        out_shape=shapes + [jax.ShapeDtypeStruct((tokens, width), BF)],
        scratch_shapes=[pltpu.VMEM((width, tokens), BF)],
        compiler_params=params(),
        name="mlp_in",
    )(hn, gy, vectors, up_bias, up_all)


def mlp_out_kernel(chunk, hn_ref, dm_ref, z_ref, slope_ref, wup_ref, wdn_ref, m_ref, dhn_ref, gup_ref, gb_ref, du_ref, turned_ref):
    tokens = hn_ref.shape[0]

    @pl.when(pl.program_id(0) == 0)
    def _():
        m_ref[...] = jnp.zeros_like(m_ref)
        dhn_ref[...] = jnp.zeros_like(dhn_ref)
        turned_ref[...] = hn_ref[...].T

    gb_ref[...] = jnp.zeros_like(gb_ref)

    def rows(step, carry):
        at = pl.ds(pl.multiple_of(step * chunk, chunk), chunk)
        m_ref[at, :] += mm_nt(z_ref[0, at, :], wdn_ref[0])
        du = (mm(dm_ref[at, :], wdn_ref[0]) * slope_ref[0, at, :].astype(F32)).astype(BF)
        du_ref[at, :] = du
        gb_ref[0] += jnp.sum(du.astype(F32), 0, keepdims=True)
        dhn_ref[at, :] += mm_nt(du, wup_ref[0])
        return carry

    lax.fori_loop(0, tokens // chunk, rows, 0)
    gup_ref[0] = mm(turned_ref[...], du_ref[...]).astype(BF)


def mlp_out(hn, dm, z, slope, up_all, down_all, chunk):
    tokens, width = hn.shape
    blocks, _, hidden = up_all.shape
    shapes = [
        jax.ShapeDtypeStruct((tokens, width), F32),
        jax.ShapeDtypeStruct((tokens, width), F32),
        jax.ShapeDtypeStruct((blocks, width, hidden), BF),
        jax.ShapeDtypeStruct((blocks, 1, hidden), F32),
    ]
    return pl.pallas_call(
        functools.partial(mlp_out_kernel, chunk),
        grid=(blocks,),
        in_specs=[fixed(hn.shape), fixed(dm.shape)] + [per_step(v.shape) for v in (z, slope, up_all, down_all)],
        out_specs=[fixed(s.shape) for s in shapes[:2]] + [per_step(s.shape) for s in shapes[2:]],
        out_shape=shapes,
        scratch_shapes=[pltpu.VMEM((tokens, hidden), BF), pltpu.VMEM((width, tokens), BF)],
        compiler_params=params(),
        name="mlp_out",
    )(hn, dm, z, slope, up_all, down_all)


def middle_kernel(
    x_ref, gy_ref, attn_ref, m_ref, dhn_ref, wproj_ref, vec_ref, out_ref, dmid_ref, dat_ref, do_ref, gvec_ref
):
    @pl.when(pl.program_id(0) == 0)
    def _():
        gvec_ref[...] = jnp.zeros_like(gvec_ref)

    attn = attn_ref[0]
    middle = x_ref[0].astype(F32) + vec_ref[8:9, :] * attn
    branch = m_ref[0] + vec_ref[3:4, :]
    out_ref[0] = (middle + vec_ref[9:10, :] * branch).astype(BF)
    cotangent = gy_ref[0].astype(F32)
    normed, factor = normalized(middle)
    dhn = dhn_ref[0]
    dmid = cotangent + layer_back(dhn, normed, factor, vec_ref[6:7, :])
    dmid_ref[0] = dmid
    dat = (vec_ref[8:9, :] * dmid).astype(BF)
    dat_ref[0] = dat
    down_in = (vec_ref[9:10, :] * cotangent).astype(BF)
    for row, value in enumerate(
        (dat.astype(F32), down_in.astype(F32), dhn * normed, dhn, dmid * attn, cotangent * branch)
    ):
        gvec_ref[row : row + 1, :] += jnp.sum(value, 0, keepdims=True)
    do_ref[0] = mm_nt(dat, wproj_ref[...]).astype(BF)


def middle_back(x, gy, attn, m, dhn, proj_weight, vectors):
    images, seq, width = x.shape
    shapes = [
        jax.ShapeDtypeStruct((images, seq, width), BF),
        jax.ShapeDtypeStruct((images, seq, width), F32),
        jax.ShapeDtypeStruct((images, seq, width), BF),
        jax.ShapeDtypeStruct((images, seq, width), BF),
        jax.ShapeDtypeStruct((8, width), F32),
    ]
    return pl.pallas_call(
        middle_kernel,
        grid=(images,),
        in_specs=[per_step(v.shape) for v in (x, gy, attn, m, dhn)] + [fixed(proj_weight.shape), fixed(vectors.shape)],
        out_specs=[per_step(s.shape) for s in shapes[:4]] + [fixed(shapes[4].shape)],
        out_shape=shapes,
        compiler_params=params(),
        name="middle_back",
    )(x, gy, attn, m, dhn, proj_weight, vectors)


def back_kernel(heads, qkv_ref, do_ref, bias_ref, dqkv_ref, ds_ref, gcol_ref):
    width = do_ref.shape[2]
    head_dim = width // heads
    scale = head_dim ** (-0.5)

    @pl.when(pl.program_id(0) == 0)
    def _():
        ds_ref[...] = jnp.zeros_like(ds_ref)
        gcol_ref[...] = jnp.zeros_like(gcol_ref)

    pair = LANES
    masks = head_masks(pair, head_dim)
    per = pair // head_dim

    def one_pair(g, carry):
        at = pl.multiple_of(g * pair, pair)
        q = qkv_ref[0, :, pl.ds(at, pair)]
        k = qkv_ref[0, :, pl.ds(at + width, pair)]
        v = qkv_ref[0, :, pl.ds(at + 2 * width, pair)]
        do = do_ref[0, :, pl.ds(at, pair)]
        dq = dk = dv = None
        for e in range(per):
            pick = jnp.where(masks[e], scale, 0.0).astype(BF)
            keep = jnp.where(masks[e], 1.0, 0.0).astype(BF)
            qm, km, dom = q * pick, k * pick, do * keep
            s = mm_nt(k, qm) + bias_ref[g * per + e]
            p = jnp.exp(s - jnp.max(s, 0, keepdims=True))
            p = p * (1.0 / jnp.sum(p, 0, keepdims=True))
            dv_e = mm(p.astype(BF), dom)
            dp = mm_nt(v, dom)
            ds = (p * (dp - jnp.sum(dp * p, 0, keepdims=True))).astype(BF)
            ds_ref[g * per + e] += ds.astype(F32)
            dk_e = mm(ds, qm)
            dq_e = mm_tn(ds, km)
            dq = dq_e if dq is None else dq + dq_e
            dk = dk_e if dk is None else dk + dk_e
            dv = dv_e if dv is None else dv + dv_e
        for part, value in ((0, dq), (1, dk), (2, dv)):
            rounded = value.astype(BF)
            dqkv_ref[0, :, pl.ds(at + part * width, pair)] = rounded
            gcol_ref[:, pl.ds(at + part * width, pair)] += jnp.sum(rounded.astype(F32), 0, keepdims=True)
        return carry

    lax.fori_loop(0, width // pair, one_pair, 0, unroll=UNROLL_B)


def back(qkv, do, bias, heads):
    images, seq, width = do.shape
    shapes = [
        jax.ShapeDtypeStruct((images, seq, 3 * width), BF),
        jax.ShapeDtypeStruct((heads, seq, seq), F32),
        jax.ShapeDtypeStruct((1, 3 * width), F32),
    ]
    return pl.pallas_call(
        functools.partial(back_kernel, heads),
        grid=(images,),
        in_specs=[per_step(qkv.shape), per_step(do.shape), fixed(bias.shape)],
        out_specs=[per_step(shapes[0].shape)] + [fixed(s.shape) for s in shapes[1:]],
        out_shape=shapes,
        compiler_params=params(),
        name="back",
    )(qkv, do, bias)


def grads_kernel(blocks, a_ref, dqkv_ref, o_ref, dat_ref, out_ref, turned_a, turned_o):
    wide_cols, thin_cols = dqkv_ref.shape[1] // blocks, dat_ref.shape[1] // blocks
    turned_a[...] = a_ref[...].T
    turned_o[...] = o_ref[...].T
    for n in range(blocks):
        out_ref[n, :, :wide_cols] = mm(
            turned_a[...], dqkv_ref[:, n * wide_cols : (n + 1) * wide_cols]
        ).astype(BF)
        out_ref[n, :, wide_cols:] = mm(
            turned_o[...], dat_ref[:, n * thin_cols : (n + 1) * thin_cols]
        ).astype(BF)


def attention_grads(first, dqkv, mixed, dat, blocks):
    width = first.shape[1]
    cols = (dqkv.shape[1] + dat.shape[1]) // blocks
    return pl.pallas_call(
        functools.partial(grads_kernel, blocks),
        grid=(1,),
        in_specs=[whole(v.shape) for v in (first, dqkv, mixed, dat)],
        out_specs=whole((blocks, width, cols)),
        out_shape=jax.ShapeDtypeStruct((blocks, width, cols), BF),
        scratch_shapes=[pltpu.VMEM((width, first.shape[0]), BF)] * 2,
        compiler_params=params(),
        name="attention_grads",
    )(first, dqkv, mixed, dat)


def input_kernel(x_ref, dqkv_ref, dmid_ref, wqkv_ref, vec_ref, out_ref, gvec_ref):
    @pl.when(pl.program_id(0) == 0)
    def _():
        gvec_ref[...] = jnp.zeros_like(gvec_ref)

    da = mm_nt(dqkv_ref[0], wqkv_ref[...])
    normed, factor = normalized(x_ref[0].astype(F32))
    gvec_ref[0:1, :] += jnp.sum(da * normed, 0, keepdims=True)
    gvec_ref[1:2, :] += jnp.sum(da, 0, keepdims=True)
    out_ref[0] = dmid_ref[0] + layer_back(da, normed, factor, vec_ref[4:5, :])


def input_grads(x, dqkv, dmid, qkv_weight, vectors):
    images, seq, width = x.shape
    shapes = [
        jax.ShapeDtypeStruct((images, seq, width), F32),
        jax.ShapeDtypeStruct((8, width), F32),
    ]
    return pl.pallas_call(
        input_kernel,
        grid=(images,),
        in_specs=[per_step(v.shape) for v in (x, dqkv, dmid)]
        + [fixed(qkv_weight.shape), fixed(vectors.shape)],
        out_specs=[per_step(shapes[0].shape), fixed(shapes[1].shape)],
        out_shape=shapes,
        compiler_params=params(),
        name="input_grads",
    )(x, dqkv, dmid, qkv_weight, vectors)


def adam_update(master, mean, square, grad, rate, decay):
    mean_new = beta_one * mean + (1.0 - beta_one) * grad
    square_new = beta_two * square + (1.0 - beta_two) * grad * grad
    fix_one = 1.0 - beta_one**STEP
    fix_two = 1.0 - beta_two**STEP
    direction = mean_new / fix_one / (jnp.sqrt(square_new / fix_two) + adam_eps)
    return (mean_new, square_new, master - rate * (direction + decay * master))


def adam_kernel(rows, ours_ref, theirs_ref, attn_ref, up_ref, down_ref, *refs):
    state, results = refs[:21], refs[21:]
    sums = ours_ref[...] + theirs_ref[...]
    heads, vec_at, bias_at, square_at = rows
    row = lax.broadcasted_iota(jnp.int32, sums.shape, 0)
    small = jnp.where(row < square_at, sums, 0.0)
    total = jnp.sum(jnp.sum(small * small, 0, keepdims=True), 1, keepdims=True) + sums[square_at : square_at + 1, :1]
    norm = jnp.sqrt(total)
    results[0][...] = norm
    clip = jnp.minimum(1.0, max_norm / (norm + clip_eps))
    split = state[0].shape[1]
    vec_rows, table_rows = state[12].shape[0], state[18].shape[1]
    bias = jnp.concatenate([sums[r : r + 1] for r in range(bias_at, square_at)], 1)
    grads = (
        attn_ref[:, :split],
        attn_ref[:, split:],
        up_ref[...],
        down_ref[...].astype(F32),
        sums[vec_at : vec_at + vec_rows],
        bias,
        sums[:heads, :table_rows],
    )
    at = 1
    for n, grad in enumerate(grads):
        large = n < 4
        mean_new, square_new, master_new = adam_update(
            *(state[3 * n + k][...] for k in range(3)),
            clip * grad,
            rate_matrix if large else rate_small,
            weight_decay if large else 0.0,
        )
        values = [mean_new, square_new, master_new]
        if large:
            values.append(master_new.astype(BF))
        for value in values:
            results[at][...] = value
            at += 1


def adam(rows, ours, theirs, shards, state):
    shapes = [jax.ShapeDtypeStruct((1, 1), F32)]
    for n in range(7):
        shapes += [jax.ShapeDtypeStruct(state[3 * n].shape, F32)] * 3
        if n < 4:
            shapes.append(jax.ShapeDtypeStruct(state[3 * n].shape, BF))
    inputs = [ours, theirs, *shards, *state]
    return pl.pallas_call(
        functools.partial(adam_kernel, rows),
        grid=(1,),
        in_specs=[whole(v.shape) for v in inputs],
        out_specs=[whole(v.shape) for v in shapes],
        out_shape=shapes,
        compiler_params=params(),
        name="adam",
    )(*inputs)


def axis_bits():
    found = []
    for axis in ("narrow", "wide"):
        count = lax.axis_size(axis).bit_length() - 1
        found += [(axis, count - 1 - at) for at in range(count)]
    return found


def swap(value, axis, bit):
    size = lax.axis_size(axis)
    return lax.ppermute(value, axis, [(i, i ^ (1 << bit)) for i in range(size)])


class Halving:
    def __init__(self, grads, steps):
        self.bits = axis_bits()
        self.shape = grads.shape[2:]
        self.parts = [[grads.reshape((2,) * len(self.bits) + self.shape)]]
        self.steps = list(steps)

    def send(self, *after):
        dims = self.steps.pop(0)
        last = [pieces[-1] for pieces in self.parts]
        if after:
            last = lax.optimization_barrier((*last, *after))
        self.parts = [[*pieces[:-1], piece] for pieces, piece in zip(self.parts, last)]
        if len(dims) > len(self.parts):
            middle = self.shape[0] // 2
            self.parts = [[p[..., :middle, :] for p in self.parts[0]], [p[..., middle:, :] for p in self.parts[0]]]
        sent = []
        for n, pieces in enumerate(self.parts):
            dim = dims[n % len(dims)]
            axis, bit = self.bits[dim]
            mine = (lax.axis_index(axis) >> bit) & 1

            def half(piece, side):
                return lax.dynamic_slice_in_dim(piece, side, 1, dim)

            sent.append(sum(half(p, 1 - mine).astype(F32) for p in pieces).astype(BF))
            self.parts[n] = [half(p, mine) for p in pieces]
        if len(dims) < len(sent):
            sent = [jnp.concatenate(sent, -2)]
        arrived = [swap(v, *self.bits[dim]) for v, dim in zip(sent, dims)]
        if len(arrived) < len(self.parts):
            arrived = jnp.split(arrived[0], 2, -2)
        for pieces, piece in zip(self.parts, arrived):
            pieces.append(piece)
        return tuple(sent)

    def result(self):
        while self.steps:
            self.send()
        sums = [sum(p.astype(F32) for p in pieces).reshape(-1, self.shape[1]) for pieces in self.parts]
        return jnp.concatenate(sums)


def gated(value, *waits):
    return lax.optimization_barrier((value,) + waits)[0] if waits else value


class Plan:
    def __init__(self, wide, narrow):
        self.wide, self.narrow = wide, narrow
        lead = list(range(narrow.bit_length() - 1))
        trail = [len(lead) + n for n in range(wide.bit_length() - 1)][::-1]
        pair = (lead[0], trail[0])
        self.steps = [(d,) for d in lead[:0:-1]] + [pair, pair[::-1]] + [(d,) for d in trail[1:]]

    def halving(self, grads):
        return Halving(grads.reshape(self.narrow, self.wide, grads.shape[1] // self.wide, grads.shape[2]), self.steps)

    def after_down(self, grads):
        rows = grads.reshape(-1, grads.shape[2])
        self.down = lax.psum_scatter(rows, ("narrow", "wide"), scatter_dimension=0, tiled=True)
        return ()

    def after_up(self, grads):
        self.up = self.halving(grads)
        return self.up.send()

    def next_up(self, *after):
        return self.up.send(*after)

    def after_attention(self, grads):
        self.attn = self.halving(grads)
        return self.attn.send()

    def next_all(self, *after):
        return self.up.send(*after) + self.attn.send(*after)


class Alone:
    def after_down(self, grads):
        self.down = grads
        return ()

    def after_up(self, grads):
        self.up = grads
        return ()

    def after_attention(self, grads):
        self.attn = grads
        return ()

    def next_up(self, *after):
        return ()

    next_all = next_up


def local_work(
    block_in, out_grad, mim_mask, rel_index, qkv_weight, proj_weight, up_all, down_all, vectors, up_bias, rel_table, plan=None
):
    plan = plan or Alone()
    images, seq, width = block_in.shape
    table_rows, heads = rel_table.shape
    blocks, _, hidden = up_all.shape
    tokens = images * seq
    chunks = -(-table_rows // LANES)
    padded_seq = -(-seq // LANES) * LANES
    key_at = jnp.arange(seq, dtype=jnp.int32)
    index = jnp.where(key_at[None, :] < VALID, rel_index, chunks * LANES)
    index_t = index.T
    padded = jnp.pad(index, ((0, 0), (0, padded_seq - seq)))
    table_t = jnp.pad(rel_table, ((0, chunks * LANES - table_rows), (0, 0))).T.reshape(heads, chunks, LANES)
    bias, bias_t = bias_tables(padded, table_t)
    gy = out_grad * mim_mask.astype(BF)[:, :, None]
    first, qkv, mixed, attn, hn = front(block_in, qkv_weight, proj_weight, vectors, bias, heads)
    flat = lambda v: v.reshape(tokens, v.shape[-1])
    z, slope, grad_down, dm = mlp_in(flat(hn), flat(gy), vectors, up_bias.reshape(blocks, 1, hidden), up_all, seq)
    dm = gated(dm, *plan.after_down(grad_down))
    m, dhn, grad_up, grad_bias = mlp_out(flat(hn), dm, z, slope, up_all, down_all, seq)
    gy = gated(gy, *plan.after_up(grad_up))
    fold = lambda v: v.reshape(images, seq, width)
    block_out, dmid, dat, do, gvec = middle_back(block_in, gy, attn, fold(m), fold(dhn), proj_weight, vectors)
    do = gated(do, *plan.next_up(do))
    dqkv, ds, gcol = back(qkv, do, bias_t, heads)
    dat = gated(dat, *plan.next_up(dqkv))
    grad_attn = attention_grads(flat(first), flat(dqkv), flat(mixed), flat(dat), blocks)
    dmid = gated(dmid, *plan.after_attention(grad_attn))
    input_grad, gvec_one = input_grads(block_in, dqkv, dmid, qkv_weight, vectors)
    by_key = jnp.pad(ds.transpose(1, 0, 2), ((0, 0), (0, (-heads) % 8), (0, 0)))
    by_key = gated(by_key, *plan.next_all(input_grad))
    sums = table_sums(index_t, by_key, chunks)
    plan.next_all(sums)
    sums = sums.reshape(chunks, 2, -1, LANES).sum(1)
    grad_table = sums.transpose(1, 0, 2).reshape(-1, chunks * LANES)
    small = jnp.concatenate(
        [
            grad_table,
            gcol[:, :width],
            gcol[:, 2 * width :],
            gvec[:2],
            gvec_one[:2],
            gvec[2:6],
            grad_bias.reshape(-1, width),
        ]
    )
    return block_out, input_grad, small, plan


def shards(
    block_in,
    out_grad,
    mim_mask,
    rel_index,
    qkv_weight,
    proj_weight,
    up_weight,
    down_weight,
    vectors,
    up_bias,
    rel_table,
    *state,
):
    width = block_in.shape[2]
    heads = rel_table.shape[1]
    up_all = lax.all_gather(up_weight, "narrow", axis=0)
    down_all = lax.all_gather(down_weight, "narrow", axis=0)
    plan = Plan(lax.axis_size("wide"), lax.axis_size("narrow"))
    block_out, input_grad, small, plan = local_work(
        block_in, out_grad, mim_mask, rel_index, qkv_weight, proj_weight, up_all, down_all, vectors, up_bias, rel_table, plan
    )
    up_shard = plan.up.result()
    down_shard = plan.down
    attn_shard = plan.attn.result()
    squares = sum(jnp.sum(jnp.square(v.astype(F32))) for v in (down_shard, up_shard, attn_shard))
    bias_rows = up_bias.shape[0] // width
    vec_at = heads + (-heads) % 8
    bias_at = vec_at + vectors.shape[0]
    square_at = bias_at + bias_rows
    ours = jnp.concatenate([small, jnp.full((1, width), squares)])
    theirs = None
    for axis, bit in reversed(axis_bits()):
        ours = ours if theirs is None else ours + theirs
        theirs = swap(ours, axis, bit)
    line = lambda v: v.reshape(1, -1)
    matrices = state[:12]
    params_small = (vectors, state[12], state[13], line(up_bias), line(state[14]), line(state[15]), rel_table.T, *(v.T for v in state[16:]))
    norm, *updated = adam(
        (heads, vec_at, bias_at, square_at),
        ours,
        theirs,
        (attn_shard, up_shard, down_shard),
        [matrices[3 * n + k] for n in range(4) for k in range(3)] + [params_small[3 * n + k] for n in range(3) for k in range(3)],
    )
    for n in range(19, 22):
        updated[n] = updated[n].reshape(up_bias.shape)
        updated[n + 3] = updated[n + 3].T
    return (block_out, input_grad, norm.reshape(()), *updated)


def solution(mesh):
    token = P(("wide", "narrow"), None, None)
    whole_spec = P()
    shard = P("wide", "narrow")
    in_specs = (
        (token, token, P(("wide", "narrow"), None))
        + (whole_spec,) * 3
        + (P(None, "narrow"),) * 2
        + (whole_spec,) * 3
        + (shard,) * 12
        + (whole_spec,) * 6
    )
    out_specs = (token, token, whole_spec) + (shard,) * 16 + (whole_spec,) * 9
    return jax.shard_map(shards, mesh=mesh, in_specs=in_specs, out_specs=out_specs, check_vma=False)
```

```python
import functools

import jax
import jax.numpy as jnp
from jax import lax
from jax.experimental import pallas as pl
from jax.experimental.pallas import tpu as pltpu
from jax.sharding import PartitionSpec as P

VALID = 197
STEP = 10
LANES = 128

norm_eps = 1e-06
clip_eps = 1e-06
max_norm = 1.0
beta_one = 0.9
beta_two = 0.999
adam_eps = 1e-08
rate_matrix = 0.05
rate_small = 0.4
weight_decay = 0.05
BF = jnp.bfloat16
F32 = jnp.float32
ROWS_ROWS = (((0,), (0,)), ((), ()))
COLS_COLS = (((1,), (1,)), ((), ()))
VMEM_LIMIT = 60000 * 1024
UNROLL_F = 3
UNROLL_B = 3
UNROLL_T = 8


def mm(a, b):
    return jnp.dot(a, b, preferred_element_type=F32)


def mm_nt(a, b):
    return lax.dot_general(a, b, COLS_COLS, preferred_element_type=F32)


def mm_tn(a, b):
    return lax.dot_general(a, b, ROWS_ROWS, preferred_element_type=F32)


def params(steps=1):
    return pltpu.CompilerParams(
        dimension_semantics=("arbitrary",) * steps, vmem_limit_bytes=VMEM_LIMIT
    )


def whole(shape):
    zeros = (0,) * len(shape)
    return pl.BlockSpec(shape, lambda i: zeros)


def fixed(shape):
    zeros = (0,) * len(shape)
    return pl.BlockSpec(shape, lambda i: zeros, pipeline_mode=pl.Buffered(1))


def per_step(shape):
    rest = (0,) * (len(shape) - 1)
    return pl.BlockSpec((1,) + tuple(shape[1:]), lambda i: (i,) + rest)


def normalized(values):
    center = values - jnp.mean(values, -1, keepdims=True)
    factor = lax.rsqrt(jnp.mean(center * center, -1, keepdims=True) + norm_eps)
    return center * factor, factor


def layer_back(grad, normed, factor, gain_vec):
    scaled = grad * gain_vec
    return factor * (
        scaled
        - jnp.mean(scaled, -1, keepdims=True)
        - normed * jnp.mean(scaled * normed, -1, keepdims=True)
    )


def head_masks(pair_width, head_dim):
    lane = lax.broadcasted_iota(jnp.int32, (1, pair_width), 1)
    return [
        ((lane >= e * head_dim) & (lane < (e + 1) * head_dim)) for e in range(pair_width // head_dim)
    ]


def bias_kernel(idx_ref, tab_ref, out_ref, back_ref, work_ref):
    heads, seq = out_ref.shape[0], out_ref.shape[1]
    chunks = tab_ref.shape[1]

    def rows(step, carry):
        at = pl.multiple_of(step * 8, 8)
        for half in range(idx_ref.shape[1] // LANES):
            cols = slice(half * LANES, (half + 1) * LANES)
            index = idx_ref[pl.ds(at, 8), cols]
            low, high = index & (LANES - 1), index >> 7
            match = [high == c for c in range(chunks)]
            for h in range(heads):
                found = jnp.full((8, LANES), -1e30, F32)
                for c in range(chunks):
                    row = jnp.broadcast_to(tab_ref[h, c : c + 1, :], (8, LANES))
                    taken = jnp.take_along_axis(row, low, axis=1, mode="promise_in_bounds")
                    found = jnp.where(match[c], taken, found)
                work_ref[h, pl.ds(at, 8), cols] = found
        return carry

    lax.fori_loop(0, seq // 8, rows, 0)

    def turn(h, carry):
        out_ref[h] = work_ref[h, :seq, :seq]
        back_ref[h] = work_ref[h].T[:seq, :seq]
        return carry

    lax.fori_loop(0, heads, turn, 0)


def bias_tables(index, table_rows):
    seq, padded = index.shape
    heads, chunks, _ = table_rows.shape
    shape = (heads, seq, seq)
    return pl.pallas_call(
        bias_kernel,
        grid=(1,),
        in_specs=[whole(index.shape), whole(table_rows.shape)],
        out_specs=[whole(shape)] * 2,
        out_shape=[jax.ShapeDtypeStruct(shape, F32)] * 2,
        scratch_shapes=[pltpu.VMEM((heads, padded, padded), F32)],
        compiler_params=params(),
        name="bias_tables",
    )(index, table_rows)


def table_kernel(idx_ref, ds_ref, out_ref):
    seq, heads, _ = ds_ref.shape
    chunks = out_ref.shape[0] // (2 * heads)
    out_ref[...] = jnp.zeros_like(out_ref)
    kinds = lax.broadcasted_iota(jnp.int32, (LANES, seq), 0)

    def one_key(j, total):
        index = idx_ref[pl.ds(j, 1), :]
        low, high = index & (LANES - 1), index >> 7
        onehot = jnp.where(jnp.broadcast_to(low, (LANES, seq)) == kinds, 1.0, 0.0).astype(BF)
        grads = ds_ref[j]
        top = grads.astype(BF).astype(F32)
        both = jnp.concatenate([top, grads - top], 0)
        high_all = jnp.broadcast_to(high, both.shape)
        parts = jnp.concatenate([jnp.where(high_all == c, both, 0.0) for c in range(chunks)], 0)
        return total + mm_nt(parts.astype(BF), onehot)

    out_ref[...] = lax.fori_loop(0, seq, one_key, jnp.zeros(out_ref.shape, F32), unroll=UNROLL_T)


def table_sums(index_t, grads, chunks):
    seq, heads, _ = grads.shape
    out = (chunks * 2 * heads, LANES)
    return pl.pallas_call(
        table_kernel,
        grid=(1,),
        in_specs=[whole(index_t.shape), whole(grads.shape)],
        out_specs=whole(out),
        out_shape=jax.ShapeDtypeStruct(out, F32),
        compiler_params=params(),
        name="table_sums",
    )(index_t, grads)


def front_kernel(heads, x_ref, wqkv_ref, wproj_ref, vec_ref, bias_ref, a_ref, qkv_ref, o_ref, attn_ref, hn_ref):
    width = x_ref.shape[2]
    head_dim = width // heads
    scale = head_dim ** (-0.5)
    x = x_ref[0].astype(F32)
    normed, _ = normalized(x)
    first = (normed * vec_ref[4:5, :] + vec_ref[5:6, :]).astype(BF)
    a_ref[0] = first
    for part, row in ((0, 0), (1, None), (2, 1)):
        cols = slice(part * width, (part + 1) * width)
        value = mm(first, wqkv_ref[:, cols])
        if row is not None:
            value = value + vec_ref[row : row + 1, :]
        qkv_ref[0, :, cols] = value.astype(BF)
    pair = LANES
    masks = head_masks(pair, head_dim)
    per = pair // head_dim

    def one_pair(g, carry):
        at = pl.multiple_of(g * pair, pair)
        q = qkv_ref[0, :, pl.ds(at, pair)]
        k = qkv_ref[0, :, pl.ds(at + width, pair)]
        v = qkv_ref[0, :, pl.ds(at + 2 * width, pair)]
        out = None
        for e in range(per):
            qm = q * jnp.where(masks[e], scale, 0.0).astype(BF)
            s = mm_nt(qm, k) + bias_ref[g * per + e]
            p = jnp.exp(s - jnp.max(s, -1, keepdims=True))
            p = p * (1.0 / jnp.sum(p, -1, keepdims=True))
            mixed = mm(p.astype(BF), v)
            out = mixed if out is None else jnp.where(masks[e], mixed, out)
        o_ref[0, :, pl.ds(at, pair)] = out.astype(BF)
        return carry

    lax.fori_loop(0, width // pair, one_pair, 0, unroll=UNROLL_F)
    attn = mm(o_ref[0], wproj_ref[...]) + vec_ref[2:3, :]
    attn_ref[0] = attn
    middle, _ = normalized(x + vec_ref[8:9, :] * attn)
    hn_ref[0] = (middle * vec_ref[6:7, :] + vec_ref[7:8, :]).astype(BF)


def front(x, qkv_weight, proj_weight, vectors, bias, heads):
    images, seq, width = x.shape
    shapes = [
        jax.ShapeDtypeStruct((images, seq, width), BF),
        jax.ShapeDtypeStruct((images, seq, 3 * width), BF),
        jax.ShapeDtypeStruct((images, seq, width), BF),
        jax.ShapeDtypeStruct((images, seq, width), F32),
        jax.ShapeDtypeStruct((images, seq, width), BF),
    ]
    return pl.pallas_call(
        functools.partial(front_kernel, heads),
        grid=(images,),
        in_specs=[
            per_step(x.shape),
            fixed(qkv_weight.shape),
            fixed(proj_weight.shape),
            fixed(vectors.shape),
            fixed(bias.shape),
        ],
        out_specs=[per_step(s.shape) for s in shapes],
        out_shape=shapes,
        compiler_params=params(),
        name="front",
    )(x, qkv_weight, proj_weight, vectors, bias)


def mlp_in_kernel(chunk, hn_ref, gy_ref, vec_ref, bup_ref, wup_ref, z_ref, slope_ref, gdn_ref, dm_ref, turned_ref):
    tokens = hn_ref.shape[0]

    @pl.when(pl.program_id(0) == 0)
    def _():
        def rows(step, carry):
            at = pl.ds(pl.multiple_of(step * chunk, chunk), chunk)
            dm_ref[at, :] = (vec_ref[9:10, :] * gy_ref[at, :].astype(F32)).astype(BF)
            return carry

        lax.fori_loop(0, tokens // chunk, rows, 0)
        turned_ref[...] = dm_ref[...].T

    def rows(step, carry):
        at = pl.ds(pl.multiple_of(step * chunk, chunk), chunk)
        u = mm(hn_ref[at, :], wup_ref[0]) + bup_ref[0]
        gate = 0.5 * (1.0 + lax.erf(u * 0.7071067811865476))
        z_ref[0, at, :] = (u * gate).astype(BF)
        slope_ref[0, at, :] = (gate + u * jnp.exp(-0.5 * u * u) * 0.3989422804014327).astype(BF)
        return carry

    lax.fori_loop(0, tokens // chunk, rows, 0)
    gdn_ref[0] = mm(turned_ref[...], z_ref[0]).astype(BF)


def mlp_in(hn, gy, vectors, up_bias, up_all, chunk):
    tokens, width = hn.shape
    blocks, _, hidden = up_all.shape
    shapes = [
        jax.ShapeDtypeStruct((blocks, tokens, hidden), BF),
        jax.ShapeDtypeStruct((blocks, tokens, hidden), BF),
        jax.ShapeDtypeStruct((blocks, width, hidden), BF),
    ]
    return pl.pallas_call(
        functools.partial(mlp_in_kernel, chunk),
        grid=(blocks,),
        in_specs=[
            fixed(hn.shape),
            fixed(gy.shape),
            fixed(vectors.shape),
            per_step(up_bias.shape),
            per_step(up_all.shape),
        ],
        out_specs=[per_step(s.shape) for s in shapes] + [fixed((tokens, width))],
        out_shape=shapes + [jax.ShapeDtypeStruct((tokens, width), BF)],
        scratch_shapes=[pltpu.VMEM((width, tokens), BF)],
        compiler_params=params(),
        name="mlp_in",
    )(hn, gy, vectors, up_bias, up_all)


def place(keep_ref, send_ref, at, core, mine, value):
    @pl.when(core == mine)
    def _():
        keep_ref[at] = value

    @pl.when(core != mine)
    def _():
        send_ref[at] = value


def mlp_out_kernel(
    chunk, mine, hn_ref, dm_ref, z_ref, slope_ref, wup_ref, wdn_ref,
    m_ref, dhn_ref, keep_ref, send_ref, gb_ref, du_ref, turned_ref,
):
    tokens = hn_ref.shape[0]

    @pl.when(pl.program_id(0) == 0)
    def _():
        m_ref[...] = jnp.zeros_like(m_ref)
        dhn_ref[...] = jnp.zeros_like(dhn_ref)
        turned_ref[...] = hn_ref[...].T

    gb_ref[...] = jnp.zeros_like(gb_ref)

    def rows(step, carry):
        at = pl.ds(pl.multiple_of(step * chunk, chunk), chunk)
        m_ref[at, :] += mm_nt(z_ref[0, at, :], wdn_ref[0])
        du = (mm(dm_ref[at, :], wdn_ref[0]) * slope_ref[0, at, :].astype(F32)).astype(BF)
        du_ref[at, :] = du
        gb_ref[0] += jnp.sum(du.astype(F32), 0, keepdims=True)
        dhn_ref[at, :] += mm_nt(du, wup_ref[0])
        return carry

    lax.fori_loop(0, tokens // chunk, rows, 0)
    place(keep_ref, send_ref, 0, pl.program_id(0) & 1, mine(), mm(turned_ref[...], du_ref[...]).astype(BF))


def mlp_out(hn, dm, z, slope, up_all, down_all, chunk, mine):
    tokens, width = hn.shape
    blocks, _, hidden = up_all.shape
    shapes = [
        jax.ShapeDtypeStruct((tokens, width), F32),
        jax.ShapeDtypeStruct((tokens, width), F32),
        jax.ShapeDtypeStruct((blocks // 2, width, hidden), BF),
        jax.ShapeDtypeStruct((blocks // 2, width, hidden), BF),
        jax.ShapeDtypeStruct((blocks, 1, hidden), F32),
    ]
    by_pair = pl.BlockSpec((1, width, hidden), lambda i: (i // 2, 0, 0))
    return pl.pallas_call(
        functools.partial(mlp_out_kernel, chunk, mine),
        grid=(blocks,),
        in_specs=[fixed(hn.shape), fixed(dm.shape)] + [per_step(v.shape) for v in (z, slope, up_all, down_all)],
        out_specs=[fixed(s.shape) for s in shapes[:2]] + [by_pair, by_pair, per_step(shapes[4].shape)],
        out_shape=shapes,
        scratch_shapes=[pltpu.VMEM((tokens, hidden), BF), pltpu.VMEM((width, tokens), BF)],
        compiler_params=params(),
        name="mlp_out",
    )(hn, dm, z, slope, up_all, down_all)


def middle_kernel(
    x_ref, gy_ref, attn_ref, m_ref, dhn_ref, wproj_ref, vec_ref, out_ref, dmid_ref, dat_ref, do_ref, gvec_ref
):
    @pl.when(pl.program_id(0) == 0)
    def _():
        gvec_ref[...] = jnp.zeros_like(gvec_ref)

    attn = attn_ref[0]
    middle = x_ref[0].astype(F32) + vec_ref[8:9, :] * attn
    branch = m_ref[0] + vec_ref[3:4, :]
    out_ref[0] = (middle + vec_ref[9:10, :] * branch).astype(BF)
    cotangent = gy_ref[0].astype(F32)
    normed, factor = normalized(middle)
    dhn = dhn_ref[0]
    dmid = cotangent + layer_back(dhn, normed, factor, vec_ref[6:7, :])
    dmid_ref[0] = dmid
    dat = (vec_ref[8:9, :] * dmid).astype(BF)
    dat_ref[0] = dat
    down_in = (vec_ref[9:10, :] * cotangent).astype(BF)
    for row, value in enumerate(
        (dat.astype(F32), down_in.astype(F32), dhn * normed, dhn, dmid * attn, cotangent * branch)
    ):
        gvec_ref[row : row + 1, :] += jnp.sum(value, 0, keepdims=True)
    do_ref[0] = mm_nt(dat, wproj_ref[...]).astype(BF)


def middle_back(x, gy, attn, m, dhn, proj_weight, vectors):
    images, seq, width = x.shape
    shapes = [
        jax.ShapeDtypeStruct((images, seq, width), BF),
        jax.ShapeDtypeStruct((images, seq, width), F32),
        jax.ShapeDtypeStruct((images, seq, width), BF),
        jax.ShapeDtypeStruct((images, seq, width), BF),
        jax.ShapeDtypeStruct((8, width), F32),
    ]
    return pl.pallas_call(
        middle_kernel,
        grid=(images,),
        in_specs=[per_step(v.shape) for v in (x, gy, attn, m, dhn)] + [fixed(proj_weight.shape), fixed(vectors.shape)],
        out_specs=[per_step(s.shape) for s in shapes[:4]] + [fixed(shapes[4].shape)],
        out_shape=shapes,
        compiler_params=params(),
        name="middle_back",
    )(x, gy, attn, m, dhn, proj_weight, vectors)


def back_kernel(heads, qkv_ref, do_ref, bias_ref, dqkv_ref, ds_ref, gcol_ref):
    width = do_ref.shape[2]
    head_dim = width // heads
    scale = head_dim ** (-0.5)

    @pl.when(pl.program_id(0) == 0)
    def _():
        ds_ref[...] = jnp.zeros_like(ds_ref)
        gcol_ref[...] = jnp.zeros_like(gcol_ref)

    pair = LANES
    masks = head_masks(pair, head_dim)
    per = pair // head_dim

    def one_pair(g, carry):
        at = pl.multiple_of(g * pair, pair)
        q = qkv_ref[0, :, pl.ds(at, pair)]
        k = qkv_ref[0, :, pl.ds(at + width, pair)]
        v = qkv_ref[0, :, pl.ds(at + 2 * width, pair)]
        do = do_ref[0, :, pl.ds(at, pair)]
        dq = dk = dv = None
        for e in range(per):
            pick = jnp.where(masks[e], scale, 0.0).astype(BF)
            keep = jnp.where(masks[e], 1.0, 0.0).astype(BF)
            qm, km, dom = q * pick, k * pick, do * keep
            s = mm_nt(k, qm) + bias_ref[g * per + e]
            p = jnp.exp(s - jnp.max(s, 0, keepdims=True))
            p = p * (1.0 / jnp.sum(p, 0, keepdims=True))
            dv_e = mm(p.astype(BF), dom)
            dp = mm_nt(v, dom)
            ds = (p * (dp - jnp.sum(dp * p, 0, keepdims=True))).astype(BF)
            ds_ref[g * per + e] += ds.astype(F32)
            dk_e = mm(ds, qm)
            dq_e = mm_tn(ds, km)
            dq = dq_e if dq is None else dq + dq_e
            dk = dk_e if dk is None else dk + dk_e
            dv = dv_e if dv is None else dv + dv_e
        for part, value in ((0, dq), (1, dk), (2, dv)):
            rounded = value.astype(BF)
            dqkv_ref[0, :, pl.ds(at + part * width, pair)] = rounded
            gcol_ref[:, pl.ds(at + part * width, pair)] += jnp.sum(rounded.astype(F32), 0, keepdims=True)
        return carry

    lax.fori_loop(0, width // pair, one_pair, 0, unroll=UNROLL_B)


def back(qkv, do, bias, heads):
    images, seq, width = do.shape
    shapes = [
        jax.ShapeDtypeStruct((images, seq, 3 * width), BF),
        jax.ShapeDtypeStruct((heads, seq, seq), F32),
        jax.ShapeDtypeStruct((1, 3 * width), F32),
    ]
    return pl.pallas_call(
        functools.partial(back_kernel, heads),
        grid=(images,),
        in_specs=[per_step(qkv.shape), per_step(do.shape), fixed(bias.shape)],
        out_specs=[per_step(shapes[0].shape)] + [fixed(s.shape) for s in shapes[1:]],
        out_shape=shapes,
        compiler_params=params(),
        name="back",
    )(qkv, do, bias)


def grads_kernel(blocks, mine, a_ref, dqkv_ref, o_ref, dat_ref, keep_ref, send_ref, turned_a, turned_o):
    wide_cols, thin_cols = dqkv_ref.shape[1] // blocks, dat_ref.shape[1] // blocks
    turned_a[...] = a_ref[...].T
    turned_o[...] = o_ref[...].T
    here = mine()
    for n in range(blocks):
        left = mm(turned_a[...], dqkv_ref[:, n * wide_cols : (n + 1) * wide_cols]).astype(BF)
        right = mm(turned_o[...], dat_ref[:, n * thin_cols : (n + 1) * thin_cols]).astype(BF)
        place(keep_ref, send_ref, n // 2, n & 1, here, jnp.concatenate([left, right], 1))


def attention_grads(first, dqkv, mixed, dat, blocks, mine):
    width = first.shape[1]
    cols = (dqkv.shape[1] + dat.shape[1]) // blocks
    shape = (blocks // 2, width, cols)
    return pl.pallas_call(
        functools.partial(grads_kernel, blocks, mine),
        grid=(1,),
        in_specs=[whole(v.shape) for v in (first, dqkv, mixed, dat)],
        out_specs=[whole(shape)] * 2,
        out_shape=[jax.ShapeDtypeStruct(shape, BF)] * 2,
        scratch_shapes=[pltpu.VMEM((width, first.shape[0]), BF)] * 2,
        compiler_params=params(),
        name="attention_grads",
    )(first, dqkv, mixed, dat)


def input_kernel(x_ref, dqkv_ref, dmid_ref, wqkv_ref, vec_ref, out_ref, gvec_ref):
    @pl.when(pl.program_id(0) == 0)
    def _():
        gvec_ref[...] = jnp.zeros_like(gvec_ref)

    da = mm_nt(dqkv_ref[0], wqkv_ref[...])
    normed, factor = normalized(x_ref[0].astype(F32))
    gvec_ref[0:1, :] += jnp.sum(da * normed, 0, keepdims=True)
    gvec_ref[1:2, :] += jnp.sum(da, 0, keepdims=True)
    out_ref[0] = dmid_ref[0] + layer_back(da, normed, factor, vec_ref[4:5, :])


def input_grads(x, dqkv, dmid, qkv_weight, vectors):
    images, seq, width = x.shape
    shapes = [
        jax.ShapeDtypeStruct((images, seq, width), F32),
        jax.ShapeDtypeStruct((8, width), F32),
    ]
    return pl.pallas_call(
        input_kernel,
        grid=(images,),
        in_specs=[per_step(v.shape) for v in (x, dqkv, dmid)]
        + [fixed(qkv_weight.shape), fixed(vectors.shape)],
        out_specs=[per_step(shapes[0].shape), fixed(shapes[1].shape)],
        out_shape=shapes,
        compiler_params=params(),
        name="input_grads",
    )(x, dqkv, dmid, qkv_weight, vectors)


def adam_update(master, mean, square, grad, rate, decay):
    mean_new = beta_one * mean + (1.0 - beta_one) * grad
    square_new = beta_two * square + (1.0 - beta_two) * grad * grad
    fix_one = 1.0 - beta_one**STEP
    fix_two = 1.0 - beta_two**STEP
    direction = mean_new / fix_one / (jnp.sqrt(square_new / fix_two) + adam_eps)
    return (mean_new, square_new, master - rate * (direction + decay * master))


def adam_kernel(rows, ours_ref, theirs_ref, attn_ref, up_ref, down_ref, *refs):
    state, results = refs[:21], refs[21:]
    sums = ours_ref[...] + theirs_ref[...]
    heads, vec_at, bias_at, square_at = rows
    row = lax.broadcasted_iota(jnp.int32, sums.shape, 0)
    small = jnp.where(row < square_at, sums, 0.0)
    total = jnp.sum(
        jnp.sum(small * small, 0, keepdims=True) + sums[square_at : square_at + 1], 1, keepdims=True
    )
    norm = jnp.sqrt(total)
    results[0][...] = norm
    clip = jnp.minimum(1.0, max_norm / (norm + clip_eps))
    split = state[0].shape[1]
    vec_rows, table_rows = state[12].shape[0], state[18].shape[1]
    bias = jnp.concatenate([sums[r : r + 1] for r in range(bias_at, square_at)], 1)
    grads = (
        attn_ref[:, :split],
        attn_ref[:, split:],
        up_ref[...],
        down_ref[...].astype(F32),
        sums[vec_at : vec_at + vec_rows],
        bias,
        sums[:heads, :table_rows],
    )
    at = 1
    for n, grad in enumerate(grads):
        large = n < 4
        mean_new, square_new, master_new = adam_update(
            *(state[3 * n + k][...] for k in range(3)),
            clip * grad,
            rate_matrix if large else rate_small,
            weight_decay if large else 0.0,
        )
        values = [mean_new, square_new, master_new]
        if large:
            values.append(master_new.astype(BF))
        for value in values:
            results[at][...] = value
            at += 1


def adam(rows, ours, theirs, shards, state):
    shapes = [jax.ShapeDtypeStruct((1, 1), F32)]
    for n in range(7):
        shapes += [jax.ShapeDtypeStruct(state[3 * n].shape, F32)] * 3
        if n < 4:
            shapes.append(jax.ShapeDtypeStruct(state[3 * n].shape, BF))
    inputs = [ours, theirs, *shards, *state]
    return pl.pallas_call(
        functools.partial(adam_kernel, rows),
        grid=(1,),
        in_specs=[whole(v.shape) for v in inputs],
        out_specs=[whole(v.shape) for v in shapes],
        out_shape=shapes,
        compiler_params=params(),
        name="adam",
    )(*inputs)


def axis_bits():
    found = []
    for axis in ("narrow", "wide"):
        count = lax.axis_size(axis).bit_length() - 1
        found += [(axis, count - 1 - at) for at in range(count)]
    return found


def swap(value, axis, bit):
    size = lax.axis_size(axis)
    return lax.ppermute(value, axis, [(i, i ^ (1 << bit)) for i in range(size)])


def split_kernel(mine, keep_ref, come_ref, keep_a, send_a, keep_b, send_b):
    half = keep_ref.shape[4] // 2
    for out_a, out_b, flip in ((keep_a, keep_b, 0), (send_a, send_b, 1)):
        side_a, side_b = mine[0]() ^ flip, mine[1]() ^ flip
        for n in range(2):
            for out, at, cols in (
                (out_a.at[0, n], (side_a, 0, n), slice(0, half)),
                (out_b.at[n, 0], (n, 0, side_b), slice(half, 2 * half)),
            ):
                total = keep_ref[(*at, slice(None), cols)].astype(F32) + come_ref[(*at, slice(None), cols)].astype(F32)
                out[...] = total.astype(BF)


def split_step(keep, come, mine):
    _, middle, _, rows, cols = keep.shape
    side = cols // 2
    block = pl.BlockSpec((2, 1, 2, rows, cols), lambda i: (0, i, 0, 0, 0))
    out_a = pl.BlockSpec((1, 2, rows, side), lambda i: (i, 0, 0, 0))
    out_b = pl.BlockSpec((2, 1, rows, side), lambda i: (0, i, 0, 0))
    shape_a = jax.ShapeDtypeStruct((middle, 2, rows, side), BF)
    shape_b = jax.ShapeDtypeStruct((2, middle, rows, side), BF)
    return pl.pallas_call(
        functools.partial(split_kernel, mine),
        grid=(middle,),
        in_specs=[block, block],
        out_specs=[out_a, out_a, out_b, out_b],
        out_shape=[shape_a, shape_a, shape_b, shape_b],
        compiler_params=params(),
        name="split_step",
    )(keep, come)


def halve_kernel(mine, places, join, *refs):
    parts = len(places)
    ins, outs = refs[: 2 * parts], refs[2 * parts :]
    for n in range(parts):
        keep_ref, come_ref = ins[2 * n : 2 * n + 2]
        count, _, cols = keep_ref.shape
        left = cols * n if join else 0
        outputs = outs[:2] if join else outs[2 * n : 2 * n + 2]
        low = places[n]

        def one(c, carry):
            for out, side in zip(outputs, (mine[n](), 1 - mine[n]())):
                at = ((c >> low) << (low + 1)) | (side << low) | (c & ((1 << low) - 1))
                total = keep_ref[at].astype(F32) + come_ref[at].astype(F32)
                out[c, :, left : left + cols] = total.astype(BF)
            return carry

        lax.fori_loop(0, count // 2, one, 0)


def halve_step(parts, places, mine, join):
    inputs = [v for pair in parts for v in pair]
    shapes = []
    for keep, _ in parts[:1] if join else parts:
        count, rows, cols = keep.shape
        shapes += [jax.ShapeDtypeStruct((count // 2, rows, cols * len(parts) if join else cols), BF)] * 2
    return pl.pallas_call(
        functools.partial(halve_kernel, mine, places, join),
        grid=(1,),
        in_specs=[whole(v.shape) for v in inputs],
        out_specs=[whole(v.shape) for v in shapes],
        out_shape=shapes,
        compiler_params=params(),
        name="halve_step",
    )(*inputs)


class Halving:
    def __init__(self, keep, send, rows):
        self.bits = axis_bits()
        cores = [d for d, (axis, _) in enumerate(self.bits) if axis == "narrow"]
        self.dims = [[d for d in range(len(self.bits)) if d != cores[-1]]]
        first, last = self.dims[0][0], self.dims[0][-1]
        self.steps = [(first, last), (last, first)] + [(d,) for d in self.dims[0][-2:0:-1]]
        shape = (-1, rows, keep.shape[-1])
        self.keep = [keep.reshape(shape)]
        self.sent = (send.reshape(shape),)
        self.come = [swap(self.sent[0], *self.bits[cores[-1]])]

    def mine(self, dim):
        axis, bit = self.bits[dim]
        return lambda: (lax.axis_index(axis) >> bit) & 1

    def send(self, *after):
        target = self.steps.pop(0)
        come = lax.optimization_barrier((*self.come, *after)) if after else self.come
        parts = len(self.keep)
        if len(target) > parts:
            rows, cols = self.keep[0].shape[1:]
            shape = (2, -1, 2, rows, cols)
            made = split_step(self.keep[0].reshape(shape), come[0].reshape(shape), [self.mine(d) for d in target])
            made = [v.reshape(-1, rows, cols // 2) for v in made]
            self.dims = self.dims * 2
        else:
            dims = target * (parts // len(target))
            places = [len(own) - 1 - own.index(d) for own, d in zip(self.dims, dims)]
            made = halve_step(
                list(zip(self.keep, come)), places, [self.mine(d) for d in dims], len(target) < parts
            )
        self.keep, self.sent = made[::2], tuple(made[1::2])
        self.dims = [[d for d in own if d != gone] for own, gone in zip(self.dims, target)]
        self.come = [swap(v, *self.bits[d]) for v, d in zip(self.sent, target)]
        return self.sent

    def last_pair(self):
        while self.steps:
            self.send()
        return self.keep[0][0], self.come[0][0]


def finish_kernel(rows, up_a, up_b, attn_a, attn_b, down_ref, table_ref, cols_ref, gvec_ref, gone_ref, gb_ref, up_ref, attn_ref, ours_ref):
    _, vec_at, bias_at, square_at = rows
    width = ours_ref.shape[1]
    up = up_a[...].astype(F32) + up_b[...].astype(F32)
    attn = attn_a[...].astype(F32) + attn_b[...].astype(F32)
    down = down_ref[...].astype(F32)
    up_ref[...] = up
    attn_ref[...] = attn
    squares = jnp.sum(up * up + attn * attn + down * down, 0, keepdims=True)
    ours_ref[...] = jnp.zeros_like(ours_ref)
    for c in range(table_ref.shape[0]):
        ours_ref[:vec_at, c * LANES : (c + 1) * LANES] = table_ref[c, 0] + table_ref[c, 1]
    ours_ref[vec_at : vec_at + 1, :] = cols_ref[:, :width]
    ours_ref[vec_at + 1 : vec_at + 2, :] = cols_ref[:, 2 * width :]
    for to, source, at in ((2, gvec_ref, 0), (3, gvec_ref, 1), (4, gone_ref, 0), (5, gone_ref, 1)) + tuple(
        (6 + n, gvec_ref, 2 + n) for n in range(4)
    ):
        ours_ref[vec_at + to : vec_at + to + 1, :] = source[at : at + 1, :]
    for n in range(square_at - bias_at):
        ours_ref[bias_at + n : bias_at + n + 1, :] = gb_ref[n]
    ours_ref[square_at : square_at + 1, :] = squares


def finish(rows, up, attn, down, small):
    inputs = [*up, *attn, down, *small]
    width = down.shape[1]
    shapes = [jax.ShapeDtypeStruct(v.shape, F32) for v in (up[0], attn[0])]
    shapes.append(jax.ShapeDtypeStruct((-(-(rows[3] + 1) // 8) * 8, width), F32))
    return pl.pallas_call(
        functools.partial(finish_kernel, rows),
        grid=(1,),
        in_specs=[whole(v.shape) for v in inputs],
        out_specs=[whole(v.shape) for v in shapes],
        out_shape=shapes,
        compiler_params=params(),
        name="finish",
    )(*inputs)


def gated(value, *waits):
    return lax.optimization_barrier((value,) + waits)[0] if waits else value


class Plan:
    def __init__(self, rows):
        self.rows = rows

    @staticmethod
    def mine():
        return lax.axis_index("narrow") & 1

    def after_down(self, grads):
        rows = grads.reshape(-1, grads.shape[2])
        self.down = lax.psum_scatter(rows, ("narrow", "wide"), scatter_dimension=0, tiled=True)

    def after_up(self, keep, send):
        self.up = Halving(keep, send, self.rows)
        return self.up.sent

    def next_up(self, *after):
        return self.up.send(*after)

    def after_attention(self, keep, send):
        self.attn = Halving(keep, send, self.rows)
        return self.attn.sent

    def next_attention(self, *after):
        return self.attn.send(*after)

    def next_both(self, *after):
        self.up.send(*after)
        self.attn.send(*after)


class Alone:
    @staticmethod
    def mine():
        return 0

    def after_down(self, grads):
        self.down = grads

    def after_up(self, *grads):
        self.up = grads
        return ()

    def after_attention(self, *grads):
        self.attn = grads
        return ()

    def next_up(self, *after):
        return ()

    next_attention = next_both = next_up


def local_work(
    block_in, out_grad, mim_mask, rel_index, qkv_weight, proj_weight, up_all, down_all, vectors, up_bias, rel_table, plan=None
):
    plan = plan or Alone()
    images, seq, width = block_in.shape
    table_rows, heads = rel_table.shape
    blocks, _, hidden = up_all.shape
    tokens = images * seq
    chunks = -(-table_rows // LANES)
    padded_seq = -(-seq // LANES) * LANES
    key_at = jnp.arange(seq, dtype=jnp.int32)
    index = jnp.where(key_at[None, :] < VALID, rel_index, chunks * LANES)
    index_t = index.T
    padded = jnp.pad(index, ((0, 0), (0, padded_seq - seq)))
    table_t = jnp.pad(rel_table, ((0, chunks * LANES - table_rows), (0, 0))).T.reshape(heads, chunks, LANES)
    bias, bias_t = bias_tables(padded, table_t)
    gy = out_grad * mim_mask.astype(BF)[:, :, None]
    first, qkv, mixed, attn, hn = front(block_in, qkv_weight, proj_weight, vectors, bias, heads)
    flat = lambda v: v.reshape(tokens, v.shape[-1])
    z, slope, grad_down, dm = mlp_in(flat(hn), flat(gy), vectors, up_bias.reshape(blocks, 1, hidden), up_all, tokens)
    plan.after_down(grad_down)
    m, dhn, keep, send, grad_bias = mlp_out(flat(hn), dm, z, slope, up_all, down_all, tokens, plan.mine)
    gy = gated(gy, *plan.after_up(keep, send))
    fold = lambda v: v.reshape(images, seq, width)
    block_out, dmid, dat, do, gvec = middle_back(block_in, gy, attn, fold(m), fold(dhn), proj_weight, vectors)
    do = gated(do, *plan.next_up(do))
    dqkv, ds, gcol = back(qkv, do, bias_t, heads)
    dat = gated(dat, *plan.next_up(dqkv))
    keep, send = attention_grads(flat(first), flat(dqkv), flat(mixed), flat(dat), blocks, plan.mine)
    dmid = gated(dmid, *plan.after_attention(keep, send))
    input_grad, gvec_one = input_grads(block_in, dqkv, dmid, qkv_weight, vectors)
    by_key = jnp.pad(ds.transpose(1, 0, 2), ((0, 0), (0, (-heads) % 8), (0, 0)))
    by_key = gated(by_key, *plan.next_attention(input_grad))
    sums = table_sums(index_t, by_key, chunks)
    plan.next_both(sums)
    small = (sums.reshape(chunks, 2, -1, LANES), gcol, gvec, gvec_one, grad_bias)
    return block_out, input_grad, small, plan


def shards(
    block_in,
    out_grad,
    mim_mask,
    rel_index,
    qkv_weight,
    proj_weight,
    up_weight,
    down_weight,
    vectors,
    up_bias,
    rel_table,
    *state,
):
    width = block_in.shape[2]
    heads = rel_table.shape[1]
    up_all = lax.all_gather(up_weight, "narrow", axis=0)
    down_all = lax.all_gather(down_weight, "narrow", axis=0)
    plan = Plan(width // lax.axis_size("wide"))
    block_out, input_grad, small, plan = local_work(
        block_in, out_grad, mim_mask, rel_index, qkv_weight, proj_weight, up_all, down_all, vectors, up_bias, rel_table, plan
    )
    vec_at = heads + (-heads) % 8
    bias_at = vec_at + vectors.shape[0]
    rows = (heads, vec_at, bias_at, bias_at + up_bias.shape[0] // width)
    down_shard = plan.down
    up_shard, attn_shard, ours = finish(rows, plan.up.last_pair(), plan.attn.last_pair(), down_shard, small)
    theirs = None
    for axis, bit in reversed(axis_bits()):
        ours = ours if theirs is None else ours + theirs
        theirs = swap(ours, axis, bit)
    line = lambda v: v.reshape(1, -1)
    matrices = state[:12]
    params_small = (vectors, state[12], state[13], line(up_bias), line(state[14]), line(state[15]), rel_table.T, *(v.T for v in state[16:]))
    norm, *updated = adam(
        rows,
        ours,
        theirs,
        (attn_shard, up_shard, down_shard),
        [matrices[3 * n + k] for n in range(4) for k in range(3)] + [params_small[3 * n + k] for n in range(3) for k in range(3)],
    )
    for n in range(19, 22):
        updated[n] = updated[n].reshape(up_bias.shape)
        updated[n + 3] = updated[n + 3].T
    return (block_out, input_grad, norm.reshape(()), *updated)


def solution(mesh):
    token = P(("wide", "narrow"), None, None)
    whole_spec = P()
    shard = P("wide", "narrow")
    in_specs = (
        (token, token, P(("wide", "narrow"), None))
        + (whole_spec,) * 3
        + (P(None, "narrow"),) * 2
        + (whole_spec,) * 3
        + (shard,) * 12
        + (whole_spec,) * 6
    )
    out_specs = (token, token, whole_spec) + (shard,) * 16 + (whole_spec,) * 9
    return jax.shard_map(shards, mesh=mesh, in_specs=in_specs, out_specs=out_specs, check_vma=False)
```

```python
import functools

import jax
import jax.numpy as jnp
from jax import lax
from jax.experimental import pallas as pl
from jax.experimental.pallas import tpu as pltpu
from jax.sharding import PartitionSpec as P

VALID = 197
STEP = 10
LANES = 128

norm_eps = 1e-06
clip_eps = 1e-06
max_norm = 1.0
beta_one = 0.9
beta_two = 0.999
adam_eps = 1e-08
rate_matrix = 0.05
rate_small = 0.4
weight_decay = 0.05
BF = jnp.bfloat16
F32 = jnp.float32
ROWS_ROWS = (((0,), (0,)), ((), ()))
COLS_COLS = (((1,), (1,)), ((), ()))
VMEM_LIMIT = 60000 * 1024
UNROLL_F = 3
UNROLL_B = 3
UNROLL_T = 8


def mm(a, b):
    return jnp.dot(a, b, preferred_element_type=F32)


def mm_nt(a, b):
    return lax.dot_general(a, b, COLS_COLS, preferred_element_type=F32)


def mm_tn(a, b):
    return lax.dot_general(a, b, ROWS_ROWS, preferred_element_type=F32)


def params(steps=1):
    return pltpu.CompilerParams(
        dimension_semantics=("arbitrary",) * steps, vmem_limit_bytes=VMEM_LIMIT
    )


def whole(shape):
    zeros = (0,) * len(shape)
    return pl.BlockSpec(shape, lambda i: zeros)


def fixed(shape):
    zeros = (0,) * len(shape)
    return pl.BlockSpec(shape, lambda i: zeros, pipeline_mode=pl.Buffered(1))


def per_step(shape):
    rest = (0,) * (len(shape) - 1)
    return pl.BlockSpec((1,) + tuple(shape[1:]), lambda i: (i,) + rest)


def normalized(values):
    center = values - jnp.mean(values, -1, keepdims=True)
    factor = lax.rsqrt(jnp.mean(center * center, -1, keepdims=True) + norm_eps)
    return center * factor, factor


def layer_back(grad, normed, factor, gain_vec):
    scaled = grad * gain_vec
    return factor * (
        scaled
        - jnp.mean(scaled, -1, keepdims=True)
        - normed * jnp.mean(scaled * normed, -1, keepdims=True)
    )


def head_masks(pair_width, head_dim):
    lane = lax.broadcasted_iota(jnp.int32, (1, pair_width), 1)
    return [
        ((lane >= e * head_dim) & (lane < (e + 1) * head_dim)) for e in range(pair_width // head_dim)
    ]


def bias_kernel(idx_ref, tab_ref, out_ref):
    heads, seq = out_ref.shape[0], out_ref.shape[1]
    chunks = tab_ref.shape[1]

    def rows(step, carry):
        at = pl.multiple_of(step * 8, 8)
        for left in range(0, seq, LANES):
            index = idx_ref[pl.ds(at, 8), left : left + LANES]
            low, high = index & (LANES - 1), index >> 7
            match = [high == c for c in range(chunks)]
            width = min(LANES, seq - left)
            for h in range(heads):
                found = jnp.full((8, LANES), -1e30, F32)
                for c in range(chunks):
                    row = jnp.broadcast_to(tab_ref[h, c : c + 1, :], (8, LANES))
                    taken = jnp.take_along_axis(row, low, axis=1, mode="promise_in_bounds")
                    found = jnp.where(match[c], taken, found)
                out_ref[h, pl.ds(at, 8), left : left + width] = found[:, :width]
        return carry

    lax.fori_loop(0, seq // 8, rows, 0)


def bias_tables(index, table_rows):
    seq, _ = index.shape
    heads, _, _ = table_rows.shape
    shape = (heads, seq, seq)
    return pl.pallas_call(
        bias_kernel,
        grid=(1,),
        in_specs=[whole(index.shape), whole(table_rows.shape)],
        out_specs=whole(shape),
        out_shape=jax.ShapeDtypeStruct(shape, F32),
        compiler_params=params(),
        name="bias_tables",
    )(index, table_rows)


def table_kernel(idx_ref, ds_ref, out_ref):
    seq, heads, _ = ds_ref.shape
    chunks = out_ref.shape[0] // (2 * heads)
    out_ref[...] = jnp.zeros_like(out_ref)
    kinds = lax.broadcasted_iota(jnp.int32, (LANES, seq), 0)

    def one_query(j, total):
        index = idx_ref[pl.ds(j, 1), :]
        low, high = index & (LANES - 1), index >> 7
        onehot = jnp.where(jnp.broadcast_to(low, (LANES, seq)) == kinds, 1.0, 0.0).astype(BF)
        grads = ds_ref[j]
        top = grads.astype(BF).astype(F32)
        both = jnp.concatenate([top, grads - top], 0)
        high_all = jnp.broadcast_to(high, both.shape)
        parts = jnp.concatenate([jnp.where(high_all == c, both, 0.0) for c in range(chunks)], 0)
        return total + mm_nt(parts.astype(BF), onehot)

    out_ref[...] = lax.fori_loop(0, seq, one_query, jnp.zeros(out_ref.shape, F32), unroll=UNROLL_T)


def table_sums(index, grads, chunks):
    seq, heads, _ = grads.shape
    out = (chunks * 2 * heads, LANES)
    return pl.pallas_call(
        table_kernel,
        grid=(1,),
        in_specs=[whole(index.shape), whole(grads.shape)],
        out_specs=whole(out),
        out_shape=jax.ShapeDtypeStruct(out, F32),
        compiler_params=params(),
        name="table_sums",
    )(index, grads)


def front_kernel(heads, x_ref, wqkv_ref, wproj_ref, vec_ref, bias_ref, a_ref, qkv_ref, p_ref, o_ref, attn_ref, hn_ref):
    width = x_ref.shape[2]
    head_dim = width // heads
    scale = head_dim ** (-0.5)
    x = x_ref[0].astype(F32)
    normed, _ = normalized(x)
    first = (normed * vec_ref[4:5, :] + vec_ref[5:6, :]).astype(BF)
    a_ref[0] = first
    for part, row in ((0, 0), (1, None), (2, 1)):
        cols = slice(part * width, (part + 1) * width)
        value = mm(first, wqkv_ref[:, cols])
        if row is not None:
            value = value + vec_ref[row : row + 1, :]
        qkv_ref[0, :, cols] = value.astype(BF)
    pair = LANES
    masks = head_masks(pair, head_dim)
    per = pair // head_dim

    def one_pair(g, carry):
        at = pl.multiple_of(g * pair, pair)
        q = qkv_ref[0, :, pl.ds(at, pair)]
        k = qkv_ref[0, :, pl.ds(at + width, pair)]
        v = qkv_ref[0, :, pl.ds(at + 2 * width, pair)]
        out = None
        for e in range(per):
            qm = q * jnp.where(masks[e], scale, 0.0).astype(BF)
            s = mm_nt(qm, k) + bias_ref[g * per + e]
            p = jnp.exp(s - jnp.max(s, -1, keepdims=True))
            p = p * (1.0 / jnp.sum(p, -1, keepdims=True))
            p = p.astype(BF)
            p_ref[0, g * per + e] = p
            mixed = mm(p, v)
            out = mixed if out is None else jnp.where(masks[e], mixed, out)
        o_ref[0, :, pl.ds(at, pair)] = out.astype(BF)
        return carry

    lax.fori_loop(0, width // pair, one_pair, 0, unroll=UNROLL_F)
    attn = mm(o_ref[0], wproj_ref[...]) + vec_ref[2:3, :]
    attn_ref[0] = attn
    middle, _ = normalized(x + vec_ref[8:9, :] * attn)
    hn_ref[0] = (middle * vec_ref[6:7, :] + vec_ref[7:8, :]).astype(BF)


def front(x, qkv_weight, proj_weight, vectors, bias, heads):
    images, seq, width = x.shape
    shapes = [
        jax.ShapeDtypeStruct((images, seq, width), BF),
        jax.ShapeDtypeStruct((images, seq, 3 * width), BF),
        jax.ShapeDtypeStruct((images, heads, seq, seq), BF),
        jax.ShapeDtypeStruct((images, seq, width), BF),
        jax.ShapeDtypeStruct((images, seq, width), F32),
        jax.ShapeDtypeStruct((images, seq, width), BF),
    ]
    return pl.pallas_call(
        functools.partial(front_kernel, heads),
        grid=(images,),
        in_specs=[
            per_step(x.shape),
            fixed(qkv_weight.shape),
            fixed(proj_weight.shape),
            fixed(vectors.shape),
            fixed(bias.shape),
        ],
        out_specs=[per_step(s.shape) for s in shapes],
        out_shape=shapes,
        compiler_params=params(),
        name="front",
    )(x, qkv_weight, proj_weight, vectors, bias)


def pick(refs, at, out_ref):
    for n, ref in enumerate(refs):

        @pl.when(at == n)
        def _():
            out_ref[...] = ref[...]


def mlp_in_kernel(
    chunk, owner, hn_ref, gy_ref, vec_ref, bup_ref, up_a, up_b, up_c, up_d,
    z_ref, slope_ref, gdn_ref, dm_ref, turned_ref, wup_ref,
):
    tokens = hn_ref.shape[0]
    pick((up_a, up_b, up_c, up_d), pl.program_id(0) ^ owner(), wup_ref)

    @pl.when(pl.program_id(0) == 0)
    def _():
        def rows(step, carry):
            at = pl.ds(pl.multiple_of(step * chunk, chunk), chunk)
            dm_ref[at, :] = (vec_ref[9:10, :] * gy_ref[at, :].astype(F32)).astype(BF)
            return carry

        lax.fori_loop(0, tokens // chunk, rows, 0)
        turned_ref[...] = dm_ref[...].T

    def rows(step, carry):
        at = pl.ds(pl.multiple_of(step * chunk, chunk), chunk)
        u = mm(hn_ref[at, :], wup_ref[...]) + bup_ref[0]
        gate = 0.5 * (1.0 + lax.erf(u * 0.7071067811865476))
        z_ref[0, at, :] = (u * gate).astype(BF)
        slope_ref[0, at, :] = (gate + u * jnp.exp(-0.5 * u * u) * 0.3989422804014327).astype(BF)
        return carry

    lax.fori_loop(0, tokens // chunk, rows, 0)
    gdn_ref[0] = mm(turned_ref[...], z_ref[0]).astype(BF)


def mlp_in(hn, gy, vectors, up_bias, ups, chunk, owner):
    tokens, width = hn.shape
    blocks, hidden = len(ups), ups[0].shape[1]
    shapes = [
        jax.ShapeDtypeStruct((blocks, tokens, hidden), BF),
        jax.ShapeDtypeStruct((blocks, tokens, hidden), BF),
        jax.ShapeDtypeStruct((blocks, width, hidden), BF),
    ]
    return pl.pallas_call(
        functools.partial(mlp_in_kernel, chunk, owner),
        grid=(blocks,),
        in_specs=[
            fixed(hn.shape),
            fixed(gy.shape),
            fixed(vectors.shape),
            per_step(up_bias.shape),
            *(fixed(v.shape) for v in ups),
        ],
        out_specs=[per_step(s.shape) for s in shapes] + [fixed((tokens, width))],
        out_shape=shapes + [jax.ShapeDtypeStruct((tokens, width), BF)],
        scratch_shapes=[pltpu.VMEM((width, tokens), BF), pltpu.VMEM((width, hidden), BF)],
        compiler_params=params(),
        name="mlp_in",
    )(hn, gy, vectors, up_bias, *ups)


def place(keep_ref, send_ref, at, core, mine, value):
    @pl.when(core == mine)
    def _():
        keep_ref[at] = value

    @pl.when(core != mine)
    def _():
        send_ref[at] = value


def mlp_out_kernel(
    chunk, owner, hn_ref, dm_ref, z_ref, slope_ref, wdn_ref, up_a, up_b, up_c, up_d,
    m_ref, dhn_ref, keep_ref, send_ref, gb_ref, du_ref, turned_ref, wup_ref,
):
    tokens = hn_ref.shape[0]
    pick((up_a, up_b, up_c, up_d), pl.program_id(0) ^ owner(), wup_ref)

    @pl.when(pl.program_id(0) == 0)
    def _():
        m_ref[...] = jnp.zeros_like(m_ref)
        dhn_ref[...] = jnp.zeros_like(dhn_ref)
        turned_ref[...] = hn_ref[...].T

    gb_ref[...] = jnp.zeros_like(gb_ref)

    def rows(step, carry):
        at = pl.ds(pl.multiple_of(step * chunk, chunk), chunk)
        m_ref[at, :] += mm_nt(z_ref[0, at, :], wdn_ref[0])
        du = (mm(dm_ref[at, :], wdn_ref[0]) * slope_ref[0, at, :].astype(F32)).astype(BF)
        du_ref[at, :] = du
        gb_ref[0] += jnp.sum(du.astype(F32), 0, keepdims=True)
        dhn_ref[at, :] += mm_nt(du, wup_ref[...])
        return carry

    lax.fori_loop(0, tokens // chunk, rows, 0)
    place(keep_ref, send_ref, 0, pl.program_id(0) & 1, owner() & 1, mm(turned_ref[...], du_ref[...]).astype(BF))


def mlp_out(hn, dm, z, slope, ups, down_all, chunk, owner):
    tokens, width = hn.shape
    blocks, _, hidden = down_all.shape
    shapes = [
        jax.ShapeDtypeStruct((tokens, width), F32),
        jax.ShapeDtypeStruct((tokens, width), F32),
        jax.ShapeDtypeStruct((blocks // 2, width, hidden), BF),
        jax.ShapeDtypeStruct((blocks // 2, width, hidden), BF),
        jax.ShapeDtypeStruct((blocks, 1, hidden), F32),
    ]
    by_pair = pl.BlockSpec((1, width, hidden), lambda i: (i // 2, 0, 0))
    return pl.pallas_call(
        functools.partial(mlp_out_kernel, chunk, owner),
        grid=(blocks,),
        in_specs=[fixed(hn.shape), fixed(dm.shape)] + [per_step(v.shape) for v in (z, slope, down_all)] + [fixed(v.shape) for v in ups],
        out_specs=[fixed(s.shape) for s in shapes[:2]] + [by_pair, by_pair, per_step(shapes[4].shape)],
        out_shape=shapes,
        scratch_shapes=[
            pltpu.VMEM((tokens, hidden), BF),
            pltpu.VMEM((width, tokens), BF),
            pltpu.VMEM((width, hidden), BF),
        ],
        compiler_params=params(),
        name="mlp_out",
    )(hn, dm, z, slope, down_all, *ups)


def middle_kernel(
    x_ref, gy_ref, attn_ref, m_ref, dhn_ref, wproj_ref, vec_ref, out_ref, dmid_ref, dat_ref, do_ref, gvec_ref
):
    @pl.when(pl.program_id(0) == 0)
    def _():
        gvec_ref[...] = jnp.zeros_like(gvec_ref)

    attn = attn_ref[0]
    middle = x_ref[0].astype(F32) + vec_ref[8:9, :] * attn
    branch = m_ref[0] + vec_ref[3:4, :]
    out_ref[0] = (middle + vec_ref[9:10, :] * branch).astype(BF)
    cotangent = gy_ref[0].astype(F32)
    normed, factor = normalized(middle)
    dhn = dhn_ref[0]
    dmid = cotangent + layer_back(dhn, normed, factor, vec_ref[6:7, :])
    dmid_ref[0] = dmid
    dat = (vec_ref[8:9, :] * dmid).astype(BF)
    dat_ref[0] = dat
    down_in = (vec_ref[9:10, :] * cotangent).astype(BF)
    for row, value in enumerate(
        (dat.astype(F32), down_in.astype(F32), dhn * normed, dhn, dmid * attn, cotangent * branch)
    ):
        gvec_ref[row : row + 1, :] += jnp.sum(value, 0, keepdims=True)
    do_ref[0] = mm_nt(dat, wproj_ref[...]).astype(BF)


def middle_back(x, gy, attn, m, dhn, proj_weight, vectors):
    images, seq, width = x.shape
    shapes = [
        jax.ShapeDtypeStruct((images, seq, width), BF),
        jax.ShapeDtypeStruct((images, seq, width), F32),
        jax.ShapeDtypeStruct((images, seq, width), BF),
        jax.ShapeDtypeStruct((images, seq, width), BF),
        jax.ShapeDtypeStruct((8, width), F32),
    ]
    return pl.pallas_call(
        middle_kernel,
        grid=(images,),
        in_specs=[per_step(v.shape) for v in (x, gy, attn, m, dhn)] + [fixed(proj_weight.shape), fixed(vectors.shape)],
        out_specs=[per_step(s.shape) for s in shapes[:4]] + [fixed(shapes[4].shape)],
        out_shape=shapes,
        compiler_params=params(),
        name="middle_back",
    )(x, gy, attn, m, dhn, proj_weight, vectors)


def back_kernel(heads, qkv_ref, do_ref, p_ref, dqkv_ref, ds_ref, gcol_ref):
    width = do_ref.shape[2]
    head_dim = width // heads
    scale = head_dim ** (-0.5)

    @pl.when(pl.program_id(0) == 0)
    def _():
        ds_ref[...] = jnp.zeros_like(ds_ref)
        gcol_ref[...] = jnp.zeros_like(gcol_ref)

    pair = LANES
    masks = head_masks(pair, head_dim)
    per = pair // head_dim

    def one_pair(g, carry):
        at = pl.multiple_of(g * pair, pair)
        q = qkv_ref[0, :, pl.ds(at, pair)]
        k = qkv_ref[0, :, pl.ds(at + width, pair)]
        v = qkv_ref[0, :, pl.ds(at + 2 * width, pair)]
        do = do_ref[0, :, pl.ds(at, pair)]
        dq = dk = dv = None
        for e in range(per):
            pick = jnp.where(masks[e], scale, 0.0).astype(BF)
            keep = jnp.where(masks[e], 1.0, 0.0).astype(BF)
            qm, km, dom = q * pick, k * pick, do * keep
            rounded = p_ref[0, g * per + e]
            p = rounded.astype(F32)
            dv_e = mm_tn(rounded, dom)
            dp = mm_nt(dom, v)
            ds = (p * (dp - jnp.sum(dp * p, -1, keepdims=True))).astype(BF)
            ds_ref[g * per + e] += ds.astype(F32)
            dk_e = mm_tn(ds, qm)
            dq_e = mm(ds, km)
            dq = dq_e if dq is None else dq + dq_e
            dk = dk_e if dk is None else dk + dk_e
            dv = dv_e if dv is None else dv + dv_e
        for part, value in ((0, dq), (1, dk), (2, dv)):
            rounded = value.astype(BF)
            dqkv_ref[0, :, pl.ds(at + part * width, pair)] = rounded
            gcol_ref[:, pl.ds(at + part * width, pair)] += jnp.sum(rounded.astype(F32), 0, keepdims=True)
        return carry

    lax.fori_loop(0, width // pair, one_pair, 0, unroll=UNROLL_B)


def back(qkv, do, p, heads):
    images, seq, width = do.shape
    shapes = [
        jax.ShapeDtypeStruct((images, seq, 3 * width), BF),
        jax.ShapeDtypeStruct((heads, seq, seq), F32),
        jax.ShapeDtypeStruct((1, 3 * width), F32),
    ]
    return pl.pallas_call(
        functools.partial(back_kernel, heads),
        grid=(images,),
        in_specs=[per_step(v.shape) for v in (qkv, do, p)],
        out_specs=[per_step(shapes[0].shape)] + [fixed(s.shape) for s in shapes[1:]],
        out_shape=shapes,
        compiler_params=params(),
        name="back",
    )(qkv, do, p)


def grads_kernel(blocks, owner, a_ref, dqkv_ref, o_ref, dat_ref, keep_ref, send_ref, turned_a, turned_o):
    wide_cols, thin_cols = dqkv_ref.shape[1] // blocks, dat_ref.shape[1] // blocks
    turned_a[...] = a_ref[...].T
    turned_o[...] = o_ref[...].T
    here = owner() & 1
    for n in range(blocks):
        left = mm(turned_a[...], dqkv_ref[:, n * wide_cols : (n + 1) * wide_cols]).astype(BF)
        right = mm(turned_o[...], dat_ref[:, n * thin_cols : (n + 1) * thin_cols]).astype(BF)
        place(keep_ref, send_ref, n // 2, n & 1, here, jnp.concatenate([left, right], 1))


def attention_grads(first, dqkv, mixed, dat, blocks, owner):
    width = first.shape[1]
    cols = (dqkv.shape[1] + dat.shape[1]) // blocks
    shape = (blocks // 2, width, cols)
    return pl.pallas_call(
        functools.partial(grads_kernel, blocks, owner),
        grid=(1,),
        in_specs=[whole(v.shape) for v in (first, dqkv, mixed, dat)],
        out_specs=[whole(shape)] * 2,
        out_shape=[jax.ShapeDtypeStruct(shape, BF)] * 2,
        scratch_shapes=[pltpu.VMEM((width, first.shape[0]), BF)] * 2,
        compiler_params=params(),
        name="attention_grads",
    )(first, dqkv, mixed, dat)


def input_kernel(x_ref, dqkv_ref, dmid_ref, wqkv_ref, vec_ref, out_ref, gvec_ref):
    @pl.when(pl.program_id(0) == 0)
    def _():
        gvec_ref[...] = jnp.zeros_like(gvec_ref)

    da = mm_nt(dqkv_ref[0], wqkv_ref[...])
    normed, factor = normalized(x_ref[0].astype(F32))
    gvec_ref[0:1, :] += jnp.sum(da * normed, 0, keepdims=True)
    gvec_ref[1:2, :] += jnp.sum(da, 0, keepdims=True)
    out_ref[0] = dmid_ref[0] + layer_back(da, normed, factor, vec_ref[4:5, :])


def input_grads(x, dqkv, dmid, qkv_weight, vectors):
    images, seq, width = x.shape
    shapes = [
        jax.ShapeDtypeStruct((images, seq, width), F32),
        jax.ShapeDtypeStruct((8, width), F32),
    ]
    return pl.pallas_call(
        input_kernel,
        grid=(images,),
        in_specs=[per_step(v.shape) for v in (x, dqkv, dmid)]
        + [fixed(qkv_weight.shape), fixed(vectors.shape)],
        out_specs=[per_step(shapes[0].shape), fixed(shapes[1].shape)],
        out_shape=shapes,
        compiler_params=params(),
        name="input_grads",
    )(x, dqkv, dmid, qkv_weight, vectors)


def adam_update(master, mean, square, grad, rate, decay):
    mean_new = beta_one * mean + (1.0 - beta_one) * grad
    square_new = beta_two * square + (1.0 - beta_two) * grad * grad
    fix_one = 1.0 - beta_one**STEP
    fix_two = 1.0 - beta_two**STEP
    direction = mean_new / fix_one / (jnp.sqrt(square_new / fix_two) + adam_eps)
    return (mean_new, square_new, master - rate * (direction + decay * master))


def adam_kernel(rows, ours_ref, theirs_ref, attn_ref, up_ref, down_ref, *refs):
    state, results = refs[:21], refs[21:]
    sums = ours_ref[...] + theirs_ref[...]
    heads, vec_at, bias_at, square_at = rows
    row = lax.broadcasted_iota(jnp.int32, sums.shape, 0)
    small = jnp.where(row < square_at, sums, 0.0)
    total = jnp.sum(
        jnp.sum(small * small, 0, keepdims=True) + sums[square_at : square_at + 1], 1, keepdims=True
    )
    norm = jnp.sqrt(total)
    results[0][...] = norm
    clip = jnp.minimum(1.0, max_norm / (norm + clip_eps))
    split = state[0].shape[1]
    vec_rows, table_rows = state[12].shape[0], state[18].shape[1]
    bias = jnp.concatenate([sums[r : r + 1] for r in range(bias_at, square_at)], 1)
    grads = (
        attn_ref[:, :split],
        attn_ref[:, split:],
        up_ref[...],
        down_ref[...].astype(F32),
        sums[vec_at : vec_at + vec_rows],
        bias,
        sums[:heads, :table_rows],
    )
    at = 1
    for n, grad in enumerate(grads):
        large = n < 4
        mean_new, square_new, master_new = adam_update(
            *(state[3 * n + k][...] for k in range(3)),
            clip * grad,
            rate_matrix if large else rate_small,
            weight_decay if large else 0.0,
        )
        values = [mean_new, square_new, master_new]
        if large:
            values.append(master_new.astype(BF))
        for value in values:
            results[at][...] = value
            at += 1


def adam(rows, ours, theirs, shards, state):
    shapes = [jax.ShapeDtypeStruct((1, 1), F32)]
    for n in range(7):
        shapes += [jax.ShapeDtypeStruct(state[3 * n].shape, F32)] * 3
        if n < 4:
            shapes.append(jax.ShapeDtypeStruct(state[3 * n].shape, BF))
    inputs = [ours, theirs, *shards, *state]
    return pl.pallas_call(
        functools.partial(adam_kernel, rows),
        grid=(1,),
        in_specs=[whole(v.shape) for v in inputs],
        out_specs=[whole(v.shape) for v in shapes],
        out_shape=shapes,
        compiler_params=params(),
        name="adam",
    )(*inputs)


def axis_bits():
    found = []
    for axis in ("narrow", "wide"):
        count = lax.axis_size(axis).bit_length() - 1
        found += [(axis, count - 1 - at) for at in range(count)]
    return found


def swap(value, axis, bit):
    size = lax.axis_size(axis)
    return lax.ppermute(value, axis, [(i, i ^ (1 << bit)) for i in range(size)])


def split_kernel(mine, keep_ref, come_ref, keep_a, send_a, keep_b, send_b):
    half = keep_ref.shape[4] // 2
    for out_a, out_b, flip in ((keep_a, keep_b, 0), (send_a, send_b, 1)):
        side_a, side_b = mine[0]() ^ flip, mine[1]() ^ flip
        for n in range(2):
            for out, at, cols in (
                (out_a.at[0, n], (side_a, 0, n), slice(0, half)),
                (out_b.at[n, 0], (n, 0, side_b), slice(half, 2 * half)),
            ):
                total = keep_ref[(*at, slice(None), cols)].astype(F32) + come_ref[(*at, slice(None), cols)].astype(F32)
                out[...] = total.astype(BF)


def split_step(keep, come, mine):
    _, middle, _, rows, cols = keep.shape
    side = cols // 2
    block = pl.BlockSpec((2, 1, 2, rows, cols), lambda i: (0, i, 0, 0, 0))
    out_a = pl.BlockSpec((1, 2, rows, side), lambda i: (i, 0, 0, 0))
    out_b = pl.BlockSpec((2, 1, rows, side), lambda i: (0, i, 0, 0))
    shape_a = jax.ShapeDtypeStruct((middle, 2, rows, side), BF)
    shape_b = jax.ShapeDtypeStruct((2, middle, rows, side), BF)
    return pl.pallas_call(
        functools.partial(split_kernel, mine),
        grid=(middle,),
        in_specs=[block, block],
        out_specs=[out_a, out_a, out_b, out_b],
        out_shape=[shape_a, shape_a, shape_b, shape_b],
        compiler_params=params(),
        name="split_step",
    )(keep, come)


def halve_kernel(mine, places, join, *refs):
    parts = len(places)
    ins, outs = refs[: 2 * parts], refs[2 * parts :]
    for n in range(parts):
        keep_ref, come_ref = ins[2 * n : 2 * n + 2]
        count, _, cols = keep_ref.shape
        left = cols * n if join else 0
        outputs = outs[:2] if join else outs[2 * n : 2 * n + 2]
        low = places[n]

        def one(c, carry):
            for out, side in zip(outputs, (mine[n](), 1 - mine[n]())):
                at = ((c >> low) << (low + 1)) | (side << low) | (c & ((1 << low) - 1))
                total = keep_ref[at].astype(F32) + come_ref[at].astype(F32)
                out[c, :, left : left + cols] = total.astype(BF)
            return carry

        lax.fori_loop(0, count // 2, one, 0)


def halve_step(parts, places, mine, join):
    inputs = [v for pair in parts for v in pair]
    shapes = []
    for keep, _ in parts[:1] if join else parts:
        count, rows, cols = keep.shape
        shapes += [jax.ShapeDtypeStruct((count // 2, rows, cols * len(parts) if join else cols), BF)] * 2
    return pl.pallas_call(
        functools.partial(halve_kernel, mine, places, join),
        grid=(1,),
        in_specs=[whole(v.shape) for v in inputs],
        out_specs=[whole(v.shape) for v in shapes],
        out_shape=shapes,
        compiler_params=params(),
        name="halve_step",
    )(*inputs)


class Spread:
    def __init__(self, block):
        rows = block.shape[0] // 2
        self.block = block
        self.side = lax.axis_index("wide") & 1
        self.half = swap(lax.dynamic_slice_in_dim(block, self.side * rows, rows, 0), "narrow", 1)
        self.other = swap(block, "narrow", 0)

    def over_x(self, *after):
        self.half = gated(self.half, *after)
        self.rest = swap(self.half, "wide", 0)
        return self.half

    def blocks(self, *after):
        half, rest = self.half, gated(self.rest, *after)
        far = jnp.where(self.side == 0, jnp.concatenate([half, rest]), jnp.concatenate([rest, half]))
        return self.block, self.other, far, swap(far, "narrow", 0)


class Halving:
    def __init__(self, keep, send, rows):
        self.bits = axis_bits()
        cores = [d for d, (axis, _) in enumerate(self.bits) if axis == "narrow"]
        self.dims = [[d for d in range(len(self.bits)) if d != cores[-1]]]
        first, last = self.dims[0][0], self.dims[0][-1]
        self.steps = [(first, last), (last, first)] + [(d,) for d in self.dims[0][-2:0:-1]]
        shape = (-1, rows, keep.shape[-1])
        self.keep = [keep.reshape(shape)]
        self.sent = (send.reshape(shape),)
        self.come = [swap(self.sent[0], *self.bits[cores[-1]])]

    def mine(self, dim):
        axis, bit = self.bits[dim]
        return lambda: (lax.axis_index(axis) >> bit) & 1

    def send(self, *after):
        target = self.steps.pop(0)
        come = lax.optimization_barrier((*self.come, *after)) if after else self.come
        parts = len(self.keep)
        if len(target) > parts:
            rows, cols = self.keep[0].shape[1:]
            shape = (2, -1, 2, rows, cols)
            made = split_step(self.keep[0].reshape(shape), come[0].reshape(shape), [self.mine(d) for d in target])
            made = [v.reshape(-1, rows, cols // 2) for v in made]
            self.dims = self.dims * 2
        else:
            dims = target * (parts // len(target))
            places = [len(own) - 1 - own.index(d) for own, d in zip(self.dims, dims)]
            made = halve_step(
                list(zip(self.keep, come)), places, [self.mine(d) for d in dims], len(target) < parts
            )
        self.keep, self.sent = made[::2], tuple(made[1::2])
        self.dims = [[d for d in own if d != gone] for own, gone in zip(self.dims, target)]
        self.come = [swap(v, *self.bits[d]) for v, d in zip(self.sent, target)]
        return self.sent

    def last_pair(self):
        while self.steps:
            self.send()
        return self.keep[0][0], self.come[0][0]


def finish_kernel(rows, up_a, up_b, attn_a, attn_b, down_ref, table_ref, cols_ref, gvec_ref, gone_ref, gb_ref, up_ref, attn_ref, ours_ref):
    _, vec_at, bias_at, square_at = rows
    width = ours_ref.shape[1]
    up = up_a[...].astype(F32) + up_b[...].astype(F32)
    attn = attn_a[...].astype(F32) + attn_b[...].astype(F32)
    down = down_ref[...].astype(F32)
    up_ref[...] = up
    attn_ref[...] = attn
    squares = jnp.sum(up * up + attn * attn + down * down, 0, keepdims=True)
    ours_ref[...] = jnp.zeros_like(ours_ref)
    for c in range(table_ref.shape[0]):
        ours_ref[:vec_at, c * LANES : (c + 1) * LANES] = table_ref[c, 0] + table_ref[c, 1]
    ours_ref[vec_at : vec_at + 1, :] = cols_ref[:, :width]
    ours_ref[vec_at + 1 : vec_at + 2, :] = cols_ref[:, 2 * width :]
    for to, source, at in ((2, gvec_ref, 0), (3, gvec_ref, 1), (4, gone_ref, 0), (5, gone_ref, 1)) + tuple(
        (6 + n, gvec_ref, 2 + n) for n in range(4)
    ):
        ours_ref[vec_at + to : vec_at + to + 1, :] = source[at : at + 1, :]
    for n in range(square_at - bias_at):
        ours_ref[bias_at + n : bias_at + n + 1, :] = gb_ref[n]
    ours_ref[square_at : square_at + 1, :] = squares


def finish(rows, up, attn, down, small):
    inputs = [*up, *attn, down, *small]
    width = down.shape[1]
    shapes = [jax.ShapeDtypeStruct(v.shape, F32) for v in (up[0], attn[0])]
    shapes.append(jax.ShapeDtypeStruct((-(-(rows[3] + 1) // 8) * 8, width), F32))
    return pl.pallas_call(
        functools.partial(finish_kernel, rows),
        grid=(1,),
        in_specs=[whole(v.shape) for v in inputs],
        out_specs=[whole(v.shape) for v in shapes],
        out_shape=shapes,
        compiler_params=params(),
        name="finish",
    )(*inputs)


def gated(value, *waits):
    return lax.optimization_barrier((value,) + waits)[0] if waits else value


class Plan:
    def __init__(self, rows, up_weight, down_weight):
        self.rows, self.down_weight = rows, down_weight
        self.spread = Spread(up_weight)

    def after_bias(self, bias):
        half = self.spread.over_x(bias)
        self.down_all = lax.all_gather(gated(self.down_weight, half), "narrow", axis=0)
        return (half,)

    def after_front(self, hn):
        return self.spread.blocks(hn), self.down_all

    @staticmethod
    def owner():
        return lax.axis_index("narrow")

    def after_down(self, grads):
        rows = grads.reshape(-1, grads.shape[2])
        self.down = lax.psum_scatter(rows, ("narrow", "wide"), scatter_dimension=0, tiled=True)

    def after_up(self, keep, send):
        self.up = Halving(keep, send, self.rows)
        return self.up.sent

    def next_up(self, *after):
        return self.up.send(*after)

    def after_attention(self, keep, send):
        self.attn = Halving(keep, send, self.rows)
        return self.attn.sent

    def next_attention(self, *after):
        return self.attn.send(*after)

    def next_both(self, *after):
        self.up.send(*after)
        self.attn.send(*after)


class Alone:
    def __init__(self, *weights):
        self.weights = weights

    def after_bias(self, bias):
        return ()

    def after_front(self, hn):
        return self.weights

    @staticmethod
    def owner():
        return 0

    def after_down(self, grads):
        self.down = grads

    def after_up(self, *grads):
        self.up = grads
        return ()

    def after_attention(self, *grads):
        self.attn = grads
        return ()

    def next_up(self, *after):
        return ()

    next_attention = next_both = next_up


def local_work(
    block_in, out_grad, mim_mask, rel_index, qkv_weight, proj_weight, vectors, up_bias, rel_table, plan
):
    images, seq, width = block_in.shape
    table_rows, heads = rel_table.shape
    tokens = images * seq
    chunks = -(-table_rows // LANES)
    padded_seq = -(-seq // LANES) * LANES
    key_at = jnp.arange(seq, dtype=jnp.int32)
    index = jnp.where(key_at[None, :] < VALID, rel_index, chunks * LANES)
    padded = jnp.pad(index, ((0, 0), (0, padded_seq - seq)))
    table_t = jnp.pad(rel_table, ((0, chunks * LANES - table_rows), (0, 0))).T.reshape(heads, chunks, LANES)
    bias = bias_tables(padded, table_t)
    gy = out_grad * mim_mask.astype(BF)[:, :, None]
    first, qkv, p, mixed, attn, hn = front(gated(block_in, gy, *plan.after_bias(bias)), qkv_weight, proj_weight, vectors, bias, heads)
    flat = lambda v: v.reshape(tokens, v.shape[-1])
    ups, down_all = plan.after_front(hn)
    blocks, _, hidden = down_all.shape
    z, slope, grad_down, dm = mlp_in(flat(hn), flat(gy), vectors, up_bias.reshape(blocks, 1, hidden), ups, tokens, plan.owner)
    plan.after_down(grad_down)
    m, dhn, keep, send, grad_bias = mlp_out(flat(hn), dm, z, slope, ups, down_all, tokens, plan.owner)
    gy = gated(gy, *plan.after_up(keep, send))
    fold = lambda v: v.reshape(images, seq, width)
    block_out, dmid, dat, do, gvec = middle_back(block_in, gy, attn, fold(m), fold(dhn), proj_weight, vectors)
    do = gated(do, *plan.next_up(do))
    dqkv, ds, gcol = back(qkv, do, p, heads)
    dat = gated(dat, *plan.next_up(dqkv))
    keep, send = attention_grads(flat(first), flat(dqkv), flat(mixed), flat(dat), blocks, plan.owner)
    dmid = gated(dmid, *plan.after_attention(keep, send))
    input_grad, gvec_one = input_grads(block_in, dqkv, dmid, qkv_weight, vectors)
    by_query = jnp.pad(ds.transpose(1, 0, 2), ((0, 0), (0, (-heads) % 8), (0, 0)))
    by_query = gated(by_query, *plan.next_attention(input_grad))
    sums = table_sums(index, by_query, chunks)
    plan.next_both(sums)
    small = (sums.reshape(chunks, 2, -1, LANES), gcol, gvec, gvec_one, grad_bias)
    return block_out, input_grad, small, plan


def shards(
    block_in,
    out_grad,
    mim_mask,
    rel_index,
    qkv_weight,
    proj_weight,
    up_weight,
    down_weight,
    vectors,
    up_bias,
    rel_table,
    *state,
):
    width = block_in.shape[2]
    heads = rel_table.shape[1]
    plan = Plan(width // lax.axis_size("wide"), up_weight, down_weight)
    block_out, input_grad, small, plan = local_work(
        block_in, out_grad, mim_mask, rel_index, qkv_weight, proj_weight, vectors, up_bias, rel_table, plan
    )
    vec_at = heads + (-heads) % 8
    bias_at = vec_at + vectors.shape[0]
    rows = (heads, vec_at, bias_at, bias_at + up_bias.shape[0] // width)
    down_shard = plan.down
    up_shard, attn_shard, ours = finish(rows, plan.up.last_pair(), plan.attn.last_pair(), down_shard, small)
    theirs = None
    for axis, bit in reversed(axis_bits()):
        ours = ours if theirs is None else ours + theirs
        theirs = swap(ours, axis, bit)
    line = lambda v: v.reshape(1, -1)
    matrices = state[:12]
    params_small = (vectors, state[12], state[13], line(up_bias), line(state[14]), line(state[15]), rel_table.T, *(v.T for v in state[16:]))
    norm, *updated = adam(
        rows,
        ours,
        theirs,
        (attn_shard, up_shard, down_shard),
        [matrices[3 * n + k] for n in range(4) for k in range(3)] + [params_small[3 * n + k] for n in range(3) for k in range(3)],
    )
    for n in range(19, 22):
        updated[n] = updated[n].reshape(up_bias.shape)
        updated[n + 3] = updated[n + 3].T
    return (block_out, input_grad, norm.reshape(()), *updated)


def solution(mesh):
    token = P(("wide", "narrow"), None, None)
    whole_spec = P()
    shard = P("wide", "narrow")
    in_specs = (
        (token, token, P(("wide", "narrow"), None))
        + (whole_spec,) * 3
        + (P(None, "narrow"),) * 2
        + (whole_spec,) * 3
        + (shard,) * 12
        + (whole_spec,) * 6
    )
    out_specs = (token, token, whole_spec) + (shard,) * 16 + (whole_spec,) * 9
    return jax.shard_map(shards, mesh=mesh, in_specs=in_specs, out_specs=out_specs, check_vma=False)
```

```python
import functools

import jax
import jax.numpy as jnp
from jax import lax
from jax.experimental import pallas as pl
from jax.experimental.pallas import tpu as pltpu
from jax.sharding import PartitionSpec as P

VALID = 197
STEP = 10
LANES = 128

norm_eps = 1e-06
clip_eps = 1e-06
max_norm = 1.0
beta_one = 0.9
beta_two = 0.999
adam_eps = 1e-08
rate_matrix = 0.05
rate_small = 0.4
weight_decay = 0.05
BF = jnp.bfloat16
F32 = jnp.float32
ROWS_ROWS = (((0,), (0,)), ((), ()))
COLS_COLS = (((1,), (1,)), ((), ()))
VMEM_LIMIT = 60000 * 1024
VMEM_WHOLE = 65536 * 1024
UNROLL_F = 3
PART = 256
UNROLL_B = 3
UNROLL_T = 8


def mm(a, b):
    return jnp.dot(a, b, preferred_element_type=F32)


def mm_nt(a, b):
    return lax.dot_general(a, b, COLS_COLS, preferred_element_type=F32)


def mm_tn(a, b):
    return lax.dot_general(a, b, ROWS_ROWS, preferred_element_type=F32)


def params(steps=1, limit=VMEM_LIMIT):
    return pltpu.CompilerParams(
        dimension_semantics=("arbitrary",) * steps, vmem_limit_bytes=limit
    )


def whole(shape):
    zeros = (0,) * len(shape)
    return pl.BlockSpec(shape, lambda i: zeros)


def fixed(shape):
    zeros = (0,) * len(shape)
    return pl.BlockSpec(shape, lambda i: zeros, pipeline_mode=pl.Buffered(1))


def per_step(shape):
    rest = (0,) * (len(shape) - 1)
    return pl.BlockSpec((1,) + tuple(shape[1:]), lambda i: (i,) + rest)


def normalized(values):
    center = values - jnp.mean(values, -1, keepdims=True)
    factor = lax.rsqrt(jnp.mean(center * center, -1, keepdims=True) + norm_eps)
    return center * factor, factor


def layer_back(grad, normed, factor, gain_vec):
    scaled = grad * gain_vec
    return factor * (
        scaled
        - jnp.mean(scaled, -1, keepdims=True)
        - normed * jnp.mean(scaled * normed, -1, keepdims=True)
    )


def head_masks(pair_width, head_dim):
    lane = lax.broadcasted_iota(jnp.int32, (1, pair_width), 1)
    return [
        ((lane >= e * head_dim) & (lane < (e + 1) * head_dim)) for e in range(pair_width // head_dim)
    ]


def bias_kernel(idx_ref, tab_ref, out_ref):
    heads, seq = out_ref.shape[0], out_ref.shape[1]
    chunks = tab_ref.shape[1]

    def rows(step, carry):
        at = pl.multiple_of(step * 8, 8)
        for left in range(0, seq, LANES):
            index = idx_ref[pl.ds(at, 8), left : left + LANES]
            low, high = index & (LANES - 1), index >> 7
            match = [high == c for c in range(chunks)]
            width = min(LANES, seq - left)
            for h in range(heads):
                found = jnp.full((8, LANES), -1e30, F32)
                for c in range(chunks):
                    row = jnp.broadcast_to(tab_ref[h, c : c + 1, :], (8, LANES))
                    taken = jnp.take_along_axis(row, low, axis=1, mode="promise_in_bounds")
                    found = jnp.where(match[c], taken, found)
                out_ref[h, pl.ds(at, 8), left : left + width] = found[:, :width]
        return carry

    lax.fori_loop(0, seq // 8, rows, 0)


def bias_tables(index, table_rows):
    seq, _ = index.shape
    heads, _, _ = table_rows.shape
    shape = (heads, seq, seq)
    return pl.pallas_call(
        bias_kernel,
        grid=(1,),
        in_specs=[whole(index.shape), whole(table_rows.shape)],
        out_specs=whole(shape),
        out_shape=jax.ShapeDtypeStruct(shape, F32),
        compiler_params=params(),
        name="bias_tables",
    )(index, table_rows)


def table_kernel(idx_ref, ds_ref, out_ref):
    seq, heads, _ = ds_ref.shape
    chunks = out_ref.shape[0] // (2 * heads)
    out_ref[...] = jnp.zeros_like(out_ref)
    kinds = lax.broadcasted_iota(jnp.int32, (LANES, seq), 0)

    def one_query(j, total):
        index = idx_ref[pl.ds(j, 1), :]
        low, high = index & (LANES - 1), index >> 7
        onehot = jnp.where(jnp.broadcast_to(low, (LANES, seq)) == kinds, 1.0, 0.0).astype(BF)
        grads = ds_ref[j]
        top = grads.astype(BF).astype(F32)
        both = jnp.concatenate([top, grads - top], 0)
        high_all = jnp.broadcast_to(high, both.shape)
        parts = jnp.concatenate([jnp.where(high_all == c, both, 0.0) for c in range(chunks)], 0)
        return total + mm_nt(parts.astype(BF), onehot)

    out_ref[...] = lax.fori_loop(0, seq, one_query, jnp.zeros(out_ref.shape, F32), unroll=UNROLL_T)


def table_sums(index, grads, chunks):
    seq, heads, _ = grads.shape
    out = (chunks * 2 * heads, LANES)
    return pl.pallas_call(
        table_kernel,
        grid=(1,),
        in_specs=[whole(index.shape), whole(grads.shape)],
        out_specs=whole(out),
        out_shape=jax.ShapeDtypeStruct(out, F32),
        compiler_params=params(),
        name="table_sums",
    )(index, grads)


def front_kernel(heads, x_ref, wqkv_ref, wproj_ref, vec_ref, bias_ref, a_ref, qkv_ref, p_ref, o_ref, attn_ref, hn_ref):
    width = x_ref.shape[2]
    head_dim = width // heads
    scale = head_dim ** (-0.5)
    x = x_ref[0].astype(F32)
    normed, _ = normalized(x)
    first = (normed * vec_ref[4:5, :] + vec_ref[5:6, :]).astype(BF)
    a_ref[0] = first
    for part, row in ((0, 0), (1, None), (2, 1)):
        cols = slice(part * width, (part + 1) * width)
        value = mm(first, wqkv_ref[:, cols])
        if row is not None:
            value = value + vec_ref[row : row + 1, :]
        qkv_ref[0, :, cols] = value.astype(BF)
    pair = LANES
    masks = head_masks(pair, head_dim)
    per = pair // head_dim

    def one_pair(g, carry):
        at = pl.multiple_of(g * pair, pair)
        q = qkv_ref[0, :, pl.ds(at, pair)]
        k = qkv_ref[0, :, pl.ds(at + width, pair)]
        v = qkv_ref[0, :, pl.ds(at + 2 * width, pair)]
        out = None
        for e in range(per):
            qm = q * jnp.where(masks[e], scale, 0.0).astype(BF)
            s = mm_nt(qm, k) + bias_ref[g * per + e]
            p = jnp.exp(s - jnp.max(s, -1, keepdims=True))
            p = p * (1.0 / jnp.sum(p, -1, keepdims=True))
            p = p.astype(BF)
            p_ref[0, g * per + e] = p
            mixed = mm(p, v)
            out = mixed if out is None else jnp.where(masks[e], mixed, out)
        o_ref[0, :, pl.ds(at, pair)] = out.astype(BF)
        return carry

    lax.fori_loop(0, width // pair, one_pair, 0, unroll=UNROLL_F)
    attn = mm(o_ref[0], wproj_ref[...]) + vec_ref[2:3, :]
    attn_ref[0] = attn
    middle, _ = normalized(x + vec_ref[8:9, :] * attn)
    hn_ref[0] = (middle * vec_ref[6:7, :] + vec_ref[7:8, :]).astype(BF)


def front(x, qkv_weight, proj_weight, vectors, bias, heads):
    images, seq, width = x.shape
    shapes = [
        jax.ShapeDtypeStruct((images, seq, width), BF),
        jax.ShapeDtypeStruct((images, seq, 3 * width), BF),
        jax.ShapeDtypeStruct((images, heads, seq, seq), BF),
        jax.ShapeDtypeStruct((images, seq, width), BF),
        jax.ShapeDtypeStruct((images, seq, width), F32),
        jax.ShapeDtypeStruct((images, seq, width), BF),
    ]
    return pl.pallas_call(
        functools.partial(front_kernel, heads),
        grid=(images,),
        in_specs=[
            per_step(x.shape),
            fixed(qkv_weight.shape),
            fixed(proj_weight.shape),
            fixed(vectors.shape),
            fixed(bias.shape),
        ],
        out_specs=[per_step(s.shape) for s in shapes],
        out_shape=shapes,
        compiler_params=params(),
        name="front",
    )(x, qkv_weight, proj_weight, vectors, bias)


def pick(refs, at, out_ref):
    for n, ref in enumerate(refs):

        @pl.when(at == n)
        def _():
            out_ref[...] = ref[...]


def mlp_in_kernel(
    chunk, owner, hn_ref, gy_ref, vec_ref, bup_ref, up_a, up_b, up_c, up_d,
    z_ref, slope_ref, gdn_ref, dm_ref, turned_ref, wup_ref,
):
    tokens = hn_ref.shape[0]
    pick((up_a, up_b, up_c, up_d), pl.program_id(0) ^ owner(), wup_ref)

    @pl.when(pl.program_id(0) == 0)
    def _():
        def rows(step, carry):
            at = pl.ds(pl.multiple_of(step * chunk, chunk), chunk)
            dm_ref[at, :] = (vec_ref[9:10, :] * gy_ref[at, :].astype(F32)).astype(BF)
            return carry

        lax.fori_loop(0, tokens // chunk, rows, 0)
        turned_ref[...] = dm_ref[...].T

    for low in range(0, tokens, PART):
        at = slice(low, min(low + PART, tokens))
        u = mm(hn_ref[at, :], wup_ref[...]) + bup_ref[0]
        gate = 0.5 * (1.0 + lax.erf(u * 0.7071067811865476))
        z_ref[0, at, :] = (u * gate).astype(BF)
        slope_ref[0, at, :] = (gate + u * jnp.exp(-0.5 * u * u) * 0.3989422804014327).astype(BF)

    gdn_ref[0] = mm(turned_ref[...], z_ref[0]).astype(BF)


def mlp_in(hn, gy, vectors, up_bias, ups, chunk, owner):
    tokens, width = hn.shape
    blocks, hidden = len(ups), ups[0].shape[1]
    shapes = [
        jax.ShapeDtypeStruct((blocks, tokens, hidden), BF),
        jax.ShapeDtypeStruct((blocks, tokens, hidden), BF),
        jax.ShapeDtypeStruct((blocks, width, hidden), BF),
    ]
    return pl.pallas_call(
        functools.partial(mlp_in_kernel, chunk, owner),
        grid=(blocks,),
        in_specs=[
            fixed(hn.shape),
            fixed(gy.shape),
            fixed(vectors.shape),
            per_step(up_bias.shape),
            *(fixed(v.shape) for v in ups),
        ],
        out_specs=[per_step(s.shape) for s in shapes] + [fixed((tokens, width))],
        out_shape=shapes + [jax.ShapeDtypeStruct((tokens, width), BF)],
        scratch_shapes=[pltpu.VMEM((width, tokens), BF), pltpu.VMEM((width, hidden), BF)],
        compiler_params=params(limit=VMEM_WHOLE),
        name="mlp_in",
    )(hn, gy, vectors, up_bias, *ups)


def place(keep_ref, send_ref, at, core, mine, value):
    @pl.when(core == mine)
    def _():
        keep_ref[at] = value

    @pl.when(core != mine)
    def _():
        send_ref[at] = value


def mlp_out_kernel(
    chunk, owner, hn_ref, dm_ref, z_ref, slope_ref, wdn_ref, up_a, up_b, up_c, up_d,
    m_ref, dhn_ref, keep_ref, send_ref, gb_ref, du_ref, turned_ref, wup_ref,
):
    tokens = hn_ref.shape[0]
    pick((up_a, up_b, up_c, up_d), pl.program_id(0) ^ owner(), wup_ref)

    @pl.when(pl.program_id(0) == 0)
    def _():
        m_ref[...] = jnp.zeros_like(m_ref)
        dhn_ref[...] = jnp.zeros_like(dhn_ref)
        turned_ref[...] = hn_ref[...].T

    gb_ref[...] = jnp.zeros_like(gb_ref)

    def rows(step, carry):
        at = pl.ds(pl.multiple_of(step * chunk, chunk), chunk)
        m_ref[at, :] += mm_nt(z_ref[0, at, :], wdn_ref[0])
        du = (mm(dm_ref[at, :], wdn_ref[0]) * slope_ref[0, at, :].astype(F32)).astype(BF)
        du_ref[at, :] = du
        gb_ref[0] += jnp.sum(du.astype(F32), 0, keepdims=True)
        dhn_ref[at, :] += mm_nt(du, wup_ref[...])
        return carry

    lax.fori_loop(0, tokens // chunk, rows, 0)
    place(keep_ref, send_ref, 0, pl.program_id(0) & 1, owner() & 1, mm(turned_ref[...], du_ref[...]).astype(BF))


def mlp_out(hn, dm, z, slope, ups, down_all, chunk, owner):
    tokens, width = hn.shape
    blocks, _, hidden = down_all.shape
    shapes = [
        jax.ShapeDtypeStruct((tokens, width), F32),
        jax.ShapeDtypeStruct((tokens, width), F32),
        jax.ShapeDtypeStruct((blocks // 2, width, hidden), BF),
        jax.ShapeDtypeStruct((blocks // 2, width, hidden), BF),
        jax.ShapeDtypeStruct((blocks, 1, hidden), F32),
    ]
    by_pair = pl.BlockSpec((1, width, hidden), lambda i: (i // 2, 0, 0))
    return pl.pallas_call(
        functools.partial(mlp_out_kernel, chunk, owner),
        grid=(blocks,),
        in_specs=[fixed(hn.shape), fixed(dm.shape)] + [per_step(v.shape) for v in (z, slope, down_all)] + [fixed(v.shape) for v in ups],
        out_specs=[fixed(s.shape) for s in shapes[:2]] + [by_pair, by_pair, per_step(shapes[4].shape)],
        out_shape=shapes,
        scratch_shapes=[
            pltpu.VMEM((tokens, hidden), BF),
            pltpu.VMEM((width, tokens), BF),
            pltpu.VMEM((width, hidden), BF),
        ],
        compiler_params=params(),
        name="mlp_out",
    )(hn, dm, z, slope, down_all, *ups)


def middle_kernel(
    x_ref, gy_ref, attn_ref, m_ref, dhn_ref, wproj_ref, vec_ref, out_ref, dmid_ref, dat_ref, do_ref, gvec_ref
):
    @pl.when(pl.program_id(0) == 0)
    def _():
        gvec_ref[...] = jnp.zeros_like(gvec_ref)

    attn = attn_ref[0]
    middle = x_ref[0].astype(F32) + vec_ref[8:9, :] * attn
    branch = m_ref[0] + vec_ref[3:4, :]
    out_ref[0] = (middle + vec_ref[9:10, :] * branch).astype(BF)
    cotangent = gy_ref[0].astype(F32)
    normed, factor = normalized(middle)
    dhn = dhn_ref[0]
    dmid = cotangent + layer_back(dhn, normed, factor, vec_ref[6:7, :])
    dmid_ref[0] = dmid
    dat = (vec_ref[8:9, :] * dmid).astype(BF)
    dat_ref[0] = dat
    down_in = (vec_ref[9:10, :] * cotangent).astype(BF)
    for row, value in enumerate(
        (dat.astype(F32), down_in.astype(F32), dhn * normed, dhn, dmid * attn, cotangent * branch)
    ):
        gvec_ref[row : row + 1, :] += jnp.sum(value, 0, keepdims=True)
    do_ref[0] = mm_nt(dat, wproj_ref[...]).astype(BF)


def middle_back(x, gy, attn, m, dhn, proj_weight, vectors):
    images, seq, width = x.shape
    shapes = [
        jax.ShapeDtypeStruct((images, seq, width), BF),
        jax.ShapeDtypeStruct((images, seq, width), F32),
        jax.ShapeDtypeStruct((images, seq, width), BF),
        jax.ShapeDtypeStruct((images, seq, width), BF),
        jax.ShapeDtypeStruct((8, width), F32),
    ]
    return pl.pallas_call(
        middle_kernel,
        grid=(images,),
        in_specs=[per_step(v.shape) for v in (x, gy, attn, m, dhn)] + [fixed(proj_weight.shape), fixed(vectors.shape)],
        out_specs=[per_step(s.shape) for s in shapes[:4]] + [fixed(shapes[4].shape)],
        out_shape=shapes,
        compiler_params=params(),
        name="middle_back",
    )(x, gy, attn, m, dhn, proj_weight, vectors)


def back_kernel(heads, qkv_ref, do_ref, p_ref, dqkv_ref, ds_ref, gcol_ref):
    width = do_ref.shape[2]
    head_dim = width // heads
    scale = head_dim ** (-0.5)

    @pl.when(pl.program_id(0) == 0)
    def _():
        ds_ref[...] = jnp.zeros_like(ds_ref)
        gcol_ref[...] = jnp.zeros_like(gcol_ref)

    pair = LANES
    masks = head_masks(pair, head_dim)
    per = pair // head_dim

    def one_pair(g, carry):
        at = pl.multiple_of(g * pair, pair)
        q = qkv_ref[0, :, pl.ds(at, pair)]
        k = qkv_ref[0, :, pl.ds(at + width, pair)]
        v = qkv_ref[0, :, pl.ds(at + 2 * width, pair)]
        do = do_ref[0, :, pl.ds(at, pair)]
        dq = dk = dv = None
        for e in range(per):
            pick = jnp.where(masks[e], scale, 0.0).astype(BF)
            keep = jnp.where(masks[e], 1.0, 0.0).astype(BF)
            qm, km, dom = q * pick, k * pick, do * keep
            rounded = p_ref[0, g * per + e]
            p = rounded.astype(F32)
            dv_e = mm_tn(rounded, dom)
            dp = mm_nt(dom, v)
            ds = (p * (dp - jnp.sum(dp * p, -1, keepdims=True))).astype(BF)
            ds_ref[g * per + e] += ds.astype(F32)
            dk_e = mm_tn(ds, qm)
            dq_e = mm(ds, km)
            dq = dq_e if dq is None else dq + dq_e
            dk = dk_e if dk is None else dk + dk_e
            dv = dv_e if dv is None else dv + dv_e
        for part, value in ((0, dq), (1, dk), (2, dv)):
            rounded = value.astype(BF)
            dqkv_ref[0, :, pl.ds(at + part * width, pair)] = rounded
            gcol_ref[:, pl.ds(at + part * width, pair)] += jnp.sum(rounded.astype(F32), 0, keepdims=True)
        return carry

    lax.fori_loop(0, width // pair, one_pair, 0, unroll=UNROLL_B)


def back(qkv, do, p, heads):
    images, seq, width = do.shape
    shapes = [
        jax.ShapeDtypeStruct((images, seq, 3 * width), BF),
        jax.ShapeDtypeStruct((heads, seq, seq), F32),
        jax.ShapeDtypeStruct((1, 3 * width), F32),
    ]
    return pl.pallas_call(
        functools.partial(back_kernel, heads),
        grid=(images,),
        in_specs=[per_step(v.shape) for v in (qkv, do, p)],
        out_specs=[per_step(shapes[0].shape)] + [fixed(s.shape) for s in shapes[1:]],
        out_shape=shapes,
        compiler_params=params(),
        name="back",
    )(qkv, do, p)


def grads_kernel(blocks, owner, a_ref, dqkv_ref, o_ref, dat_ref, keep_ref, send_ref, turned_a, turned_o):
    wide_cols, thin_cols = dqkv_ref.shape[1] // blocks, dat_ref.shape[1] // blocks
    turned_a[...] = a_ref[...].T
    turned_o[...] = o_ref[...].T
    here = owner() & 1
    for n in range(blocks):
        left = mm(turned_a[...], dqkv_ref[:, n * wide_cols : (n + 1) * wide_cols]).astype(BF)
        right = mm(turned_o[...], dat_ref[:, n * thin_cols : (n + 1) * thin_cols]).astype(BF)
        place(keep_ref, send_ref, n // 2, n & 1, here, jnp.concatenate([left, right], 1))


def attention_grads(first, dqkv, mixed, dat, blocks, owner):
    width = first.shape[1]
    cols = (dqkv.shape[1] + dat.shape[1]) // blocks
    shape = (blocks // 2, width, cols)
    return pl.pallas_call(
        functools.partial(grads_kernel, blocks, owner),
        grid=(1,),
        in_specs=[whole(v.shape) for v in (first, dqkv, mixed, dat)],
        out_specs=[whole(shape)] * 2,
        out_shape=[jax.ShapeDtypeStruct(shape, BF)] * 2,
        scratch_shapes=[pltpu.VMEM((width, first.shape[0]), BF)] * 2,
        compiler_params=params(),
        name="attention_grads",
    )(first, dqkv, mixed, dat)


def input_kernel(x_ref, dqkv_ref, dmid_ref, wqkv_ref, vec_ref, out_ref, gvec_ref):
    @pl.when(pl.program_id(0) == 0)
    def _():
        gvec_ref[...] = jnp.zeros_like(gvec_ref)

    da = mm_nt(dqkv_ref[0], wqkv_ref[...])
    normed, factor = normalized(x_ref[0].astype(F32))
    gvec_ref[0:1, :] += jnp.sum(da * normed, 0, keepdims=True)
    gvec_ref[1:2, :] += jnp.sum(da, 0, keepdims=True)
    out_ref[0] = dmid_ref[0] + layer_back(da, normed, factor, vec_ref[4:5, :])


def input_grads(x, dqkv, dmid, qkv_weight, vectors):
    images, seq, width = x.shape
    shapes = [
        jax.ShapeDtypeStruct((images, seq, width), F32),
        jax.ShapeDtypeStruct((8, width), F32),
    ]
    return pl.pallas_call(
        input_kernel,
        grid=(images,),
        in_specs=[per_step(v.shape) for v in (x, dqkv, dmid)]
        + [fixed(qkv_weight.shape), fixed(vectors.shape)],
        out_specs=[per_step(shapes[0].shape), fixed(shapes[1].shape)],
        out_shape=shapes,
        compiler_params=params(),
        name="input_grads",
    )(x, dqkv, dmid, qkv_weight, vectors)


def adam_update(master, mean, square, grad, rate, decay):
    mean_new = beta_one * mean + (1.0 - beta_one) * grad
    square_new = beta_two * square + (1.0 - beta_two) * grad * grad
    fix_one = 1.0 - beta_one**STEP
    fix_two = 1.0 - beta_two**STEP
    direction = mean_new / fix_one / (jnp.sqrt(square_new / fix_two) + adam_eps)
    return (mean_new, square_new, master - rate * (direction + decay * master))


def adam_kernel(rows, ours_ref, theirs_ref, attn_ref, up_ref, down_ref, *refs):
    state, results = refs[:21], refs[21:]
    sums = ours_ref[...] + theirs_ref[...]
    heads, vec_at, bias_at, square_at = rows
    row = lax.broadcasted_iota(jnp.int32, sums.shape, 0)
    small = jnp.where(row < square_at, sums, 0.0)
    total = jnp.sum(
        jnp.sum(small * small, 0, keepdims=True) + sums[square_at : square_at + 1], 1, keepdims=True
    )
    norm = jnp.sqrt(total)
    results[0][...] = norm
    clip = jnp.minimum(1.0, max_norm / (norm + clip_eps))
    split = state[0].shape[1]
    vec_rows, table_rows = state[12].shape[0], state[18].shape[1]
    bias = jnp.concatenate([sums[r : r + 1] for r in range(bias_at, square_at)], 1)
    grads = (
        attn_ref[:, :split],
        attn_ref[:, split:],
        up_ref[...],
        down_ref[...].astype(F32),
        sums[vec_at : vec_at + vec_rows],
        bias,
        sums[:heads, :table_rows],
    )
    at = 1
    for n, grad in enumerate(grads):
        large = n < 4
        mean_new, square_new, master_new = adam_update(
            *(state[3 * n + k][...] for k in range(3)),
            clip * grad,
            rate_matrix if large else rate_small,
            weight_decay if large else 0.0,
        )
        values = [mean_new, square_new, master_new]
        if large:
            values.append(master_new.astype(BF))
        for value in values:
            results[at][...] = value
            at += 1


def adam(rows, ours, theirs, shards, state):
    shapes = [jax.ShapeDtypeStruct((1, 1), F32)]
    for n in range(7):
        shapes += [jax.ShapeDtypeStruct(state[3 * n].shape, F32)] * 3
        if n < 4:
            shapes.append(jax.ShapeDtypeStruct(state[3 * n].shape, BF))
    inputs = [ours, theirs, *shards, *state]
    return pl.pallas_call(
        functools.partial(adam_kernel, rows),
        grid=(1,),
        in_specs=[whole(v.shape) for v in inputs],
        out_specs=[whole(v.shape) for v in shapes],
        out_shape=shapes,
        compiler_params=params(limit=VMEM_WHOLE),
        name="adam",
    )(*inputs)


def axis_bits():
    found = []
    for axis in ("narrow", "wide"):
        count = lax.axis_size(axis).bit_length() - 1
        found += [(axis, count - 1 - at) for at in range(count)]
    return found


def swap(value, axis, bit):
    size = lax.axis_size(axis)
    return lax.ppermute(value, axis, [(i, i ^ (1 << bit)) for i in range(size)])


def split_kernel(mine, keep_ref, come_ref, keep_a, send_a, keep_b, send_b):
    half = keep_ref.shape[4] // 2
    for out_a, out_b, flip in ((keep_a, keep_b, 0), (send_a, send_b, 1)):
        side_a, side_b = mine[0]() ^ flip, mine[1]() ^ flip
        for n in range(2):
            for out, at, cols in (
                (out_a.at[0, n], (side_a, 0, n), slice(0, half)),
                (out_b.at[n, 0], (n, 0, side_b), slice(half, 2 * half)),
            ):
                total = keep_ref[(*at, slice(None), cols)].astype(F32) + come_ref[(*at, slice(None), cols)].astype(F32)
                out[...] = total.astype(BF)


def split_step(keep, come, mine):
    _, middle, _, rows, cols = keep.shape
    side = cols // 2
    block = pl.BlockSpec((2, 1, 2, rows, cols), lambda i: (0, i, 0, 0, 0))
    out_a = pl.BlockSpec((1, 2, rows, side), lambda i: (i, 0, 0, 0))
    out_b = pl.BlockSpec((2, 1, rows, side), lambda i: (0, i, 0, 0))
    shape_a = jax.ShapeDtypeStruct((middle, 2, rows, side), BF)
    shape_b = jax.ShapeDtypeStruct((2, middle, rows, side), BF)
    return pl.pallas_call(
        functools.partial(split_kernel, mine),
        grid=(middle,),
        in_specs=[block, block],
        out_specs=[out_a, out_a, out_b, out_b],
        out_shape=[shape_a, shape_a, shape_b, shape_b],
        compiler_params=params(limit=VMEM_WHOLE),
        name="split_step",
    )(keep, come)


def halve_kernel(mine, places, join, *refs):
    parts = len(places)
    ins, outs = refs[: 2 * parts], refs[2 * parts :]
    for n in range(parts):
        keep_ref, come_ref = ins[2 * n : 2 * n + 2]
        count, _, cols = keep_ref.shape
        left = cols * n if join else 0
        outputs = outs[:2] if join else outs[2 * n : 2 * n + 2]
        low = places[n]

        def one(c, carry):
            for out, side in zip(outputs, (mine[n](), 1 - mine[n]())):
                at = ((c >> low) << (low + 1)) | (side << low) | (c & ((1 << low) - 1))
                total = keep_ref[at].astype(F32) + come_ref[at].astype(F32)
                out[c, :, left : left + cols] = total.astype(BF)
            return carry

        lax.fori_loop(0, count // 2, one, 0)


def halve_step(parts, places, mine, join):
    inputs = [v for pair in parts for v in pair]
    shapes = []
    for keep, _ in parts[:1] if join else parts:
        count, rows, cols = keep.shape
        shapes += [jax.ShapeDtypeStruct((count // 2, rows, cols * len(parts) if join else cols), BF)] * 2
    return pl.pallas_call(
        functools.partial(halve_kernel, mine, places, join),
        grid=(1,),
        in_specs=[whole(v.shape) for v in inputs],
        out_specs=[whole(v.shape) for v in shapes],
        out_shape=shapes,
        compiler_params=params(limit=VMEM_WHOLE),
        name="halve_step",
    )(*inputs)


class Spread:
    def __init__(self, block):
        rows = block.shape[0] // 2
        self.block = block
        self.side = lax.axis_index("wide") & 1
        self.half = swap(lax.dynamic_slice_in_dim(block, self.side * rows, rows, 0), "narrow", 1)
        self.other = swap(block, "narrow", 0)

    def over_x(self, *after):
        self.half = gated(self.half, *after)
        self.rest = swap(self.half, "wide", 0)
        return self.half

    def blocks(self, *after):
        half, rest = self.half, gated(self.rest, *after)
        far = jnp.where(self.side == 0, jnp.concatenate([half, rest]), jnp.concatenate([rest, half]))
        return self.block, self.other, far, swap(far, "narrow", 0)


class Halving:
    def __init__(self, keep, send, rows):
        self.bits = axis_bits()
        cores = [d for d, (axis, _) in enumerate(self.bits) if axis == "narrow"]
        self.dims = [[d for d in range(len(self.bits)) if d != cores[-1]]]
        first, last = self.dims[0][0], self.dims[0][-1]
        self.steps = [(first, last), (last, first)] + [(d,) for d in self.dims[0][-2:0:-1]]
        shape = (-1, rows, keep.shape[-1])
        self.keep = [keep.reshape(shape)]
        self.sent = (send.reshape(shape),)
        self.come = [swap(self.sent[0], *self.bits[cores[-1]])]

    def mine(self, dim):
        axis, bit = self.bits[dim]
        return lambda: (lax.axis_index(axis) >> bit) & 1

    def send(self, *after):
        target = self.steps.pop(0)
        come = lax.optimization_barrier((*self.come, *after)) if after else self.come
        parts = len(self.keep)
        if len(target) > parts:
            rows, cols = self.keep[0].shape[1:]
            shape = (2, -1, 2, rows, cols)
            made = split_step(self.keep[0].reshape(shape), come[0].reshape(shape), [self.mine(d) for d in target])
            made = [v.reshape(-1, rows, cols // 2) for v in made]
            self.dims = self.dims * 2
        else:
            dims = target * (parts // len(target))
            places = [len(own) - 1 - own.index(d) for own, d in zip(self.dims, dims)]
            made = halve_step(
                list(zip(self.keep, come)), places, [self.mine(d) for d in dims], len(target) < parts
            )
        self.keep, self.sent = made[::2], tuple(made[1::2])
        self.dims = [[d for d in own if d != gone] for own, gone in zip(self.dims, target)]
        self.come = [swap(v, *self.bits[d]) for v, d in zip(self.sent, target)]
        return self.sent

    def last_pair(self):
        while self.steps:
            self.send()
        return self.keep[0][0], self.come[0][0]


def finish_kernel(rows, up_a, up_b, attn_a, attn_b, down_ref, table_ref, cols_ref, gvec_ref, gone_ref, gb_ref, up_ref, attn_ref, ours_ref):
    _, vec_at, bias_at, square_at = rows
    width = ours_ref.shape[1]
    up = up_a[...].astype(F32) + up_b[...].astype(F32)
    attn = attn_a[...].astype(F32) + attn_b[...].astype(F32)
    down = down_ref[...].astype(F32)
    up_ref[...] = up
    attn_ref[...] = attn
    squares = jnp.sum(up * up + attn * attn + down * down, 0, keepdims=True)
    ours_ref[...] = jnp.zeros_like(ours_ref)
    for c in range(table_ref.shape[0]):
        ours_ref[:vec_at, c * LANES : (c + 1) * LANES] = table_ref[c, 0] + table_ref[c, 1]
    ours_ref[vec_at : vec_at + 1, :] = cols_ref[:, :width]
    ours_ref[vec_at + 1 : vec_at + 2, :] = cols_ref[:, 2 * width :]
    for to, source, at in ((2, gvec_ref, 0), (3, gvec_ref, 1), (4, gone_ref, 0), (5, gone_ref, 1)) + tuple(
        (6 + n, gvec_ref, 2 + n) for n in range(4)
    ):
        ours_ref[vec_at + to : vec_at + to + 1, :] = source[at : at + 1, :]
    for n in range(square_at - bias_at):
        ours_ref[bias_at + n : bias_at + n + 1, :] = gb_ref[n]
    ours_ref[square_at : square_at + 1, :] = squares


def finish(rows, up, attn, down, small):
    inputs = [*up, *attn, down, *small]
    width = down.shape[1]
    shapes = [jax.ShapeDtypeStruct(v.shape, F32) for v in (up[0], attn[0])]
    shapes.append(jax.ShapeDtypeStruct((-(-(rows[3] + 1) // 8) * 8, width), F32))
    return pl.pallas_call(
        functools.partial(finish_kernel, rows),
        grid=(1,),
        in_specs=[whole(v.shape) for v in inputs],
        out_specs=[whole(v.shape) for v in shapes],
        out_shape=shapes,
        compiler_params=params(limit=VMEM_WHOLE),
        name="finish",
    )(*inputs)


def gated(value, *waits):
    return lax.optimization_barrier((value,) + waits)[0] if waits else value


class Plan:
    def __init__(self, rows, up_weight, down_weight):
        self.rows, self.down_weight = rows, down_weight
        self.spread = Spread(up_weight)

    def after_bias(self, bias):
        half = self.spread.over_x(bias)
        self.down_all = lax.all_gather(gated(self.down_weight, half), "narrow", axis=0)
        return (half,)

    def after_front(self, hn):
        return self.spread.blocks(hn), self.down_all

    @staticmethod
    def owner():
        return lax.axis_index("narrow")

    def after_down(self, grads):
        rows = grads.reshape(-1, grads.shape[2])
        self.down = lax.psum_scatter(rows, ("narrow", "wide"), scatter_dimension=0, tiled=True)

    def after_up(self, keep, send):
        self.up = Halving(keep, send, self.rows)
        return self.up.sent

    def next_up(self, *after):
        return self.up.send(*after)

    def after_attention(self, keep, send):
        self.attn = Halving(keep, send, self.rows)
        return self.attn.sent

    def next_attention(self, *after):
        return self.attn.send(*after)

    def next_both(self, *after):
        self.up.send(*after)
        self.attn.send(*after)


class Alone:
    def __init__(self, *weights):
        self.weights = weights

    def after_bias(self, bias):
        return ()

    def after_front(self, hn):
        return self.weights

    @staticmethod
    def owner():
        return 0

    def after_down(self, grads):
        self.down = grads

    def after_up(self, *grads):
        self.up = grads
        return ()

    def after_attention(self, *grads):
        self.attn = grads
        return ()

    def next_up(self, *after):
        return ()

    next_attention = next_both = next_up


def local_work(
    block_in, out_grad, mim_mask, rel_index, qkv_weight, proj_weight, vectors, up_bias, rel_table, plan
):
    images, seq, width = block_in.shape
    table_rows, heads = rel_table.shape
    tokens = images * seq
    chunks = -(-table_rows // LANES)
    padded_seq = -(-seq // LANES) * LANES
    key_at = jnp.arange(seq, dtype=jnp.int32)
    index = jnp.where(key_at[None, :] < VALID, rel_index, chunks * LANES)
    padded = jnp.pad(index, ((0, 0), (0, padded_seq - seq)))
    table_t = jnp.pad(rel_table, ((0, chunks * LANES - table_rows), (0, 0))).T.reshape(heads, chunks, LANES)
    bias = bias_tables(padded, table_t)
    gy = out_grad * mim_mask.astype(BF)[:, :, None]
    first, qkv, p, mixed, attn, hn = front(gated(block_in, *plan.after_bias(bias)), qkv_weight, proj_weight, vectors, bias, heads)
    flat = lambda v: v.reshape(tokens, v.shape[-1])
    ups, down_all = plan.after_front(hn)
    blocks, _, hidden = down_all.shape
    z, slope, grad_down, dm = mlp_in(flat(hn), flat(gy), vectors, up_bias.reshape(blocks, 1, hidden), ups, tokens, plan.owner)
    plan.after_down(grad_down)
    m, dhn, keep, send, grad_bias = mlp_out(flat(hn), dm, z, slope, ups, down_all, tokens, plan.owner)
    gy = gated(gy, *plan.after_up(keep, send))
    fold = lambda v: v.reshape(images, seq, width)
    block_out, dmid, dat, do, gvec = middle_back(block_in, gy, attn, fold(m), fold(dhn), proj_weight, vectors)
    do = gated(do, *plan.next_up(do))
    dqkv, ds, gcol = back(qkv, do, p, heads)
    dat = gated(dat, *plan.next_up(dqkv))
    keep, send = attention_grads(flat(first), flat(dqkv), flat(mixed), flat(dat), blocks, plan.owner)
    dmid = gated(dmid, *plan.after_attention(keep, send))
    input_grad, gvec_one = input_grads(block_in, dqkv, dmid, qkv_weight, vectors)
    by_query = jnp.pad(ds.transpose(1, 0, 2), ((0, 0), (0, (-heads) % 8), (0, 0)))
    by_query = gated(by_query, *plan.next_attention(input_grad))
    sums = table_sums(index, by_query, chunks)
    plan.next_both(sums)
    small = (sums.reshape(chunks, 2, -1, LANES), gcol, gvec, gvec_one, grad_bias)
    return block_out, input_grad, small, plan


def shards(
    block_in,
    out_grad,
    mim_mask,
    rel_index,
    qkv_weight,
    proj_weight,
    up_weight,
    down_weight,
    vectors,
    up_bias,
    rel_table,
    *state,
):
    width = block_in.shape[2]
    heads = rel_table.shape[1]
    plan = Plan(width // lax.axis_size("wide"), up_weight, down_weight)
    block_out, input_grad, small, plan = local_work(
        block_in, out_grad, mim_mask, rel_index, qkv_weight, proj_weight, vectors, up_bias, rel_table, plan
    )
    vec_at = heads + (-heads) % 8
    bias_at = vec_at + vectors.shape[0]
    rows = (heads, vec_at, bias_at, bias_at + up_bias.shape[0] // width)
    down_shard = plan.down
    up_shard, attn_shard, ours = finish(rows, plan.up.last_pair(), plan.attn.last_pair(), down_shard, small)
    theirs = None
    for axis, bit in reversed(axis_bits()):
        ours = ours if theirs is None else ours + theirs
        theirs = swap(ours, axis, bit)
    line = lambda v: v.reshape(1, -1)
    matrices = state[:12]
    params_small = (vectors, state[12], state[13], line(up_bias), line(state[14]), line(state[15]), rel_table.T, *(v.T for v in state[16:]))
    norm, *updated = adam(
        rows,
        ours,
        theirs,
        (attn_shard, up_shard, down_shard),
        [matrices[3 * n + k] for n in range(4) for k in range(3)] + [params_small[3 * n + k] for n in range(3) for k in range(3)],
    )
    for n in range(19, 22):
        updated[n] = updated[n].reshape(up_bias.shape)
        updated[n + 3] = updated[n + 3].T
    return (block_out, input_grad, norm.reshape(()), *updated)


def solution(mesh):
    token = P(("wide", "narrow"), None, None)
    whole_spec = P()
    shard = P("wide", "narrow")
    in_specs = (
        (token, token, P(("wide", "narrow"), None))
        + (whole_spec,) * 3
        + (P(None, "narrow"),) * 2
        + (whole_spec,) * 3
        + (shard,) * 12
        + (whole_spec,) * 6
    )
    out_specs = (token, token, whole_spec) + (shard,) * 16 + (whole_spec,) * 9
    return jax.shard_map(shards, mesh=mesh, in_specs=in_specs, out_specs=out_specs, check_vma=False)
```

```python
import functools

import jax
import jax.numpy as jnp
from jax import lax
from jax.experimental import pallas as pl
from jax.experimental.pallas import tpu as pltpu
from jax.sharding import PartitionSpec as P

VALID = 197
STEP = 10
LANES = 128

norm_eps = 1e-06
clip_eps = 1e-06
max_norm = 1.0
beta_one = 0.9
beta_two = 0.999
adam_eps = 1e-08
rate_matrix = 0.05
rate_small = 0.4
weight_decay = 0.05
BF = jnp.bfloat16
F32 = jnp.float32
ROWS_ROWS = (((0,), (0,)), ((), ()))
COLS_COLS = (((1,), (1,)), ((), ()))
VMEM_LIMIT = 60000 * 1024
VMEM_WHOLE = 65536 * 1024
UNROLL_F = 3
PART = 256
UNROLL_B = 3
UNROLL_T = 8


def mm(a, b):
    return jnp.dot(a, b, preferred_element_type=F32)


def mm_nt(a, b):
    return lax.dot_general(a, b, COLS_COLS, preferred_element_type=F32)


def mm_tn(a, b):
    return lax.dot_general(a, b, ROWS_ROWS, preferred_element_type=F32)


def params(steps=1, limit=VMEM_LIMIT):
    return pltpu.CompilerParams(
        dimension_semantics=("arbitrary",) * steps, vmem_limit_bytes=limit
    )


def whole(shape):
    zeros = (0,) * len(shape)
    return pl.BlockSpec(shape, lambda i: zeros)


def fixed(shape):
    zeros = (0,) * len(shape)
    return pl.BlockSpec(shape, lambda i: zeros, pipeline_mode=pl.Buffered(1))


def per_step(shape):
    rest = (0,) * (len(shape) - 1)
    return pl.BlockSpec((1,) + tuple(shape[1:]), lambda i: (i,) + rest)


def normalized(values):
    center = values - jnp.mean(values, -1, keepdims=True)
    factor = lax.rsqrt(jnp.mean(center * center, -1, keepdims=True) + norm_eps)
    return center * factor, factor


def layer_back(grad, normed, factor, gain_vec):
    scaled = grad * gain_vec
    return factor * (
        scaled
        - jnp.mean(scaled, -1, keepdims=True)
        - normed * jnp.mean(scaled * normed, -1, keepdims=True)
    )


def head_masks(pair_width, head_dim):
    lane = lax.broadcasted_iota(jnp.int32, (1, pair_width), 1)
    return [
        ((lane >= e * head_dim) & (lane < (e + 1) * head_dim)) for e in range(pair_width // head_dim)
    ]


def bias_kernel(idx_ref, tab_ref, out_ref):
    heads, seq = out_ref.shape[0], out_ref.shape[1]
    chunks = tab_ref.shape[1]

    def rows(step, carry):
        at = pl.multiple_of(step * 8, 8)
        for left in range(0, seq, LANES):
            index = idx_ref[pl.ds(at, 8), left : left + LANES]
            low, high = index & (LANES - 1), index >> 7
            match = [high == c for c in range(chunks)]
            width = min(LANES, seq - left)
            for h in range(heads):
                found = jnp.full((8, LANES), -1e30, F32)
                for c in range(chunks):
                    row = jnp.broadcast_to(tab_ref[h, c : c + 1, :], (8, LANES))
                    taken = jnp.take_along_axis(row, low, axis=1, mode="promise_in_bounds")
                    found = jnp.where(match[c], taken, found)
                out_ref[h, pl.ds(at, 8), left : left + width] = found[:, :width]
        return carry

    lax.fori_loop(0, seq // 8, rows, 0)


def bias_tables(index, table_rows):
    seq, _ = index.shape
    heads, _, _ = table_rows.shape
    shape = (heads, seq, seq)
    return pl.pallas_call(
        bias_kernel,
        grid=(1,),
        in_specs=[whole(index.shape), whole(table_rows.shape)],
        out_specs=whole(shape),
        out_shape=jax.ShapeDtypeStruct(shape, F32),
        compiler_params=params(),
        name="bias_tables",
    )(index, table_rows)


def table_kernel(idx_ref, ds_ref, out_ref):
    seq, heads, _ = ds_ref.shape
    chunks = out_ref.shape[0] // (2 * heads)
    out_ref[...] = jnp.zeros_like(out_ref)
    kinds = lax.broadcasted_iota(jnp.int32, (LANES, seq), 0)

    def one_query(j, total):
        index = idx_ref[pl.ds(j, 1), :]
        low, high = index & (LANES - 1), index >> 7
        onehot = jnp.where(jnp.broadcast_to(low, (LANES, seq)) == kinds, 1.0, 0.0).astype(BF)
        grads = ds_ref[j]
        top = grads.astype(BF).astype(F32)
        both = jnp.concatenate([top, grads - top], 0)
        high_all = jnp.broadcast_to(high, both.shape)
        parts = jnp.concatenate([jnp.where(high_all == c, both, 0.0) for c in range(chunks)], 0)
        return total + mm_nt(parts.astype(BF), onehot)

    out_ref[...] = lax.fori_loop(0, seq, one_query, jnp.zeros(out_ref.shape, F32), unroll=UNROLL_T)


def table_sums(index, grads, chunks):
    seq, heads, _ = grads.shape
    out = (chunks * 2 * heads, LANES)
    return pl.pallas_call(
        table_kernel,
        grid=(1,),
        in_specs=[whole(index.shape), whole(grads.shape)],
        out_specs=whole(out),
        out_shape=jax.ShapeDtypeStruct(out, F32),
        compiler_params=params(),
        name="table_sums",
    )(index, grads)


def front_kernel(heads, x_ref, wqkv_ref, wproj_ref, vec_ref, bias_ref, a_ref, qkv_ref, p_ref, o_ref, attn_ref, hn_ref):
    width = x_ref.shape[2]
    head_dim = width // heads
    scale = head_dim ** (-0.5)
    x = x_ref[0].astype(F32)
    normed, _ = normalized(x)
    first = (normed * vec_ref[4:5, :] + vec_ref[5:6, :]).astype(BF)
    a_ref[0] = first
    for part, row in ((0, 0), (1, None), (2, 1)):
        cols = slice(part * width, (part + 1) * width)
        value = mm(first, wqkv_ref[:, cols])
        if row is not None:
            value = value + vec_ref[row : row + 1, :]
        qkv_ref[0, :, cols] = value.astype(BF)
    pair = LANES
    masks = head_masks(pair, head_dim)
    per = pair // head_dim

    def one_pair(g, carry):
        at = pl.multiple_of(g * pair, pair)
        q = qkv_ref[0, :, pl.ds(at, pair)]
        k = qkv_ref[0, :, pl.ds(at + width, pair)]
        v = qkv_ref[0, :, pl.ds(at + 2 * width, pair)]
        out = None
        for e in range(per):
            qm = q * jnp.where(masks[e], scale, 0.0).astype(BF)
            s = mm_nt(qm, k) + bias_ref[g * per + e]
            p = jnp.exp(s - jnp.max(s, -1, keepdims=True))
            p = p * (1.0 / jnp.sum(p, -1, keepdims=True))
            p = p.astype(BF)
            p_ref[0, g * per + e] = p
            mixed = mm(p, v)
            out = mixed if out is None else jnp.where(masks[e], mixed, out)
        o_ref[0, :, pl.ds(at, pair)] = out.astype(BF)
        return carry

    lax.fori_loop(0, width // pair, one_pair, 0, unroll=UNROLL_F)
    attn = mm(o_ref[0], wproj_ref[...]) + vec_ref[2:3, :]
    attn_ref[0] = attn
    middle, _ = normalized(x + vec_ref[8:9, :] * attn)
    hn_ref[0] = (middle * vec_ref[6:7, :] + vec_ref[7:8, :]).astype(BF)


def front(x, qkv_weight, proj_weight, vectors, bias, heads):
    images, seq, width = x.shape
    shapes = [
        jax.ShapeDtypeStruct((images, seq, width), BF),
        jax.ShapeDtypeStruct((images, seq, 3 * width), BF),
        jax.ShapeDtypeStruct((images, heads, seq, seq), BF),
        jax.ShapeDtypeStruct((images, seq, width), BF),
        jax.ShapeDtypeStruct((images, seq, width), F32),
        jax.ShapeDtypeStruct((images, seq, width), BF),
    ]
    return pl.pallas_call(
        functools.partial(front_kernel, heads),
        grid=(images,),
        in_specs=[
            per_step(x.shape),
            fixed(qkv_weight.shape),
            fixed(proj_weight.shape),
            fixed(vectors.shape),
            fixed(bias.shape),
        ],
        out_specs=[per_step(s.shape) for s in shapes],
        out_shape=shapes,
        compiler_params=params(),
        name="front",
    )(x, qkv_weight, proj_weight, vectors, bias)


def pick(refs, at, out_ref):
    for n, ref in enumerate(refs):

        @pl.when(at == n)
        def _():
            out_ref[...] = ref[...]


def mlp_in_kernel(
    chunk, owner, hn_ref, gy_ref, vec_ref, bup_ref, up_a, up_b, up_c, up_d,
    z_ref, slope_ref, gdn_ref, dm_ref, turned_ref, wup_ref,
):
    tokens = hn_ref.shape[0]
    pick((up_a, up_b, up_c, up_d), pl.program_id(0) ^ owner(), wup_ref)

    @pl.when(pl.program_id(0) == 0)
    def _():
        def rows(step, carry):
            at = pl.ds(pl.multiple_of(step * chunk, chunk), chunk)
            dm_ref[at, :] = (vec_ref[9:10, :] * gy_ref[at, :].astype(F32)).astype(BF)
            return carry

        lax.fori_loop(0, tokens // chunk, rows, 0)
        turned_ref[...] = dm_ref[...].T

    for low in range(0, tokens, PART):
        at = slice(low, min(low + PART, tokens))
        u = mm(hn_ref[at, :], wup_ref[...]) + bup_ref[0]
        gate = 0.5 * (1.0 + lax.erf(u * 0.7071067811865476))
        z_ref[0, at, :] = (u * gate).astype(BF)
        slope_ref[0, at, :] = (gate + u * jnp.exp(-0.5 * u * u) * 0.3989422804014327).astype(BF)

    gdn_ref[0] = mm(turned_ref[...], z_ref[0]).astype(BF)


def mlp_in(hn, gy, vectors, up_bias, ups, chunk, owner):
    tokens, width = hn.shape
    blocks, hidden = len(ups), ups[0].shape[1]
    shapes = [
        jax.ShapeDtypeStruct((blocks, tokens, hidden), BF),
        jax.ShapeDtypeStruct((blocks, tokens, hidden), BF),
        jax.ShapeDtypeStruct((blocks, width, hidden), BF),
    ]
    return pl.pallas_call(
        functools.partial(mlp_in_kernel, chunk, owner),
        grid=(blocks,),
        in_specs=[
            fixed(hn.shape),
            fixed(gy.shape),
            fixed(vectors.shape),
            per_step(up_bias.shape),
            *(fixed(v.shape) for v in ups),
        ],
        out_specs=[per_step(s.shape) for s in shapes] + [fixed((tokens, width))],
        out_shape=shapes + [jax.ShapeDtypeStruct((tokens, width), BF)],
        scratch_shapes=[pltpu.VMEM((width, tokens), BF), pltpu.VMEM((width, hidden), BF)],
        compiler_params=params(limit=VMEM_WHOLE),
        name="mlp_in",
    )(hn, gy, vectors, up_bias, *ups)


def place(keep_ref, send_ref, at, core, mine, value):
    @pl.when(core == mine)
    def _():
        keep_ref[at] = value

    @pl.when(core != mine)
    def _():
        send_ref[at] = value


def mlp_out_kernel(
    chunk, owner, hn_ref, dm_ref, z_ref, slope_ref, wdn_ref, up_a, up_b, up_c, up_d,
    m_ref, dhn_ref, keep_ref, send_ref, gb_ref, du_ref, turned_ref, wup_ref,
):
    tokens = hn_ref.shape[0]
    pick((up_a, up_b, up_c, up_d), pl.program_id(0) ^ owner(), wup_ref)

    @pl.when(pl.program_id(0) == 0)
    def _():
        m_ref[...] = jnp.zeros_like(m_ref)
        dhn_ref[...] = jnp.zeros_like(dhn_ref)
        turned_ref[...] = hn_ref[...].T

    gb_ref[...] = jnp.zeros_like(gb_ref)

    def rows(step, carry):
        at = pl.ds(pl.multiple_of(step * chunk, chunk), chunk)
        m_ref[at, :] += mm_nt(z_ref[0, at, :], wdn_ref[0])
        du = (mm(dm_ref[at, :], wdn_ref[0]) * slope_ref[0, at, :].astype(F32)).astype(BF)
        du_ref[at, :] = du
        gb_ref[0] += jnp.sum(du.astype(F32), 0, keepdims=True)
        dhn_ref[at, :] += mm_nt(du, wup_ref[...])
        return carry

    lax.fori_loop(0, tokens // chunk, rows, 0)
    place(keep_ref, send_ref, 0, pl.program_id(0) & 1, owner() & 1, mm(turned_ref[...], du_ref[...]).astype(BF))


def mlp_out(hn, dm, z, slope, ups, down_all, chunk, owner):
    tokens, width = hn.shape
    blocks, _, hidden = down_all.shape
    shapes = [
        jax.ShapeDtypeStruct((tokens, width), F32),
        jax.ShapeDtypeStruct((tokens, width), F32),
        jax.ShapeDtypeStruct((blocks // 2, width, hidden), BF),
        jax.ShapeDtypeStruct((blocks // 2, width, hidden), BF),
        jax.ShapeDtypeStruct((blocks, 1, hidden), F32),
    ]
    by_pair = pl.BlockSpec((1, width, hidden), lambda i: (i // 2, 0, 0))
    return pl.pallas_call(
        functools.partial(mlp_out_kernel, chunk, owner),
        grid=(blocks,),
        in_specs=[fixed(hn.shape), fixed(dm.shape)] + [per_step(v.shape) for v in (z, slope, down_all)] + [fixed(v.shape) for v in ups],
        out_specs=[fixed(s.shape) for s in shapes[:2]] + [by_pair, by_pair, per_step(shapes[4].shape)],
        out_shape=shapes,
        scratch_shapes=[
            pltpu.VMEM((tokens, hidden), BF),
            pltpu.VMEM((width, tokens), BF),
            pltpu.VMEM((width, hidden), BF),
        ],
        compiler_params=params(limit=VMEM_WHOLE),
        name="mlp_out",
    )(hn, dm, z, slope, down_all, *ups)


def middle_kernel(
    x_ref, gy_ref, attn_ref, m_ref, dhn_ref, wproj_ref, vec_ref, out_ref, dmid_ref, dat_ref, do_ref, gvec_ref
):
    @pl.when(pl.program_id(0) == 0)
    def _():
        gvec_ref[...] = jnp.zeros_like(gvec_ref)

    attn = attn_ref[0]
    middle = x_ref[0].astype(F32) + vec_ref[8:9, :] * attn
    branch = m_ref[0] + vec_ref[3:4, :]
    out_ref[0] = (middle + vec_ref[9:10, :] * branch).astype(BF)
    cotangent = gy_ref[0].astype(F32)
    normed, factor = normalized(middle)
    dhn = dhn_ref[0]
    dmid = cotangent + layer_back(dhn, normed, factor, vec_ref[6:7, :])
    dmid_ref[0] = dmid
    dat = (vec_ref[8:9, :] * dmid).astype(BF)
    dat_ref[0] = dat
    down_in = (vec_ref[9:10, :] * cotangent).astype(BF)
    for row, value in enumerate(
        (dat.astype(F32), down_in.astype(F32), dhn * normed, dhn, dmid * attn, cotangent * branch)
    ):
        gvec_ref[row : row + 1, :] += jnp.sum(value, 0, keepdims=True)
    do_ref[0] = mm_nt(dat, wproj_ref[...]).astype(BF)


def middle_back(x, gy, attn, m, dhn, proj_weight, vectors):
    images, seq, width = x.shape
    shapes = [
        jax.ShapeDtypeStruct((images, seq, width), BF),
        jax.ShapeDtypeStruct((images, seq, width), F32),
        jax.ShapeDtypeStruct((images, seq, width), BF),
        jax.ShapeDtypeStruct((images, seq, width), BF),
        jax.ShapeDtypeStruct((8, width), F32),
    ]
    return pl.pallas_call(
        middle_kernel,
        grid=(images,),
        in_specs=[per_step(v.shape) for v in (x, gy, attn, m, dhn)] + [fixed(proj_weight.shape), fixed(vectors.shape)],
        out_specs=[per_step(s.shape) for s in shapes[:4]] + [fixed(shapes[4].shape)],
        out_shape=shapes,
        compiler_params=params(),
        name="middle_back",
    )(x, gy, attn, m, dhn, proj_weight, vectors)


def back_kernel(heads, qkv_ref, do_ref, p_ref, dqkv_ref, ds_ref, gcol_ref):
    width = do_ref.shape[2]
    head_dim = width // heads
    scale = head_dim ** (-0.5)

    @pl.when(pl.program_id(0) == 0)
    def _():
        ds_ref[...] = jnp.zeros_like(ds_ref)
        gcol_ref[...] = jnp.zeros_like(gcol_ref)

    pair = LANES
    masks = head_masks(pair, head_dim)
    per = pair // head_dim

    def one_pair(g, carry):
        at = pl.multiple_of(g * pair, pair)
        q = qkv_ref[0, :, pl.ds(at, pair)]
        k = qkv_ref[0, :, pl.ds(at + width, pair)]
        v = qkv_ref[0, :, pl.ds(at + 2 * width, pair)]
        do = do_ref[0, :, pl.ds(at, pair)]
        dq = dk = dv = None
        for e in range(per):
            pick = jnp.where(masks[e], scale, 0.0).astype(BF)
            keep = jnp.where(masks[e], 1.0, 0.0).astype(BF)
            qm, km, dom = q * pick, k * pick, do * keep
            rounded = p_ref[0, g * per + e]
            p = rounded.astype(F32)
            dv_e = mm_tn(rounded, dom)
            dp = mm_nt(dom, v)
            ds = (p * (dp - jnp.sum(dp * p, -1, keepdims=True))).astype(BF)
            ds_ref[g * per + e] += ds.astype(F32)
            dk_e = mm_tn(ds, qm)
            dq_e = mm(ds, km)
            dq = dq_e if dq is None else dq + dq_e
            dk = dk_e if dk is None else dk + dk_e
            dv = dv_e if dv is None else dv + dv_e
        for part, value in ((0, dq), (1, dk), (2, dv)):
            rounded = value.astype(BF)
            dqkv_ref[0, :, pl.ds(at + part * width, pair)] = rounded
            gcol_ref[:, pl.ds(at + part * width, pair)] += jnp.sum(rounded.astype(F32), 0, keepdims=True)
        return carry

    lax.fori_loop(0, width // pair, one_pair, 0, unroll=UNROLL_B)


def back(qkv, do, p, heads):
    images, seq, width = do.shape
    shapes = [
        jax.ShapeDtypeStruct((images, seq, 3 * width), BF),
        jax.ShapeDtypeStruct((heads + (-heads) % 8, seq, seq), F32),
        jax.ShapeDtypeStruct((1, 3 * width), F32),
    ]
    return pl.pallas_call(
        functools.partial(back_kernel, heads),
        grid=(images,),
        in_specs=[per_step(v.shape) for v in (qkv, do, p)],
        out_specs=[per_step(shapes[0].shape)] + [fixed(s.shape) for s in shapes[1:]],
        out_shape=shapes,
        compiler_params=params(),
        name="back",
    )(qkv, do, p)


def grads_kernel(blocks, owner, a_ref, dqkv_ref, o_ref, dat_ref, keep_ref, send_ref, turned_a, turned_o):
    wide_cols, thin_cols = dqkv_ref.shape[1] // blocks, dat_ref.shape[1] // blocks
    turned_a[...] = a_ref[...].T
    turned_o[...] = o_ref[...].T
    here = owner() & 1
    for n in range(blocks):
        left = mm(turned_a[...], dqkv_ref[:, n * wide_cols : (n + 1) * wide_cols]).astype(BF)
        right = mm(turned_o[...], dat_ref[:, n * thin_cols : (n + 1) * thin_cols]).astype(BF)
        place(keep_ref, send_ref, n // 2, n & 1, here, jnp.concatenate([left, right], 1))


def attention_grads(first, dqkv, mixed, dat, blocks, owner):
    width = first.shape[1]
    cols = (dqkv.shape[1] + dat.shape[1]) // blocks
    shape = (blocks // 2, width, cols)
    return pl.pallas_call(
        functools.partial(grads_kernel, blocks, owner),
        grid=(1,),
        in_specs=[whole(v.shape) for v in (first, dqkv, mixed, dat)],
        out_specs=[whole(shape)] * 2,
        out_shape=[jax.ShapeDtypeStruct(shape, BF)] * 2,
        scratch_shapes=[pltpu.VMEM((width, first.shape[0]), BF)] * 2,
        compiler_params=params(),
        name="attention_grads",
    )(first, dqkv, mixed, dat)


def input_kernel(x_ref, dqkv_ref, dmid_ref, wqkv_ref, vec_ref, out_ref, gvec_ref):
    @pl.when(pl.program_id(0) == 0)
    def _():
        gvec_ref[...] = jnp.zeros_like(gvec_ref)

    da = mm_nt(dqkv_ref[0], wqkv_ref[...])
    normed, factor = normalized(x_ref[0].astype(F32))
    gvec_ref[0:1, :] += jnp.sum(da * normed, 0, keepdims=True)
    gvec_ref[1:2, :] += jnp.sum(da, 0, keepdims=True)
    out_ref[0] = dmid_ref[0] + layer_back(da, normed, factor, vec_ref[4:5, :])


def input_grads(x, dqkv, dmid, qkv_weight, vectors):
    images, seq, width = x.shape
    shapes = [
        jax.ShapeDtypeStruct((images, seq, width), F32),
        jax.ShapeDtypeStruct((8, width), F32),
    ]
    return pl.pallas_call(
        input_kernel,
        grid=(images,),
        in_specs=[per_step(v.shape) for v in (x, dqkv, dmid)]
        + [fixed(qkv_weight.shape), fixed(vectors.shape)],
        out_specs=[per_step(shapes[0].shape), fixed(shapes[1].shape)],
        out_shape=shapes,
        compiler_params=params(),
        name="input_grads",
    )(x, dqkv, dmid, qkv_weight, vectors)


def adam_update(master, mean, square, grad, rate, decay):
    mean_new = beta_one * mean + (1.0 - beta_one) * grad
    square_new = beta_two * square + (1.0 - beta_two) * grad * grad
    fix_one = 1.0 - beta_one**STEP
    fix_two = 1.0 - beta_two**STEP
    direction = mean_new / fix_one / (jnp.sqrt(square_new / fix_two) + adam_eps)
    return (mean_new, square_new, master - rate * (direction + decay * master))


def adam_kernel(rows, ours_ref, theirs_ref, attn_ref, up_ref, down_ref, *refs):
    state, results = refs[:21], refs[21:]
    sums = ours_ref[...] + theirs_ref[...]
    heads, vec_at, bias_at, square_at = rows
    row = lax.broadcasted_iota(jnp.int32, sums.shape, 0)
    small = jnp.where(row < square_at, sums, 0.0)
    total = jnp.sum(
        jnp.sum(small * small, 0, keepdims=True) + sums[square_at : square_at + 1], 1, keepdims=True
    )
    norm = jnp.sqrt(total)
    results[0][...] = norm
    clip = jnp.minimum(1.0, max_norm / (norm + clip_eps))
    split = state[0].shape[1]
    vec_rows, table_rows = state[12].shape[0], state[18].shape[1]
    bias = jnp.concatenate([sums[r : r + 1] for r in range(bias_at, square_at)], 1)
    grads = (
        attn_ref[:, :split],
        attn_ref[:, split:],
        up_ref[...],
        down_ref[...].astype(F32),
        sums[vec_at : vec_at + vec_rows],
        bias,
        sums[:heads, :table_rows],
    )
    at = 1
    for n, grad in enumerate(grads):
        large = n < 4
        mean_new, square_new, master_new = adam_update(
            *(state[3 * n + k][...] for k in range(3)),
            clip * grad,
            rate_matrix if large else rate_small,
            weight_decay if large else 0.0,
        )
        values = [mean_new, square_new, master_new]
        if large:
            values.append(master_new.astype(BF))
        for value in values:
            results[at][...] = value
            at += 1


def adam(rows, ours, theirs, shards, state):
    shapes = [jax.ShapeDtypeStruct((1, 1), F32)]
    for n in range(7):
        shapes += [jax.ShapeDtypeStruct(state[3 * n].shape, F32)] * 3
        if n < 4:
            shapes.append(jax.ShapeDtypeStruct(state[3 * n].shape, BF))
    inputs = [ours, theirs, *shards, *state]
    return pl.pallas_call(
        functools.partial(adam_kernel, rows),
        grid=(1,),
        in_specs=[whole(v.shape) for v in inputs],
        out_specs=[whole(v.shape) for v in shapes],
        out_shape=shapes,
        compiler_params=params(limit=VMEM_WHOLE),
        name="adam",
    )(*inputs)


def axis_bits():
    found = []
    for axis in ("narrow", "wide"):
        count = lax.axis_size(axis).bit_length() - 1
        found += [(axis, count - 1 - at) for at in range(count)]
    return found


def swap(value, axis, bit):
    size = lax.axis_size(axis)
    return lax.ppermute(value, axis, [(i, i ^ (1 << bit)) for i in range(size)])


def split_kernel(mine, keep_ref, come_ref, keep_a, send_a, keep_b, send_b):
    half = keep_ref.shape[4] // 2
    for out_a, out_b, flip in ((keep_a, keep_b, 0), (send_a, send_b, 1)):
        side_a, side_b = mine[0]() ^ flip, mine[1]() ^ flip
        for n in range(2):
            for out, at, cols in (
                (out_a.at[0, n], (side_a, 0, n), slice(0, half)),
                (out_b.at[n, 0], (n, 0, side_b), slice(half, 2 * half)),
            ):
                total = keep_ref[(*at, slice(None), cols)].astype(F32) + come_ref[(*at, slice(None), cols)].astype(F32)
                out[...] = total.astype(BF)


def split_step(keep, come, mine):
    _, middle, _, rows, cols = keep.shape
    side = cols // 2
    block = pl.BlockSpec((2, 1, 2, rows, cols), lambda i: (0, i, 0, 0, 0))
    out_a = pl.BlockSpec((1, 2, rows, side), lambda i: (i, 0, 0, 0))
    out_b = pl.BlockSpec((2, 1, rows, side), lambda i: (0, i, 0, 0))
    shape_a = jax.ShapeDtypeStruct((middle, 2, rows, side), BF)
    shape_b = jax.ShapeDtypeStruct((2, middle, rows, side), BF)
    return pl.pallas_call(
        functools.partial(split_kernel, mine),
        grid=(middle,),
        in_specs=[block, block],
        out_specs=[out_a, out_a, out_b, out_b],
        out_shape=[shape_a, shape_a, shape_b, shape_b],
        compiler_params=params(limit=VMEM_WHOLE),
        name="split_step",
    )(keep, come)


def halve_kernel(mine, places, join, *refs):
    parts = len(places)
    ins, outs = refs[: 2 * parts], refs[2 * parts :]
    for n in range(parts):
        keep_ref, come_ref = ins[2 * n : 2 * n + 2]
        count, _, cols = keep_ref.shape
        left = cols * n if join else 0
        outputs = outs[:2] if join else outs[2 * n : 2 * n + 2]
        low = places[n]

        def one(c, carry):
            for out, side in zip(outputs, (mine[n](), 1 - mine[n]())):
                at = ((c >> low) << (low + 1)) | (side << low) | (c & ((1 << low) - 1))
                total = keep_ref[at].astype(F32) + come_ref[at].astype(F32)
                out[c, :, left : left + cols] = total.astype(BF)
            return carry

        lax.fori_loop(0, count // 2, one, 0)


def halve_step(parts, places, mine, join):
    inputs = [v for pair in parts for v in pair]
    shapes = []
    for keep, _ in parts[:1] if join else parts:
        count, rows, cols = keep.shape
        shapes += [jax.ShapeDtypeStruct((count // 2, rows, cols * len(parts) if join else cols), BF)] * 2
    return pl.pallas_call(
        functools.partial(halve_kernel, mine, places, join),
        grid=(1,),
        in_specs=[whole(v.shape) for v in inputs],
        out_specs=[whole(v.shape) for v in shapes],
        out_shape=shapes,
        compiler_params=params(limit=VMEM_WHOLE),
        name="halve_step",
    )(*inputs)


class Spread:
    def __init__(self, block):
        rows = block.shape[0] // 2
        self.block = block
        self.side = lax.axis_index("wide") & 1
        self.half = swap(lax.dynamic_slice_in_dim(block, self.side * rows, rows, 0), "narrow", 1)
        self.other = swap(block, "narrow", 0)

    def over_x(self, *after):
        self.half = gated(self.half, *after)
        self.rest = swap(self.half, "wide", 0)
        return self.half

    def blocks(self, *after):
        half, rest = self.half, gated(self.rest, *after)
        far = jnp.where(self.side == 0, jnp.concatenate([half, rest]), jnp.concatenate([rest, half]))
        return self.block, self.other, far, swap(far, "narrow", 0)


class Halving:
    def __init__(self, keep, send, rows):
        self.bits = axis_bits()
        cores = [d for d, (axis, _) in enumerate(self.bits) if axis == "narrow"]
        self.dims = [[d for d in range(len(self.bits)) if d != cores[-1]]]
        first, last = self.dims[0][0], self.dims[0][-1]
        self.steps = [(first, last), (last, first)] + [(d,) for d in self.dims[0][-2:0:-1]]
        shape = (-1, rows, keep.shape[-1])
        self.keep = [keep.reshape(shape)]
        self.sent = (send.reshape(shape),)
        self.come = [swap(self.sent[0], *self.bits[cores[-1]])]

    def mine(self, dim):
        axis, bit = self.bits[dim]
        return lambda: (lax.axis_index(axis) >> bit) & 1

    def send(self, *after):
        target = self.steps.pop(0)
        come = lax.optimization_barrier((*self.come, *after)) if after else self.come
        parts = len(self.keep)
        if len(target) > parts:
            rows, cols = self.keep[0].shape[1:]
            shape = (2, -1, 2, rows, cols)
            made = split_step(self.keep[0].reshape(shape), come[0].reshape(shape), [self.mine(d) for d in target])
            made = [v.reshape(-1, rows, cols // 2) for v in made]
            self.dims = self.dims * 2
        else:
            dims = target * (parts // len(target))
            places = [len(own) - 1 - own.index(d) for own, d in zip(self.dims, dims)]
            made = halve_step(
                list(zip(self.keep, come)), places, [self.mine(d) for d in dims], len(target) < parts
            )
        self.keep, self.sent = made[::2], tuple(made[1::2])
        self.dims = [[d for d in own if d != gone] for own, gone in zip(self.dims, target)]
        self.come = [swap(v, *self.bits[d]) for v, d in zip(self.sent, target)]
        return self.sent

    def last_pair(self):
        while self.steps:
            self.send()
        return self.keep[0][0], self.come[0][0]


def finish_kernel(rows, up_a, up_b, attn_a, attn_b, down_ref, table_ref, cols_ref, gvec_ref, gone_ref, gb_ref, up_ref, attn_ref, ours_ref):
    _, vec_at, bias_at, square_at = rows
    width = ours_ref.shape[1]
    up = up_a[...].astype(F32) + up_b[...].astype(F32)
    attn = attn_a[...].astype(F32) + attn_b[...].astype(F32)
    down = down_ref[...].astype(F32)
    up_ref[...] = up
    attn_ref[...] = attn
    squares = jnp.sum(up * up + attn * attn + down * down, 0, keepdims=True)
    ours_ref[...] = jnp.zeros_like(ours_ref)
    for c in range(table_ref.shape[0]):
        ours_ref[:vec_at, c * LANES : (c + 1) * LANES] = table_ref[c, 0] + table_ref[c, 1]
    ours_ref[vec_at : vec_at + 1, :] = cols_ref[:, :width]
    ours_ref[vec_at + 1 : vec_at + 2, :] = cols_ref[:, 2 * width :]
    for to, source, at in ((2, gvec_ref, 0), (3, gvec_ref, 1), (4, gone_ref, 0), (5, gone_ref, 1)) + tuple(
        (6 + n, gvec_ref, 2 + n) for n in range(4)
    ):
        ours_ref[vec_at + to : vec_at + to + 1, :] = source[at : at + 1, :]
    for n in range(square_at - bias_at):
        ours_ref[bias_at + n : bias_at + n + 1, :] = gb_ref[n]
    ours_ref[square_at : square_at + 1, :] = squares


def finish(rows, up, attn, down, small):
    inputs = [*up, *attn, down, *small]
    width = down.shape[1]
    shapes = [jax.ShapeDtypeStruct(v.shape, F32) for v in (up[0], attn[0])]
    shapes.append(jax.ShapeDtypeStruct((-(-(rows[3] + 1) // 8) * 8, width), F32))
    return pl.pallas_call(
        functools.partial(finish_kernel, rows),
        grid=(1,),
        in_specs=[whole(v.shape) for v in inputs],
        out_specs=[whole(v.shape) for v in shapes],
        out_shape=shapes,
        compiler_params=params(limit=VMEM_WHOLE),
        name="finish",
    )(*inputs)


def gated(value, *waits):
    return lax.optimization_barrier((value,) + waits)[0] if waits else value


class Plan:
    def __init__(self, rows, up_weight, down_weight):
        self.rows, self.down_weight = rows, down_weight
        self.spread = Spread(up_weight)

    def after_bias(self, bias):
        half = self.spread.over_x(bias)
        self.down_all = lax.all_gather(gated(self.down_weight, half), "narrow", axis=0)
        return (half,)

    def after_front(self, hn):
        return self.spread.blocks(hn), self.down_all

    @staticmethod
    def owner():
        return lax.axis_index("narrow")

    def after_down(self, grads):
        rows = grads.reshape(-1, grads.shape[2])
        self.down = lax.psum_scatter(rows, ("narrow", "wide"), scatter_dimension=0, tiled=True)

    def after_up(self, keep, send):
        self.up = Halving(keep, send, self.rows)
        return self.up.sent

    def next_up(self, *after):
        return self.up.send(*after)

    def after_attention(self, keep, send):
        self.attn = Halving(keep, send, self.rows)
        return self.attn.sent

    def next_attention(self, *after):
        return self.attn.send(*after)

    def next_both(self, *after):
        self.up.send(*after)
        self.attn.send(*after)


class Alone:
    def __init__(self, *weights):
        self.weights = weights

    def after_bias(self, bias):
        return ()

    def after_front(self, hn):
        return self.weights

    @staticmethod
    def owner():
        return 0

    def after_down(self, grads):
        self.down = grads

    def after_up(self, *grads):
        self.up = grads
        return ()

    def after_attention(self, *grads):
        self.attn = grads
        return ()

    def next_up(self, *after):
        return ()

    next_attention = next_both = next_up


def local_work(
    block_in, out_grad, mim_mask, rel_index, qkv_weight, proj_weight, vectors, up_bias, rel_table, plan
):
    images, seq, width = block_in.shape
    table_rows, heads = rel_table.shape
    tokens = images * seq
    chunks = -(-table_rows // LANES)
    padded_seq = -(-seq // LANES) * LANES
    key_at = jnp.arange(seq, dtype=jnp.int32)
    index = jnp.where(key_at[None, :] < VALID, rel_index, chunks * LANES)
    padded = jnp.pad(index, ((0, 0), (0, padded_seq - seq)))
    table_t = jnp.pad(rel_table, ((0, chunks * LANES - table_rows), (0, 0))).T.reshape(heads, chunks, LANES)
    bias = bias_tables(padded, table_t)
    gy = out_grad * mim_mask.astype(BF)[:, :, None]
    first, qkv, p, mixed, attn, hn = front(gated(block_in, *plan.after_bias(bias)), qkv_weight, proj_weight, vectors, bias, heads)
    flat = lambda v: v.reshape(tokens, v.shape[-1])
    ups, down_all = plan.after_front(hn)
    blocks, _, hidden = down_all.shape
    z, slope, grad_down, dm = mlp_in(flat(hn), flat(gy), vectors, up_bias.reshape(blocks, 1, hidden), ups, tokens, plan.owner)
    plan.after_down(grad_down)
    m, dhn, keep, send, grad_bias = mlp_out(flat(hn), dm, z, slope, ups, down_all, tokens, plan.owner)
    gy = gated(gy, *plan.after_up(keep, send))
    fold = lambda v: v.reshape(images, seq, width)
    block_out, dmid, dat, do, gvec = middle_back(block_in, gy, attn, fold(m), fold(dhn), proj_weight, vectors)
    do = gated(do, *plan.next_up(do))
    dqkv, ds, gcol = back(qkv, do, p, heads)
    dat = gated(dat, *plan.next_up(dqkv))
    keep, send = attention_grads(flat(first), flat(dqkv), flat(mixed), flat(dat), blocks, plan.owner)
    dmid = gated(dmid, *plan.after_attention(keep, send))
    input_grad, gvec_one = input_grads(block_in, dqkv, dmid, qkv_weight, vectors)
    by_query = ds.transpose(1, 0, 2)
    by_query = gated(by_query, *plan.next_attention(input_grad))
    sums = table_sums(index, by_query, chunks)
    plan.next_both(sums)
    small = (sums.reshape(chunks, 2, -1, LANES), gcol, gvec, gvec_one, grad_bias)
    return block_out, input_grad, small, plan


def shards(
    block_in,
    out_grad,
    mim_mask,
    rel_index,
    qkv_weight,
    proj_weight,
    up_weight,
    down_weight,
    vectors,
    up_bias,
    rel_table,
    *state,
):
    width = block_in.shape[2]
    heads = rel_table.shape[1]
    plan = Plan(width // lax.axis_size("wide"), up_weight, down_weight)
    block_out, input_grad, small, plan = local_work(
        block_in, out_grad, mim_mask, rel_index, qkv_weight, proj_weight, vectors, up_bias, rel_table, plan
    )
    vec_at = heads + (-heads) % 8
    bias_at = vec_at + vectors.shape[0]
    rows = (heads, vec_at, bias_at, bias_at + up_bias.shape[0] // width)
    down_shard = plan.down
    up_shard, attn_shard, ours = finish(rows, plan.up.last_pair(), plan.attn.last_pair(), down_shard, small)
    theirs = None
    for axis, bit in reversed(axis_bits()):
        ours = ours if theirs is None else ours + theirs
        theirs = swap(ours, axis, bit)
    line = lambda v: v.reshape(1, -1)
    matrices = state[:12]
    params_small = (vectors, state[12], state[13], line(up_bias), line(state[14]), line(state[15]), rel_table.T, *(v.T for v in state[16:]))
    norm, *updated = adam(
        rows,
        ours,
        theirs,
        (attn_shard, up_shard, down_shard),
        [matrices[3 * n + k] for n in range(4) for k in range(3)] + [params_small[3 * n + k] for n in range(3) for k in range(3)],
    )
    for n in range(19, 22):
        updated[n] = updated[n].reshape(up_bias.shape)
        updated[n + 3] = updated[n + 3].T
    return (block_out, input_grad, norm.reshape(()), *updated)


def solution(mesh):
    token = P(("wide", "narrow"), None, None)
    whole_spec = P()
    shard = P("wide", "narrow")
    in_specs = (
        (token, token, P(("wide", "narrow"), None))
        + (whole_spec,) * 3
        + (P(None, "narrow"),) * 2
        + (whole_spec,) * 3
        + (shard,) * 12
        + (whole_spec,) * 6
    )
    out_specs = (token, token, whole_spec) + (shard,) * 16 + (whole_spec,) * 9
    return jax.shard_map(shards, mesh=mesh, in_specs=in_specs, out_specs=out_specs, check_vma=False)
```
